128 devices in a mesh: dp: 32 (over x, z, core), rep: 4 (over y).
Axes of the slice: x: 4, y: 4, z: 4, core: 2. Of those that a mesh axis runs over, the one named last changes fastest.
Arguments:
- cross_in: bfloat16 [65536, 3456], P(('dp', 'rep')), may hold values from -24 to 24
- cotangent: bfloat16 [65536, 3456], P(('dp', 'rep')), may hold values from -24 to 24
- weight_down: bfloat16 [3456, 512], replicated, may hold values from -0.109375 to 0.109375
- weight_up: bfloat16 [512, 3456], replicated, may hold values from -0.25 to 0.25
- cross_bias: float32 [3456], replicated, may hold values from -3 to 3
- row_place: int32 [65536, 26], P(('dp', 'rep')), may hold values from 0 to 66559, as said below
- frequent_table: float32 [1024, 128], replicated, may hold values from -0.6 to 0.6
- frequent_accum: float32 [1024], replicated, may hold values from 416 to 106496
- shard_table: float32 [65536, 128], P('dp'), may hold values from -0.6 to 0.6
- shard_accum: float32 [65536], P('dp'), may hold values from 0.01 to 1
Outputs:
- new_frequent: float32 [1024, 128], replicated
- new_frequent_accum: float32 [1024], replicated
- new_shard: float32 [65536, 128], P('dp')
- new_shard_accum: float32 [65536], P('dp')
- grad_up: float32 [512, 3456], P(('dp', 'rep'))
- grad_down: float32 [3456, 512], P(('dp', 'rep'))
- grad_bias: float32 [3456], P(('dp', 'rep'))
The draws below stay inside these ranges and needn't reach their ends.
Inputs may be any that keep to these rules, and one draw needn't show every extreme that they name: `row_place`: within the rows of one device (aligned blocks of 512 samples), at most 208 entries name rows of any one owner, and in every block some owner is named by exactly 208 entries; every owner is named at least once in every block.
All inputs are finite; a program needn't handle non-finite values.
Results may differ from the reference program's by a relative error of at most 0.0013.
The reference program's roundings to bfloat16 on the way (of `hidden`, `inner_half` and `back_low`) count: a program that leaves them out, or rounds other values in their place, can miss the bound.
Values sent between devices are 32-bit elements; how exact they have to be, the bound alone decides.
A program may use at most 192 MiB of HBM per device.

```python
import math
import jax
import jax.numpy as jnp
from jax import lax

EMB = 128
TABLES = 26
RANK = 512
B_DEV = 512
F_ROWS = 1024
R_DEV = 2048
WIDTH = 3456
SHARDS = 32
BATCH = 65536
CAP = 208


def first_of(flags):
    running = jnp.cumsum(flags.astype(jnp.int32))
    return jnp.logical_and(flags, running == 1)


def draw_row_place(key, part):
    blocks = BATCH // B_DEV
    entries = B_DEV * TABLES

    def one_block(index):
        block_key = jax.random.fold_in(key, index)
        keys = jax.random.split(block_key, 7)
        counts = jax.random.randint(keys[0], (SHARDS,), 1, CAP + 1)
        forced = jax.random.randint(keys[1], (), 0, SHARDS)
        counts = jnp.where(jnp.arange(SHARDS) == forced, CAP, counts)
        ends = jnp.cumsum(counts)
        position = jnp.arange(entries)
        owners = jnp.sum((position[:, None] >= ends[None, :]).astype(jnp.int32), axis=1)
        owners = jax.random.permutation(keys[2], owners)
        local_top = jax.random.randint(keys[3], (entries,), 1, R_DEV + 1)
        local_row = jax.random.randint(keys[4], (entries,), 0, local_top)
        local_row = jnp.where(first_of(owners == SHARDS - 1), R_DEV - 1, local_row)
        hot_top = jax.random.randint(keys[5], (entries,), 1, F_ROWS + 1)
        hot_row = jax.random.randint(keys[6], (entries,), 0, hot_top)
        hot_row = jnp.where(first_of(owners == SHARDS), 0, hot_row)
        placed = jnp.where(owners < SHARDS, F_ROWS + owners * R_DEV + local_row, hot_row)
        return placed.astype(jnp.int32)
    result = lax.map(one_block, jnp.arange(blocks))
    return result.reshape(BATCH, TABLES)


def strengthened(values, stream_key, source, target, parts, factor):
    def block_of(dim):
        return (jnp.arange(values.shape[dim]) // (values.shape[dim] // parts)).reshape((-1,) + (1,) * (values.ndim - 1 - dim))

    first = jax.random.permutation(stream_key, parts)[block_of(target)]
    other_side = (block_of(target) + parts // 2) % parts
    return jnp.where((block_of(source) == first) | (block_of(source) == other_side), factor * values, values)


def level_of(key, shape, cuts, least, top_value):
    def one(axis_at, parts):
        heights = jax.random.uniform(jax.random.fold_in(jax.random.fold_in(key, 6), axis_at), (parts,), jnp.float32, least / len(cuts), top_value / len(cuts))
        return jnp.repeat(jnp.exp(heights), shape[axis_at] // parts).reshape((-1,) + (1,) * (len(shape) - axis_at - 1))

    gain = one(*cuts[0])
    for cut in cuts[1:]:
        gain = gain * one(*cut)
    return gain


def bell_draw(stream_key, shape, scale, most, cuts=(), kind=jnp.bfloat16):
    values = scale * jax.random.normal(stream_key, shape, jnp.float32)
    if cuts:
        values = values * level_of(stream_key, shape, cuts, -0.22, 0.18)
    return jnp.clip(values, -most, most).astype(kind)


def noise_with(rng, shape, scale, bound, cuts, heavy, held_as=jnp.bfloat16):
    values = scale * jax.random.normal(rng, shape, jnp.float32)
    if cuts:
        values = values * level_of(rng, shape, cuts, -0.22, 0.18)
    return jnp.clip(strengthened(values, jax.random.fold_in(rng, 3), *heavy), -bound, bound).astype(held_as)


def setup_inputs(seed: int = 0) -> dict:
    key_of = jax.random.split(jax.random.key(seed), 11)
    return {
        "cross_in": noise_with(key_of[0], (BATCH, WIDTH), 1.0, 24.0, ((0, 128),), (0, 1, 128, 5.5)),
        "cotangent": noise_with(key_of[1], (BATCH, WIDTH), 1.0, 24.0, ((0, 128),), (0, 1, 128, 5.5)),
        "weight_down": bell_draw(key_of[2], (WIDTH, RANK), WIDTH ** -0.5, 0.109375),
        "weight_up": bell_draw(key_of[3], (RANK, WIDTH), RANK ** -0.5, 0.25),
        "cross_bias": bell_draw(key_of[4], (WIDTH,), 0.5, 3.0, (), jnp.float32),
        "row_place": draw_row_place(jax.random.fold_in(key_of[10], 71), 0),
        "frequent_table": bell_draw(key_of[6], (F_ROWS, EMB), 0.1, 0.6, (), jnp.float32),
        "frequent_accum": jnp.clip(jnp.exp(jax.random.uniform(key_of[7], (F_ROWS,), jnp.float32, math.log(416.0), math.log(106496.0))), 416.0, 106496.0),
        "shard_table": bell_draw(key_of[8], (SHARDS * R_DEV, EMB), 0.1, 0.6, ((0, 32),), jnp.float32),
        "shard_accum": jnp.clip(jnp.exp(math.log(1.0) - 4.6051702 * jax.random.uniform(key_of[9], (SHARDS * R_DEV,), jnp.float32) ** level_of(key_of[9], (SHARDS * R_DEV,), ((0, 32),), -0.2, 0.2)), 0.01, 1.0),
    }


learn_rate = 0.05
eps_ada = 1e-08

def row_adagrad(table, accum, grad):
    accum_new = accum + lax.optimization_barrier(jnp.mean(grad * grad, axis=1))
    return (table - learn_rate * grad / (jnp.sqrt(accum_new)[:, None] + eps_ada), accum_new)

def reference(cross_in, cotangent, weight_down, weight_up, cross_bias, row_place, frequent_table, frequent_accum, shard_table, shard_accum):
    total_rows = SHARDS * R_DEV
    blocks = BATCH // B_DEV
    inputs_blk = cross_in.reshape(blocks, B_DEV, WIDTH)
    cot_blk = cotangent.reshape(blocks, B_DEV, WIDTH)
    place_blk = row_place.reshape(blocks, B_DEV * TABLES)

    def step(carry, pieces):
        acc_up, acc_down, acc_bias, freq_grad, rows_grad = carry
        block_in, block_cot, places = pieces
        hidden = jnp.dot(block_in, weight_down, preferred_element_type=jnp.float32).astype(jnp.bfloat16)
        scaled = jnp.dot(hidden, weight_up, preferred_element_type=jnp.float32) + cross_bias
        cot_wide = block_cot.astype(jnp.float32)
        inner = cot_wide * block_in.astype(jnp.float32)
        inner_half = inner.astype(jnp.bfloat16)
        back_low = jnp.dot(inner_half, weight_up.T, preferred_element_type=jnp.float32).astype(jnp.bfloat16)
        back_in = cot_wide * (scaled + 1.0) + jnp.dot(back_low, weight_down.T, preferred_element_type=jnp.float32)
        acc_up = acc_up + jnp.dot(hidden.T, inner_half, preferred_element_type=jnp.float32)
        acc_down = acc_down + jnp.dot(block_in.T, back_low, preferred_element_type=jnp.float32)
        acc_bias = acc_bias + lax.optimization_barrier(jnp.sum(inner, axis=0))
        values = back_in[:, EMB:].reshape(B_DEV * TABLES, EMB)
        freq_ids = jnp.where(places < F_ROWS, places, F_ROWS).astype(jnp.int32)
        freq_grad = freq_grad + jax.ops.segment_sum(values, freq_ids, F_ROWS + 1)[:F_ROWS]
        rows_ids = jnp.where(places >= F_ROWS, places - F_ROWS, total_rows).astype(jnp.int32)
        rows_grad = rows_grad + jax.ops.segment_sum(values, rows_ids, total_rows + 1)[:total_rows]
        return ((acc_up, acc_down, acc_bias, freq_grad, rows_grad), None)
    start = (jnp.zeros((RANK, WIDTH), jnp.float32), jnp.zeros((WIDTH, RANK), jnp.float32), jnp.zeros((WIDTH,), jnp.float32), jnp.zeros((F_ROWS, EMB), jnp.float32), jnp.zeros((total_rows, EMB), jnp.float32))
    final, _ = lax.scan(step, start, (inputs_blk, cot_blk, place_blk))
    acc_up, acc_down, acc_bias, freq_grad, rows_grad = final
    new_frequent, new_frequent_accum = row_adagrad(frequent_table, frequent_accum, freq_grad)
    new_shard, new_shard_accum = row_adagrad(shard_table, shard_accum, rows_grad)
    return (new_frequent, new_frequent_accum, new_shard, new_shard_accum, acc_up, acc_down, acc_bias)
```

```python
import functools
import jax
import jax.numpy as jnp
from jax import lax
from jax.experimental import pallas as pl
from jax.experimental.pallas import tpu as pltpu
from jax.sharding import PartitionSpec as P

learn_rate = 0.05
eps_ada = 1e-08
f32, bf16, i32 = jnp.float32, jnp.bfloat16, jnp.int32
VLIM = 60 * 1024 * 1024


def row_adagrad(table, accum, grad):
    accum_new = accum + jnp.mean(grad * grad, axis=1)
    return (table - learn_rate * grad / (jnp.sqrt(accum_new)[:, None] + eps_ada), accum_new)


def dot_nt(a, b):
    return lax.dot_general(a, b, (((1,), (1,)), ((), ())), preferred_element_type=f32)


def dot_tn(a, b):
    return lax.dot_general(a, b, (((0,), (0,)), ((), ())), preferred_element_type=f32)


def hi_lo(v):
    hi = v.astype(bf16)
    lo = (v - hi.astype(f32)).astype(bf16)
    return jnp.concatenate([hi, lo], axis=1)


def one_hot(flags):
    return jnp.where(flags, 1.0, 0.0).astype(bf16)


def index_kernel(frequent, owned, place, idx, row, hot, cum):
    tables, samples = place.shape
    owners, slots = idx.shape
    at = lax.broadcasted_iota(i32, (1, samples), 1)
    owner_iota = lax.broadcasted_iota(i32, (owners, samples), 0)
    tri = one_hot(
        lax.broadcasted_iota(i32, (samples, samples), 0)
        < lax.broadcasted_iota(i32, (samples, samples), 1)
    )
    shift = owned.bit_length() - 1
    for t in range(tables):
        owner = lax.shift_right_arithmetic(place[t : t + 1, :] - frequent, shift)
        hot[t * owners : (t + 1) * owners, :] = one_hot(owner_iota == owner)
    cum[...] = jnp.dot(hot[...], tri, preferred_element_type=f32)
    base = jnp.zeros((owners, 1), f32)
    total = jnp.zeros((4 * owners, slots), f32)
    slot_iota = lax.broadcasted_iota(i32, (slots, samples), 0)
    at_hi = lax.shift_right_logical(at, 7).astype(f32)
    at_lo = (at & 127).astype(f32)
    blocks = samples // 128
    for t in range(tables):
        mine = hot[t * owners : (t + 1) * owners, :].astype(f32)
        before = cum[t * owners : (t + 1) * owners, :] + base
        rank = jnp.sum(mine * before, axis=0, keepdims=True).astype(i32)
        base = before[:, samples - 1 :] + mine[:, samples - 1 :]
        local = (place[t : t + 1, :] - frequent) & (owned - 1)
        parts = [
            mine * (at_hi + float((t + 1) * blocks)),
            mine * at_lo,
            mine * (lax.shift_right_logical(local, 7) + 1).astype(f32),
            mine * (local & 127).astype(f32),
        ]
        left = jnp.concatenate(parts, axis=0).astype(bf16)
        total = total + dot_nt(left, one_hot(slot_iota == rank))
    idx[...] = (total[:owners] * 128.0 + total[owners : 2 * owners]).astype(i32)
    row[...] = (total[2 * owners : 3 * owners] - 1.0) * 128.0 + total[3 * owners :]


def values_kernel(hidden, back_low, cot, up, down, bias, out):
    scaled = jnp.dot(hidden[...], up[...], preferred_element_type=f32) + bias[...]
    back = dot_nt(back_low[...], down[...])
    v = cot[...].astype(f32) * (scaled + 1.0) + back
    for k in range(out.shape[0]):
        out[k] = v[:, k * 128 : (k + 1) * 128]


def gather_kernel(idx, values, row, out):
    o = pl.program_id(0)
    slots = out.shape[1] - 8

    def step(i, _):
        at = pl.multiple_of(i * 16, 16)
        for k in range(16):
            src = idx[o, at + k]
            out[0, pl.ds(at + k, 1), :] = values[pl.ds(src, 1), :]
        return 0

    lax.fori_loop(0, slots // 16, step, 0)
    out[0, slots : slots + 8, :] = jnp.zeros((8, 128), f32)
    out[0, slots : slots + 1, :] = row[0, :, 0:128]
    out[0, slots + 1 : slots + 2, :] = row[0, :, 128:256]


def weights_kernel(count, steps, hidden, back_low, cross, cot, values, place, both, freq, hidden_t, down, up):
    g = pl.program_id(0)
    rank = hidden.shape[1]
    wide = cross.shape[1]
    per = wide // 128
    frequent = freq.shape[0]
    block = both.shape[0] // count
    up_rows = rank // count
    width = wide * steps
    down_rows = width // count

    @pl.when(g == 0)
    def _():
        hidden_t[...] = hidden[...].T
        freq[...] = jnp.zeros_like(freq)

    inner = cot[...].astype(f32) * cross[...].astype(f32)
    u = jnp.dot(hidden_t[...], inner.astype(bf16), preferred_element_type=f32)
    for k in range(per):
        up[k * rank : (k + 1) * rank, :] = u[:, k * 128 : (k + 1) * 128]
    d = dot_tn(cross[...], back_low[...])
    for k in range(rank // 128):
        down[pl.ds(pl.multiple_of(k * width + g * wide, 128), wide), :] = d[:, k * 128 : (k + 1) * 128]
    row_iota = lax.broadcasted_iota(i32, (frequent, 512), 0)
    for k in range(per):
        hot = one_hot(row_iota == place[0, k : k + 1, :])
        s = jnp.dot(hot, hi_lo(values[k]), preferred_element_type=f32)
        freq[...] += s[:, :128] + s[:, 128:]

    cols = per * steps

    def put_up(i, _):
        for k in range(per):
            both[pl.ds(i * block + g * per + k, up_rows, stride=cols), :] = up[
                pl.ds(k * rank + i * up_rows, up_rows), :
            ]
        return 0

    lax.fori_loop(0, count, put_up, 0)

    @pl.when(g == steps - 1)
    def _():
        def put_down(i, _):
            for k in range(rank // 128):
                both[pl.ds(i * block + up_rows * cols + k, down_rows, stride=rank // 128), :] = down[
                    pl.ds(k * width + i * down_rows, down_rows), :
                ]
            return 0

        lax.fori_loop(0, count, put_down, 0)


def segment_kernel(arrived, out, acc):
    g = pl.program_id(0)
    owned = out.shape[0]
    slots = arrived.shape[1] - 8

    @pl.when(g == 0)
    def _():
        acc[...] = jnp.zeros_like(acc)

    hots, parts = [], []
    for b in range(arrived.shape[0]):
        r0 = arrived[b, slots : slots + 1, :]
        r1 = arrived[b, slots + 1 : slots + 2, : slots - 128]
        hots.append(jnp.concatenate([r0, r1], axis=1).astype(i32))
        parts.append(hi_lo(arrived[b, :slots, :]))
    rows = jnp.concatenate(hots, axis=1)
    right = jnp.concatenate(parts, axis=0)
    step = 512
    for m in range(0, owned, step):
        hot = one_hot(lax.broadcasted_iota(i32, (step, rows.shape[1]), 0) + m == rows)
        acc[m : m + step, :] += jnp.dot(hot, right, preferred_element_type=f32)

    @pl.when(g == pl.num_programs(0) - 1)
    def _():
        out[...] = acc[:, :128] + acc[:, 128:]


def params(**kw):
    return pltpu.CompilerParams(vmem_limit_bytes=VLIM, **kw)


def body(cross_in, cotangent, weight_down, weight_up, cross_bias, row_place, frequent_table, frequent_accum, shard_table, shard_accum):
    samples, width = cross_in.shape
    rank = weight_down.shape[1]
    tables = row_place.shape[1]
    emb = frequent_table.shape[1]
    f_count = frequent_table.shape[0]
    owned = shard_table.shape[0]
    shards = lax.axis_size("dp")
    count = shards * lax.axis_size("rep")
    capacity = samples * tables // (2 * shards)
    blocks = width // emb
    per = 3
    steps = blocks // per
    wide = per * emb
    vmem = pl.BlockSpec(memory_space=pltpu.VMEM)

    place_t = row_place.T
    idx, row = pl.pallas_call(
        functools.partial(index_kernel, f_count, owned),
        out_shape=(jax.ShapeDtypeStruct((shards, 256), i32), jax.ShapeDtypeStruct((shards, 256), f32)),
        in_specs=[vmem],
        out_specs=(vmem, vmem),
        scratch_shapes=[pltpu.VMEM((tables * shards, samples), bf16), pltpu.VMEM((tables * shards, samples), f32)],
        compiler_params=params(),
        name="index_kernel",
    )(place_t)

    hidden = jnp.dot(cross_in, weight_down, preferred_element_type=f32).astype(bf16)
    inner = cotangent.astype(f32) * cross_in.astype(f32)
    back_low = lax.dot_general(
        inner.astype(bf16), weight_up, (((1,), (1,)), ((), ())), preferred_element_type=f32
    ).astype(bf16)

    values = pl.pallas_call(
        values_kernel,
        grid=(steps,),
        out_shape=jax.ShapeDtypeStruct((blocks, samples, emb), f32),
        in_specs=[
            pl.BlockSpec((samples, rank), lambda g: (0, 0)),
            pl.BlockSpec((samples, rank), lambda g: (0, 0)),
            pl.BlockSpec((samples, wide), lambda g: (0, g)),
            pl.BlockSpec((rank, wide), lambda g: (0, g)),
            pl.BlockSpec((wide, rank), lambda g: (g, 0)),
            pl.BlockSpec((1, wide), lambda g: (0, g)),
        ],
        out_specs=pl.BlockSpec((per, samples, emb), lambda g: (g, 0, 0)),
        compiler_params=params(),
        name="values_kernel",
    )(hidden, back_low, cotangent, weight_up, weight_down, cross_bias.reshape(1, -1))

    bucket = pl.pallas_call(
        gather_kernel,
        grid=(shards,),
        out_shape=jax.ShapeDtypeStruct((shards, capacity + 8, emb), f32),
        in_specs=[
            pl.BlockSpec(memory_space=pltpu.SMEM),
            pl.BlockSpec((blocks * samples, emb), lambda g: (0, 0)),
            pl.BlockSpec((1, 1, 256), lambda g: (g, 0, 0)),
        ],
        out_specs=pl.BlockSpec((1, capacity + 8, emb), lambda g: (g, 0, 0)),
        compiler_params=params(),
        name="gather_kernel",
    )(idx, values.reshape(blocks * samples, emb), row.reshape(shards, 1, 256))

    arrived = lax.all_to_all(bucket, "dp", split_axis=0, concat_axis=0, tiled=True)

    place3 = jnp.concatenate([jnp.full((1, samples), -1, i32), place_t], axis=0).reshape(steps, per, samples)
    block = rank * width // count // 128 * 2
    both, freq = pl.pallas_call(
        functools.partial(weights_kernel, count, steps),
        grid=(steps,),
        out_shape=(
            jax.ShapeDtypeStruct((count * block, 128), f32),
            jax.ShapeDtypeStruct((f_count, emb), f32),
        ),
        in_specs=[
            pl.BlockSpec((samples, rank), lambda g: (0, 0)),
            pl.BlockSpec((samples, rank), lambda g: (0, 0)),
            pl.BlockSpec((samples, wide), lambda g: (0, g)),
            pl.BlockSpec((samples, wide), lambda g: (0, g)),
            pl.BlockSpec((per, samples, emb), lambda g: (g, 0, 0)),
            pl.BlockSpec((1, per, samples), lambda g: (g, 0, 0)),
        ],
        out_specs=(
            pl.BlockSpec((count * block, 128), lambda g: (0, 0)),
            pl.BlockSpec((f_count, emb), lambda g: (0, 0)),
        ),
        scratch_shapes=[
            pltpu.VMEM((rank, samples), bf16),
            pltpu.VMEM((rank // 128 * width, 128), f32),
            pltpu.VMEM((per * rank, 128), f32),
        ],
        compiler_params=params(),
        name="weights_kernel",
    )(hidden, back_low, cross_in, cotangent, values, place3)
    local_bias = jnp.sum(inner, axis=0)

    mine = lax.psum_scatter(both, ("dp", "rep"), scatter_dimension=0, tiled=True)
    mine = lax.optimization_barrier(mine)
    small = jnp.concatenate([freq, local_bias.reshape(blocks, emb)], axis=0)
    small = lax.psum(jnp.pad(small, ((0, -small.shape[0] % 8), (0, 0))), ("dp", "rep"))
    me = lax.axis_index("dp") * lax.axis_size("rep") + lax.axis_index("rep")
    bias_all = small[f_count : f_count + blocks].reshape(-1)
    grad_bias = lax.dynamic_slice(bias_all, (me * (width // count),), (width // count,))
    grad_up = mine[: block // 2].reshape(rank // count, width)
    grad_down = mine[block // 2 :].reshape(width // count, rank)

    shard_grad = pl.pallas_call(
        segment_kernel,
        grid=(shards // 4,),
        out_shape=jax.ShapeDtypeStruct((owned, emb), f32),
        in_specs=[pl.BlockSpec((4, capacity + 8, emb), lambda g: (g, 0, 0))],
        out_specs=pl.BlockSpec((owned, emb), lambda g: (0, 0)),
        scratch_shapes=[pltpu.VMEM((owned, 256), f32)],
        compiler_params=params(),
        name="segment_kernel",
    )(arrived)
    shard_grad = lax.psum(shard_grad, "rep")
    new_shard, new_shard_accum = row_adagrad(shard_table, shard_accum, shard_grad)
    new_frequent, new_frequent_accum = row_adagrad(frequent_table, frequent_accum, small[:f_count])
    return (new_frequent, new_frequent_accum, new_shard, new_shard_accum, grad_up, grad_down, grad_bias)


def solution(mesh):
    both = ("dp", "rep")
    in_specs = (P(both, None), P(both, None), P(), P(), P(), P(both, None), P(), P(), P("dp", None), P("dp"))
    out_specs = (P(), P(), P("dp", None), P("dp"), P(both, None), P(both, None), P(both))
    return jax.shard_map(body, mesh=mesh, in_specs=in_specs, out_specs=out_specs, check_vma=False)
```

```python
import functools
import jax
import jax.numpy as jnp
from jax import lax
from jax.experimental import pallas as pl
from jax.experimental.pallas import tpu as pltpu
from jax.sharding import PartitionSpec as P

learn_rate = 0.05
eps_ada = 1e-08
f32, bf16, i32 = jnp.float32, jnp.bfloat16, jnp.int32
VLIM = 60 * 1024 * 1024


def row_adagrad(table, accum, grad):
    accum_new = accum + jnp.mean(grad * grad, axis=1)
    return (table - learn_rate * grad / (jnp.sqrt(accum_new)[:, None] + eps_ada), accum_new)


def dot_nt(a, b):
    return lax.dot_general(a, b, (((1,), (1,)), ((), ())), preferred_element_type=f32)


def dot_tn(a, b):
    return lax.dot_general(a, b, (((0,), (0,)), ((), ())), preferred_element_type=f32)


def hi_lo(v):
    hi = v.astype(bf16)
    lo = (v - hi.astype(f32)).astype(bf16)
    return jnp.concatenate([hi, lo], axis=1)


def one_hot(flags):
    return jnp.where(flags, 1.0, 0.0).astype(bf16)


def index_kernel(frequent, owned, place, idx, row, hot, cum):
    tables, samples = place.shape
    owners, slots = idx.shape
    at = lax.broadcasted_iota(i32, (1, samples), 1)
    owner_iota = lax.broadcasted_iota(i32, (owners, samples), 0)
    tri = one_hot(
        lax.broadcasted_iota(i32, (samples, samples), 0)
        < lax.broadcasted_iota(i32, (samples, samples), 1)
    )
    shift = owned.bit_length() - 1
    for t in range(tables):
        owner = lax.shift_right_arithmetic(place[t : t + 1, :] - frequent, shift)
        hot[t * owners : (t + 1) * owners, :] = one_hot(owner_iota == owner)
    cum[...] = jnp.dot(hot[...], tri, preferred_element_type=f32)
    base = jnp.zeros((owners, 1), f32)
    total = jnp.zeros((4 * owners, slots), f32)
    slot_iota = lax.broadcasted_iota(i32, (slots, samples), 0)
    at_hi = lax.shift_right_logical(at, 7).astype(f32)
    at_lo = (at & 127).astype(f32)
    blocks = samples // 128
    for t in range(tables):
        mine = hot[t * owners : (t + 1) * owners, :].astype(f32)
        before = cum[t * owners : (t + 1) * owners, :] + base
        rank = jnp.sum(mine * before, axis=0, keepdims=True).astype(i32)
        base = before[:, samples - 1 :] + mine[:, samples - 1 :]
        local = (place[t : t + 1, :] - frequent) & (owned - 1)
        parts = [
            mine * (at_hi + float((t + 1) * blocks)),
            mine * at_lo,
            mine * (lax.shift_right_logical(local, 7) + 1).astype(f32),
            mine * (local & 127).astype(f32),
        ]
        left = jnp.concatenate(parts, axis=0).astype(bf16)
        total = total + dot_nt(left, one_hot(slot_iota == rank))
    idx[...] = (total[:owners] * 128.0 + total[owners : 2 * owners]).astype(i32)
    row[...] = (total[2 * owners : 3 * owners] - 1.0) * 128.0 + total[3 * owners :]


def values_kernel(hidden, back_low, cot, up, down, bias, out):
    scaled = jnp.dot(hidden[...], up[...], preferred_element_type=f32) + bias[...]
    back = dot_nt(back_low[...], down[...])
    v = cot[...].astype(f32) * (scaled + 1.0) + back
    for k in range(out.shape[0]):
        out[k] = v[:, k * 128 : (k + 1) * 128]


def gather_kernel(idx, values, row, out):
    o = pl.program_id(0)
    slots = out.shape[1] - 8

    def step(i, _):
        at = pl.multiple_of(i * 16, 16)
        for k in range(16):
            src = idx[o, at + k]
            out[0, pl.ds(at + k, 1), :] = values[pl.ds(src, 1), :]
        return 0

    lax.fori_loop(0, slots // 16, step, 0)
    out[0, slots : slots + 8, :] = jnp.zeros((8, 128), f32)
    out[0, slots : slots + 1, :] = row[0, :, 0:128]
    out[0, slots + 1 : slots + 2, :] = row[0, :, 128:256]


def weights_kernel(count, steps, hidden, back_low, cross, cot, values, place, both, bias, freq, hidden_t, down, up):
    g = pl.program_id(0)
    rank = hidden.shape[1]
    wide = cross.shape[1]
    per = wide // 128
    frequent = freq.shape[0]
    block = both.shape[0] // count
    up_rows = rank // count
    width = wide * steps
    down_rows = width // count

    @pl.when(g == 0)
    def _():
        hidden_t[...] = hidden[...].T
        freq[...] = jnp.zeros_like(freq)

    inner = cot[...].astype(f32) * cross[...].astype(f32)
    bias[...] = jnp.sum(inner, axis=0, keepdims=True)
    u = jnp.dot(hidden_t[...], inner.astype(bf16), preferred_element_type=f32)
    for k in range(per):
        up[k * rank : (k + 1) * rank, :] = u[:, k * 128 : (k + 1) * 128]
    d = dot_tn(cross[...], back_low[...])
    for k in range(rank // 128):
        down[pl.ds(pl.multiple_of(k * width + g * wide, 128), wide), :] = d[:, k * 128 : (k + 1) * 128]
    row_iota = lax.broadcasted_iota(i32, (frequent, 512), 0)
    for k in range(per):
        hot = one_hot(row_iota == place[0, k : k + 1, :])
        s = jnp.dot(hot, hi_lo(values[k]), preferred_element_type=f32)
        freq[...] += s[:, :128] + s[:, 128:]

    cols = per * steps

    def put_up(i, _):
        for k in range(per):
            both[pl.ds(i * block + g * per + k, up_rows, stride=cols), :] = up[
                pl.ds(k * rank + i * up_rows, up_rows), :
            ]
        return 0

    lax.fori_loop(0, count, put_up, 0)

    @pl.when(g == steps - 1)
    def _():
        def put_down(i, _):
            for k in range(rank // 128):
                both[pl.ds(i * block + up_rows * cols + k, down_rows, stride=rank // 128), :] = down[
                    pl.ds(k * width + i * down_rows, down_rows), :
                ]
            both[pl.ds(i * block + block - 8, 8), :] = freq[pl.ds(pl.multiple_of(i * 8, 8), 8), :]
            return 0

        lax.fori_loop(0, count, put_down, 0)


def segment_kernel(arrived, out, acc):
    g = pl.program_id(0)
    owned = out.shape[0]
    slots = arrived.shape[1] - 8

    @pl.when(g == 0)
    def _():
        acc[...] = jnp.zeros_like(acc)

    hots, parts = [], []
    for b in range(arrived.shape[0]):
        r0 = arrived[b, slots : slots + 1, :]
        r1 = arrived[b, slots + 1 : slots + 2, : slots - 128]
        hots.append(jnp.concatenate([r0, r1], axis=1).astype(i32))
        parts.append(hi_lo(arrived[b, :slots, :]))
    rows = jnp.concatenate(hots, axis=1)
    right = jnp.concatenate(parts, axis=0)
    step = 512
    for m in range(0, owned, step):
        hot = one_hot(lax.broadcasted_iota(i32, (step, rows.shape[1]), 0) + m == rows)
        acc[m : m + step, :] += jnp.dot(hot, right, preferred_element_type=f32)

    @pl.when(g == pl.num_programs(0) - 1)
    def _():
        out[...] = acc[:, :128] + acc[:, 128:]


PORT = ((0, 96, 48, "xzy"), (96, 96, 48, "zxy"), (192, 40, 24, "yxz"))


def params(**kw):
    return pltpu.CompilerParams(vmem_limit_bytes=VLIM, **kw)


def reduce_kernel(both, bias, seg, mine, freq_out, seg_out, *scratch):
    n_port = len(PORT)
    it = iter(scratch)
    work = [next(it) for _ in PORT]
    pair = [next(it) for _ in PORT]
    land = [[[next(it) for _ in range(4)] for _ in range(3)] for _ in PORT]
    swork = next(it)
    sland = [next(it) for _ in range(4)]
    sgath = next(it)
    gath = next(it)
    send_sems, recv_sems, local_sems = next(it), next(it), next(it)

    dp, y = lax.axis_index("dp"), lax.axis_index("rep")
    me = {"x": dp // 8, "z": (dp // 2) % 4, "y": y}
    core = dp % 2

    def device(axis, to):
        at = dict(me, **{axis: to})
        return ((at["x"] * 4 + at["z"]) * 2 + core, at["y"])

    partner = (dp + 1 - 2 * core, y)
    up = {a: (me[a] + 1) % 4 for a in "xzy"}
    down = {a: (me[a] + 3) % 4 for a in "xzy"}
    far = {a: (me[a] + 2) % 4 for a in "xzy"}
    peers = [partner] + [device(a, s[a]) for a in "xzy" for s in (up, down)]
    barrier = pltpu.get_barrier_semaphore()
    for peer in peers:
        pl.semaphore_signal(barrier, inc=1, device_id=peer, device_id_type=pl.DeviceIdType.MESH)
    pl.semaphore_wait(barrier, len(peers))

    sent, used = [], [0]

    def send(src, dst, to):
        k = used[0]
        used[0] += 1
        copy = pltpu.make_async_remote_copy(
            src_ref=src, dst_ref=dst, send_sem=send_sems.at[k], recv_sem=recv_sems.at[k],
            device_id=to, device_id_type=pl.DeviceIdType.MESH,
        )
        copy.start()
        sent.append(copy)
        return copy

    def place(done, axis, t, rem=None):
        rem = iter(rem) if rem is not None else None
        out = []
        for a in "xzy":
            if a in done:
                out.append(me[a])
            elif a == axis:
                out.append(t)
            else:
                out.append(slice(None) if rem is None else next(rem))
        return tuple(out)

    def each(n_rem, fn):
        if n_rem == 0:
            fn(())
        elif n_rem == 1:
            lax.fori_loop(0, 4, lambda i, _: (fn((i,)), 0)[1], 0)
        else:
            lax.fori_loop(0, 16, lambda i, _: (fn((i // 4, i % 4)), 0)[1], 0)

    class Reduce:
        def __init__(self, ref, done, axis, rows, half, lands, free=2):
            self.ref, self.done, self.axis, self.rows, self.half, self.lands = ref, done, axis, rows, half, lands
            self.n = free

        def at(self, t, lo, hi):
            if self.done is None:
                return self.ref.at[t, pl.ds(lo, hi - lo), :]
            return self.ref.at[place(self.done, self.axis, t) + (pl.ds(lo, hi - lo), slice(None))]

        def add(self, t, lo, hi, *refs):
            def one(rem):
                if self.done is None:
                    step = 128
                    for r in range(lo, hi, step):
                        v = self.ref[t, r : r + step, :]
                        for ref in refs:
                            v = v + ref[r - lo : r - lo + step, :]
                        self.ref[t, r : r + step, :] = v
                    return
                where = place(self.done, self.axis, t, rem)
                v = self.ref[where + (slice(lo, hi), slice(None))]
                for ref in refs:
                    v = v + ref[rem + (slice(None), slice(None))]
                self.ref[where + (slice(lo, hi), slice(None))] = v

            each(self.n, one)

        def start(self):
            a = self.axis
            self.c0 = send(self.at(far[a], 0, self.half), self.lands[0], device(a, up[a]))
            self.c1 = send(self.at(far[a], self.half, self.rows), self.lands[1], device(a, down[a]))

        def middle(self):
            a = self.axis
            self.c0.wait_recv()
            self.add(up[a], 0, self.half, self.lands[0])
            self.c2 = send(self.at(up[a], 0, self.rows), self.lands[2], device(a, up[a]))
            self.c1.wait_recv()
            self.add(down[a], self.half, self.rows, self.lands[1])
            self.c3 = send(self.at(down[a], 0, self.rows), self.lands[3], device(a, down[a]))

        def finish(self):
            self.c2.wait_recv()
            self.c3.wait_recv()
            self.add(me[self.axis], 0, self.rows, self.lands[2], self.lands[3])

    class Gather:
        def __init__(self, axis, at):
            self.axis, self.at = axis, at

        def start(self):
            a = self.axis
            src = self.at(me[a], None)
            self.c0 = send(src, src, device(a, up[a]))
            self.c1 = send(src, src, device(a, down[a]))

        def middle(self):
            a = self.axis
            self.c0.wait_recv()
            src = self.at(down[a], 0)
            self.c2 = send(src, src, device(a, up[a]))
            self.c1.wait_recv()
            src = self.at(up[a], 1)
            self.c3 = None
            if src is not None:
                self.c3 = send(src, src, device(a, down[a]))

        def finish(self):
            self.c2.wait_recv()
            if self.c3 is not None:
                self.c3.wait_recv()

    firsts, locals_ = [], []
    for p, (first, rows, half, order) in enumerate(PORT):
        whole = rows if p < n_port - 1 else rows - 8
        got = [
            send(
                both.at[:, :, 1 - core, :, pl.ds(first, whole), :],
                pair[p].at[:, :, :, pl.ds(0, whole), :],
                partner,
            )
        ]
        loc = [pltpu.make_async_copy(
            both.at[:, :, core, :, pl.ds(first, whole), :], work[p].at[:, :, :, pl.ds(0, whole), :], local_sems.at[p])]
        if p == n_port - 1:
            got.append(send(bias.at[:, :, 1 - core], pair[p].at[:, :, :, pl.ds(whole, 8), :], partner))
            loc.append(pltpu.make_async_copy(
                bias.at[:, :, core], work[p].at[:, :, :, pl.ds(whole, 8), :], local_sems.at[n_port]))
        for c in loc:
            c.start()
        firsts.append(got)
        locals_.append(loc)
    load = pltpu.make_async_copy(seg, swork, local_sems.at[n_port + 1])
    load.start()
    load.wait()
    owned = swork.shape[1]
    s_red = Reduce(swork, None, "y", owned, owned // 2, sland, 0)
    s_red.start()

    reds = []
    for p, (first, rows, half, order) in enumerate(PORT):
        phases = []
        for k in range(3):
            phases.append(Reduce(work[p], order[:k], order[k], rows, half, land[p][k], 2 - k))
        reds.append(phases)

    def begin(p):
        for c in locals_[p]:
            c.wait()
        for c in firsts[p]:
            c.wait_recv()

        def one(i, _):
            w = (i // 16, (i // 4) % 4, i % 4)
            work[p][w] = work[p][w] + pair[p][w]
            return 0

        lax.fori_loop(0, 64, one, 0)
        reds[p][0].start()

    def s_half(t, h):
        if h is None:
            return sgath.at[t]
        return sgath.at[t, pl.ds(h * (owned // 2), owned // 2), :]

    s_gat = Gather("y", s_half)

    def y_at(t, h):
        return None if h == 1 else gath.at[me["x"], me["z"], core, t]

    def z_at(t, h):
        return gath.at[me["x"], t, core] if h is None else gath.at[me["x"], t, core, pl.ds(2 * h, 2)]

    def x_at(t, h):
        return gath.at[t, :, core] if h is None else gath.at[t, pl.ds(2 * h, 2), core]

    g_y, g_z, g_x = Gather("y", y_at), Gather("z", z_at), Gather("x", x_at)
    here = (me["x"], me["z"], me["y"])

    begin(2)
    begin(0)
    begin(1)
    s_red.middle()
    reds[2][0].middle()
    reds[0][0].middle()
    reds[1][0].middle()
    reds[2][0].finish()
    reds[2][1].start()
    s_red.finish()
    sgath[me["y"]] = swork[me["y"]]
    s_gat.start()
    reds[2][1].middle()
    reds[2][1].finish()
    reds[2][2].start()
    reds[2][2].middle()
    reds[2][2].finish()
    last = n_port - 1
    rows_last = PORT[last][1]
    gath[me["x"], me["z"], core, me["y"]] = work[last][here + (slice(rows_last - 16, rows_last - 8), slice(None))]
    g_y.start()
    s_gat.middle()
    g_y.middle()
    reds[0][0].finish()
    reds[0][1].start()
    reds[1][0].finish()
    reds[1][1].start()
    g_y.finish()
    g_z.start()
    s_gat.finish()
    reds[0][1].middle()
    reds[1][1].middle()
    g_z.middle()
    reds[0][1].finish()
    reds[0][2].start()
    reds[1][1].finish()
    reds[1][2].start()
    g_z.finish()
    g_x.start()
    reds[0][2].middle()
    reds[1][2].middle()
    g_x.middle()
    reds[0][2].finish()
    reds[1][2].finish()
    g_x.finish()
    g_c = send(gath.at[:, :, core], gath.at[:, :, core], partner)
    for p, (first, rows, half, order) in enumerate(PORT):
        mine[first : first + rows, :] = work[p][here]
    seg_out[...] = sgath[...]
    g_c.wait_recv()
    freq_out[...] = gath[...]
    for c in sent:
        c.wait_send()


def reduce_scratch(owned):
    v = lambda *s: pltpu.VMEM(s, f32)
    out = [v(4, 4, 4, r, 128) for _, r, _, _ in PORT] * 2
    for _, r, h, _ in PORT:
        for k in range(3):
            lead = (4,) * (2 - k)
            out += [v(*lead, h, 128), v(*lead, r - h, 128), v(*lead, r, 128), v(*lead, r, 128)]
    out += [v(4, owned // 4, 128), v(owned // 8, 128), v(owned // 8, 128), v(owned // 4, 128), v(owned // 4, 128), v(4, owned // 4, 128)]
    out += [v(4, 4, 2, 4, 8, 128)]
    out += [pltpu.SemaphoreType.DMA((80,)), pltpu.SemaphoreType.DMA((80,)), pltpu.SemaphoreType.DMA((8,))]
    return out


def reduce_all(both, bias, seg):
    owned = seg.shape[0]
    per = both.shape[0] // 128
    vmem = pl.BlockSpec(memory_space=pltpu.VMEM)
    anyw = pl.BlockSpec(memory_space=pl.ANY)
    mine, freq, seg = pl.pallas_call(
        reduce_kernel,
        out_shape=(
            jax.ShapeDtypeStruct((per + 8, 128), f32),
            jax.ShapeDtypeStruct((4, 4, 2, 4, 8, 128), f32),
            jax.ShapeDtypeStruct((4, owned // 4, 128), f32),
        ),
        in_specs=[anyw, anyw, anyw],
        out_specs=(vmem, vmem, vmem),
        scratch_shapes=reduce_scratch(owned),
        compiler_params=params(collective_id=0, has_side_effects=True),
        name="reduce_kernel",
    )(both.reshape(4, 4, 2, 4, per, 128), bias.reshape(4, 4, 2, 4, 8, 128), seg.reshape(4, owned // 4, 128))
    return mine, freq.reshape(1024, 128), seg.reshape(owned, 128)


def body(cross_in, cotangent, weight_down, weight_up, cross_bias, row_place, frequent_table, frequent_accum, shard_table, shard_accum):
    samples, width = cross_in.shape
    rank = weight_down.shape[1]
    tables = row_place.shape[1]
    emb = frequent_table.shape[1]
    f_count = frequent_table.shape[0]
    owned = shard_table.shape[0]
    shards = lax.axis_size("dp")
    count = shards * lax.axis_size("rep")
    capacity = samples * tables // (2 * shards)
    blocks = width // emb
    per = 3
    steps = blocks // per
    wide = per * emb
    vmem = pl.BlockSpec(memory_space=pltpu.VMEM)

    place_t = row_place.T
    idx, row = pl.pallas_call(
        functools.partial(index_kernel, f_count, owned),
        out_shape=(jax.ShapeDtypeStruct((shards, 256), i32), jax.ShapeDtypeStruct((shards, 256), f32)),
        in_specs=[vmem],
        out_specs=(vmem, vmem),
        scratch_shapes=[pltpu.VMEM((tables * shards, samples), bf16), pltpu.VMEM((tables * shards, samples), f32)],
        compiler_params=params(),
        name="index_kernel",
    )(place_t)

    hidden = jnp.dot(cross_in, weight_down, preferred_element_type=f32).astype(bf16)
    inner = cotangent.astype(f32) * cross_in.astype(f32)
    back_low = lax.dot_general(
        inner.astype(bf16), weight_up, (((1,), (1,)), ((), ())), preferred_element_type=f32
    ).astype(bf16)

    values = pl.pallas_call(
        values_kernel,
        grid=(steps,),
        out_shape=jax.ShapeDtypeStruct((blocks, samples, emb), f32),
        in_specs=[
            pl.BlockSpec((samples, rank), lambda g: (0, 0)),
            pl.BlockSpec((samples, rank), lambda g: (0, 0)),
            pl.BlockSpec((samples, wide), lambda g: (0, g)),
            pl.BlockSpec((rank, wide), lambda g: (0, g)),
            pl.BlockSpec((wide, rank), lambda g: (g, 0)),
            pl.BlockSpec((1, wide), lambda g: (0, g)),
        ],
        out_specs=pl.BlockSpec((per, samples, emb), lambda g: (g, 0, 0)),
        compiler_params=params(),
        name="values_kernel",
    )(hidden, back_low, cotangent, weight_up, weight_down, cross_bias.reshape(1, -1))

    bucket = pl.pallas_call(
        gather_kernel,
        grid=(shards,),
        out_shape=jax.ShapeDtypeStruct((shards, capacity + 8, emb), f32),
        in_specs=[
            pl.BlockSpec(memory_space=pltpu.SMEM),
            pl.BlockSpec((blocks * samples, emb), lambda g: (0, 0)),
            pl.BlockSpec((1, 1, 256), lambda g: (g, 0, 0)),
        ],
        out_specs=pl.BlockSpec((1, capacity + 8, emb), lambda g: (g, 0, 0)),
        compiler_params=params(),
        name="gather_kernel",
    )(idx, values.reshape(blocks * samples, emb), row.reshape(shards, 1, 256))

    arrived = lax.all_to_all(bucket, "dp", split_axis=0, concat_axis=0, tiled=True)

    place3 = jnp.concatenate([jnp.full((1, samples), -1, i32), place_t], axis=0).reshape(steps, per, samples)
    block = rank * width // count // 128 * 2 + f_count // count
    both, bias = pl.pallas_call(
        functools.partial(weights_kernel, count, steps),
        grid=(steps,),
        out_shape=(
            jax.ShapeDtypeStruct((count * block, 128), f32),
            jax.ShapeDtypeStruct((1, width), f32),
        ),
        in_specs=[
            pl.BlockSpec((samples, rank), lambda g: (0, 0)),
            pl.BlockSpec((samples, rank), lambda g: (0, 0)),
            pl.BlockSpec((samples, wide), lambda g: (0, g)),
            pl.BlockSpec((samples, wide), lambda g: (0, g)),
            pl.BlockSpec((per, samples, emb), lambda g: (g, 0, 0)),
            pl.BlockSpec((1, per, samples), lambda g: (g, 0, 0)),
        ],
        out_specs=(
            pl.BlockSpec((count * block, 128), lambda g: (0, 0)),
            pl.BlockSpec((1, wide), lambda g: (0, g)),
        ),
        scratch_shapes=[
            pltpu.VMEM((f_count, emb), f32),
            pltpu.VMEM((rank, samples), bf16),
            pltpu.VMEM((rank // 128 * width, 128), f32),
            pltpu.VMEM((per * rank, 128), f32),
        ],
        compiler_params=params(),
        name="weights_kernel",
    )(hidden, back_low, cross_in, cotangent, values, place3)
    bias = jnp.pad(bias.reshape(count, 1, width // count), ((0, 0), (0, 7), (0, 128 - width // count)))

    shard_grad = pl.pallas_call(
        segment_kernel,
        grid=(shards // 4,),
        out_shape=jax.ShapeDtypeStruct((owned, emb), f32),
        in_specs=[pl.BlockSpec((4, capacity + 8, emb), lambda g: (g, 0, 0))],
        out_specs=pl.BlockSpec((owned, emb), lambda g: (0, 0)),
        scratch_shapes=[pltpu.VMEM((owned, 256), f32)],
        compiler_params=params(),
        name="segment_kernel",
    )(arrived)
    mine, freq, shard_grad = reduce_all(both, bias, shard_grad)
    n = rank * width // count // 128
    grad_up = mine[:n].reshape(rank // count, width)
    grad_down = mine[n : 2 * n].reshape(width // count, rank)
    grad_bias = mine[block, : width // count]
    new_shard, new_shard_accum = row_adagrad(shard_table, shard_accum, shard_grad)
    new_frequent, new_frequent_accum = row_adagrad(frequent_table, frequent_accum, freq)
    return (new_frequent, new_frequent_accum, new_shard, new_shard_accum, grad_up, grad_down, grad_bias)


def solution(mesh):
    both = ("dp", "rep")
    in_specs = (P(both, None), P(both, None), P(), P(), P(), P(both, None), P(), P(), P("dp", None), P("dp"))
    out_specs = (P(), P(), P("dp", None), P("dp"), P(both, None), P(both, None), P(both))
    return jax.shard_map(body, mesh=mesh, in_specs=in_specs, out_specs=out_specs, check_vma=False)
```

```python
import functools
import jax
import jax.numpy as jnp
from jax import lax
from jax.experimental import pallas as pl
from jax.experimental.pallas import tpu as pltpu
from jax.sharding import PartitionSpec as P

learn_rate = 0.05
eps_ada = 1e-08
f32, bf16, i32 = jnp.float32, jnp.bfloat16, jnp.int32
VLIM = 60 * 1024 * 1024


def row_adagrad(table, accum, grad):
    accum_new = accum + jnp.mean(grad * grad, axis=1)
    return (table - learn_rate * grad / (jnp.sqrt(accum_new)[:, None] + eps_ada), accum_new)


def dot_nt(a, b):
    return lax.dot_general(a, b, (((1,), (1,)), ((), ())), preferred_element_type=f32)


def dot_tn(a, b):
    return lax.dot_general(a, b, (((0,), (0,)), ((), ())), preferred_element_type=f32)


def hi_lo(v):
    hi = v.astype(bf16)
    lo = (v - hi.astype(f32)).astype(bf16)
    return jnp.concatenate([hi, lo], axis=1)


def one_hot(flags):
    return jnp.where(flags, 1.0, 0.0).astype(bf16)


def index_work(frequent, owned, place, idx, row_a, row_b, hot, cum):
    tables, samples = place.shape
    owners, slots = idx.shape
    at = lax.broadcasted_iota(i32, (1, samples), 1)
    owner_iota = lax.broadcasted_iota(i32, (owners, samples), 0)
    tri = one_hot(
        lax.broadcasted_iota(i32, (samples, samples), 0)
        < lax.broadcasted_iota(i32, (samples, samples), 1)
    )
    shift = owned.bit_length() - 1
    for t in range(tables):
        owner = lax.shift_right_arithmetic(place[t : t + 1, :] - frequent, shift)
        hot[t * owners : (t + 1) * owners, :] = one_hot(owner_iota == owner)
    cum[...] = jnp.dot(hot[...], tri, preferred_element_type=f32)
    base = jnp.zeros((owners, 1), f32)
    total = jnp.zeros((4 * owners, slots), f32)
    slot_iota = lax.broadcasted_iota(i32, (slots, samples), 0)
    at_hi = lax.shift_right_logical(at, 7).astype(f32)
    at_lo = (at & 127).astype(f32)
    blocks = samples // 128
    for t in range(tables):
        mine = hot[t * owners : (t + 1) * owners, :].astype(f32)
        before = cum[t * owners : (t + 1) * owners, :] + base
        rank = jnp.sum(mine * before, axis=0, keepdims=True).astype(i32)
        base = before[:, samples - 1 :] + mine[:, samples - 1 :]
        local = (place[t : t + 1, :] - frequent) & (owned - 1)
        parts = [
            mine * (at_hi + float((t + 1) * blocks)),
            mine * at_lo,
            mine * (lax.shift_right_logical(local, 7) + 1).astype(f32),
            mine * (local & 127).astype(f32),
        ]
        left = jnp.concatenate(parts, axis=0).astype(bf16)
        total = total + dot_nt(left, one_hot(slot_iota == rank))
    idx[...] = (total[:owners] * 128.0 + total[owners : 2 * owners]).astype(i32)
    row = (total[2 * owners : 3 * owners] - 1.0) * 128.0 + total[3 * owners :]
    row_a[...] = row[:, :128]
    row_b[...] = row[:, 128:]


def front_kernel(
    frequent, owned, place, bias, cross_hbm, cot_hbm, down_hbm, up_hbm,
    hidden, back_low, values_hbm, bucket_hbm,
    cross, cot, down, up, values, bucket, hot, cum, idx_v, row_a, row_b, idx, h_acc, b_acc, in_sems, v_sems, b_sems, i_sem,
):
    samples = hidden.shape[0]
    emb = values.shape[1]
    steps = in_sems.shape[0]
    wide = cross.shape[1] // steps
    per = wide // emb
    owners = bucket.shape[0]
    slots = bucket.shape[1] - 8

    def loads(g):
        cols = pl.ds(pl.multiple_of(g * wide, wide), wide)
        return [
            pltpu.make_async_copy(cross_hbm.at[:, cols], cross.at[:, cols], in_sems.at[g, 0]),
            pltpu.make_async_copy(cot_hbm.at[:, cols], cot.at[:, cols], in_sems.at[g, 1]),
            pltpu.make_async_copy(down_hbm.at[cols, :], down.at[cols, :], in_sems.at[g, 2]),
            pltpu.make_async_copy(up_hbm.at[:, cols], up.at[:, cols], in_sems.at[g, 3]),
        ]

    for g in range(steps):
        for c in loads(g):
            c.start()
    index_work(frequent, owned, place, idx_v, row_a, row_b, hot, cum)
    to_scalar = pltpu.make_async_copy(idx_v, idx, i_sem)
    to_scalar.start()
    h_acc[...] = jnp.zeros_like(h_acc)
    b_acc[...] = jnp.zeros_like(b_acc)

    def low(g, _):
        for c in loads(g):
            c.wait()
        cols = pl.ds(pl.multiple_of(g * wide, wide), wide)
        x = cross[:, cols]
        inner = (cot[:, cols].astype(f32) * x.astype(f32)).astype(bf16)
        h_acc[...] += jnp.dot(x, down[cols, :], preferred_element_type=f32)
        b_acc[...] += dot_nt(inner, up[:, cols])
        return 0

    lax.fori_loop(0, steps, low, 0)
    hidden[...] = h_acc[...].astype(bf16)
    back_low[...] = b_acc[...].astype(bf16)

    def store(g):
        part = pl.ds(pl.multiple_of(g * per * samples, 128), per * samples)
        return pltpu.make_async_copy(values.at[part], values_hbm.at[part], v_sems.at[g])

    def high(g, _):
        cols = pl.ds(pl.multiple_of(g * wide, wide), wide)
        scaled = jnp.dot(hidden[...], up[:, cols], preferred_element_type=f32) + bias[:, cols]
        v = cot[:, cols].astype(f32) * (scaled + 1.0) + dot_nt(back_low[...], down[cols, :])
        for k in range(per):
            values[pl.ds(pl.multiple_of((g * per + k) * samples, 128), samples), :] = v[:, k * emb : (k + 1) * emb]
        store(g).start()
        return 0

    lax.fori_loop(0, steps, high, 0)
    to_scalar.wait()

    def ship(o):
        return pltpu.make_async_copy(bucket.at[o], bucket_hbm.at[o], b_sems.at[o])

    def pick(o, _):
        for k in range(slots):
            src = idx[o, k]
            bucket[o, k : k + 1, :] = values[pl.ds(src, 1), :]
        bucket[o, slots : slots + 8, :] = jnp.zeros((8, emb), f32)
        bucket[o, slots : slots + 1, :] = row_a[pl.ds(o, 1), :]
        bucket[o, slots + 1 : slots + 2, :] = row_b[pl.ds(o, 1), :]
        ship(o).start()
        return 0

    lax.fori_loop(0, owners, pick, 0)
    lax.fori_loop(0, steps, lambda g, _: (store(g).wait(), 0)[1], 0)
    lax.fori_loop(0, owners, lambda o, _: (ship(o).wait(), 0)[1], 0)


def weights_kernel(count, steps, hidden, back_low, cross, cot, values, place, both, bias, freq, hidden_t, down, up):
    g = pl.program_id(0)
    rank = hidden.shape[1]
    wide = cross.shape[1]
    per = wide // 128
    frequent = freq.shape[0]
    block = both.shape[0] // count
    up_rows = rank // count
    width = wide * steps
    down_rows = width // count

    @pl.when(g == 0)
    def _():
        hidden_t[...] = hidden[...].T
        freq[...] = jnp.zeros_like(freq)

    inner = cot[...].astype(f32) * cross[...].astype(f32)
    bias[...] = jnp.sum(inner, axis=0, keepdims=True)
    u = jnp.dot(hidden_t[...], inner.astype(bf16), preferred_element_type=f32)
    for k in range(per):
        up[k * rank : (k + 1) * rank, :] = u[:, k * 128 : (k + 1) * 128]
    d = dot_tn(cross[...], back_low[...])
    for k in range(rank // 128):
        down[pl.ds(pl.multiple_of(k * width + g * wide, 128), wide), :] = d[:, k * 128 : (k + 1) * 128]
    row_iota = lax.broadcasted_iota(i32, (frequent, 512), 0)
    for k in range(per):
        hot = one_hot(row_iota == place[0, k : k + 1, :])
        s = jnp.dot(hot, hi_lo(values[k]), preferred_element_type=f32)
        freq[...] += s[:, :128] + s[:, 128:]

    cols = per * steps

    def put_up(i, _):
        for k in range(per):
            both[pl.ds(i * block + g * per + k, up_rows, stride=cols), :] = up[
                pl.ds(k * rank + i * up_rows, up_rows), :
            ]
        return 0

    lax.fori_loop(0, count, put_up, 0)

    @pl.when(g == steps - 1)
    def _():
        def put_down(i, _):
            for k in range(rank // 128):
                both[pl.ds(i * block + up_rows * cols + k, down_rows, stride=rank // 128), :] = down[
                    pl.ds(k * width + i * down_rows, down_rows), :
                ]
            both[pl.ds(i * block + block - 8, 8), :] = freq[pl.ds(pl.multiple_of(i * 8, 8), 8), :]
            return 0

        lax.fori_loop(0, count, put_down, 0)


def segment_kernel(arrived, out, acc):
    g = pl.program_id(0)
    owned = out.shape[0]
    slots = arrived.shape[1] - 8

    @pl.when(g == 0)
    def _():
        acc[...] = jnp.zeros_like(acc)

    hots, parts = [], []
    for b in range(arrived.shape[0]):
        r0 = arrived[b, slots : slots + 1, :]
        r1 = arrived[b, slots + 1 : slots + 2, : slots - 128]
        hots.append(jnp.concatenate([r0, r1], axis=1).astype(i32))
        parts.append(hi_lo(arrived[b, :slots, :]))
    rows = jnp.concatenate(hots, axis=1)
    right = jnp.concatenate(parts, axis=0)
    step = 512
    for m in range(0, owned, step):
        hot = one_hot(lax.broadcasted_iota(i32, (step, rows.shape[1]), 0) + m == rows)
        acc[m : m + step, :] += jnp.dot(hot, right, preferred_element_type=f32)

    @pl.when(g == pl.num_programs(0) - 1)
    def _():
        out[...] = acc[:, :128] + acc[:, 128:]


PORT = ((0, 96, 48, "xzy"), (96, 96, 48, "zxy"), (192, 40, 24, "yxz"))


def params(**kw):
    return pltpu.CompilerParams(vmem_limit_bytes=VLIM, **kw)


def reduce_kernel(both, bias, seg, mine, freq_out, seg_out, *scratch):
    n_port = len(PORT)
    it = iter(scratch)
    work = [next(it) for _ in PORT]
    pair = [next(it) for _ in PORT]
    land = [[[next(it) for _ in range(4)] for _ in range(3)] for _ in PORT]
    swork = next(it)
    sland = [next(it) for _ in range(4)]
    sgath = next(it)
    gath = next(it)
    send_sems, recv_sems, local_sems = next(it), next(it), next(it)

    dp, y = lax.axis_index("dp"), lax.axis_index("rep")
    me = {"x": dp // 8, "z": (dp // 2) % 4, "y": y}
    core = dp % 2

    def device(axis, to):
        at = dict(me, **{axis: to})
        return ((at["x"] * 4 + at["z"]) * 2 + core, at["y"])

    partner = (dp + 1 - 2 * core, y)
    up = {a: (me[a] + 1) % 4 for a in "xzy"}
    down = {a: (me[a] + 3) % 4 for a in "xzy"}
    far = {a: (me[a] + 2) % 4 for a in "xzy"}
    peers = [partner] + [device(a, s[a]) for a in "xzy" for s in (up, down)]
    barrier = pltpu.get_barrier_semaphore()
    for peer in peers:
        pl.semaphore_signal(barrier, inc=1, device_id=peer, device_id_type=pl.DeviceIdType.MESH)
    pl.semaphore_wait(barrier, len(peers))

    sent, used = [], [0]

    def send(src, dst, to):
        k = used[0]
        used[0] += 1
        copy = pltpu.make_async_remote_copy(
            src_ref=src, dst_ref=dst, send_sem=send_sems.at[k], recv_sem=recv_sems.at[k],
            device_id=to, device_id_type=pl.DeviceIdType.MESH,
        )
        copy.start()
        sent.append(copy)
        return copy

    def place(done, axis, t, rem=None):
        rem = iter(rem) if rem is not None else None
        out = []
        for a in "xzy":
            if a in done:
                out.append(me[a])
            elif a == axis:
                out.append(t)
            else:
                out.append(slice(None) if rem is None else next(rem))
        return tuple(out)

    def each(n_rem, fn):
        if n_rem == 0:
            fn(())
        elif n_rem == 1:
            lax.fori_loop(0, 4, lambda i, _: (fn((i,)), 0)[1], 0)
        else:
            lax.fori_loop(0, 16, lambda i, _: (fn((i // 4, i % 4)), 0)[1], 0)

    class Reduce:
        def __init__(self, ref, done, axis, rows, half, lands, free=2):
            self.ref, self.done, self.axis, self.rows, self.half, self.lands = ref, done, axis, rows, half, lands
            self.n = free

        def at(self, t, lo, hi):
            if self.done is None:
                return self.ref.at[t, pl.ds(lo, hi - lo), :]
            return self.ref.at[place(self.done, self.axis, t) + (pl.ds(lo, hi - lo), slice(None))]

        def add(self, t, lo, hi, *refs):
            def one(rem):
                if self.done is None:
                    step = 128
                    for r in range(lo, hi, step):
                        v = self.ref[t, r : r + step, :]
                        for ref in refs:
                            v = v + ref[r - lo : r - lo + step, :]
                        self.ref[t, r : r + step, :] = v
                    return
                where = place(self.done, self.axis, t, rem)
                v = self.ref[where + (slice(lo, hi), slice(None))]
                for ref in refs:
                    v = v + ref[rem + (slice(None), slice(None))]
                self.ref[where + (slice(lo, hi), slice(None))] = v

            each(self.n, one)

        def start(self):
            a = self.axis
            self.c0 = send(self.at(far[a], 0, self.half), self.lands[0], device(a, up[a]))
            self.c1 = send(self.at(far[a], self.half, self.rows), self.lands[1], device(a, down[a]))

        def middle(self):
            a = self.axis
            self.c0.wait_recv()
            self.add(up[a], 0, self.half, self.lands[0])
            self.c2 = send(self.at(up[a], 0, self.rows), self.lands[2], device(a, up[a]))
            self.c1.wait_recv()
            self.add(down[a], self.half, self.rows, self.lands[1])
            self.c3 = send(self.at(down[a], 0, self.rows), self.lands[3], device(a, down[a]))

        def finish(self):
            self.c2.wait_recv()
            self.c3.wait_recv()
            self.add(me[self.axis], 0, self.rows, self.lands[2], self.lands[3])

    class Gather:
        def __init__(self, axis, at):
            self.axis, self.at = axis, at

        def start(self):
            a = self.axis
            src = self.at(me[a], None)
            self.c0 = send(src, src, device(a, up[a]))
            self.c1 = send(src, src, device(a, down[a]))

        def middle(self):
            a = self.axis
            self.c0.wait_recv()
            src = self.at(down[a], 0)
            self.c2 = send(src, src, device(a, up[a]))
            self.c1.wait_recv()
            src = self.at(up[a], 1)
            self.c3 = None
            if src is not None:
                self.c3 = send(src, src, device(a, down[a]))

        def finish(self):
            self.c2.wait_recv()
            if self.c3 is not None:
                self.c3.wait_recv()

    firsts, locals_ = [], []
    for p, (first, rows, half, order) in enumerate(PORT):
        whole = rows if p < n_port - 1 else rows - 8
        got = [
            send(
                both.at[:, :, 1 - core, :, pl.ds(first, whole), :],
                pair[p].at[:, :, :, pl.ds(0, whole), :],
                partner,
            )
        ]
        loc = [pltpu.make_async_copy(
            both.at[:, :, core, :, pl.ds(first, whole), :], work[p].at[:, :, :, pl.ds(0, whole), :], local_sems.at[p])]
        if p == n_port - 1:
            got.append(send(bias.at[:, :, 1 - core], pair[p].at[:, :, :, pl.ds(whole, 8), :], partner))
            loc.append(pltpu.make_async_copy(
                bias.at[:, :, core], work[p].at[:, :, :, pl.ds(whole, 8), :], local_sems.at[n_port]))
        for c in loc:
            c.start()
        firsts.append(got)
        locals_.append(loc)
    load = pltpu.make_async_copy(seg, swork, local_sems.at[n_port + 1])
    load.start()
    load.wait()
    owned = swork.shape[1]
    s_red = Reduce(swork, None, "y", owned, owned // 2, sland, 0)
    s_red.start()

    reds = []
    for p, (first, rows, half, order) in enumerate(PORT):
        phases = []
        for k in range(3):
            phases.append(Reduce(work[p], order[:k], order[k], rows, half, land[p][k], 2 - k))
        reds.append(phases)

    def begin(p):
        for c in locals_[p]:
            c.wait()
        for c in firsts[p]:
            c.wait_recv()

        def one(i, _):
            w = (i // 16, (i // 4) % 4, i % 4)
            work[p][w] = work[p][w] + pair[p][w]
            return 0

        lax.fori_loop(0, 64, one, 0)
        reds[p][0].start()

    def s_half(t, h):
        if h is None:
            return sgath.at[t]
        return sgath.at[t, pl.ds(h * (owned // 2), owned // 2), :]

    s_gat = Gather("y", s_half)

    def y_at(t, h):
        return None if h == 1 else gath.at[me["x"], me["z"], core, t]

    def z_at(t, h):
        return gath.at[me["x"], t, core] if h is None else gath.at[me["x"], t, core, pl.ds(2 * h, 2)]

    def x_at(t, h):
        return gath.at[t, :, core] if h is None else gath.at[t, pl.ds(2 * h, 2), core]

    g_y, g_z, g_x = Gather("y", y_at), Gather("z", z_at), Gather("x", x_at)
    here = (me["x"], me["z"], me["y"])

    begin(2)
    begin(0)
    begin(1)
    s_red.middle()
    reds[2][0].middle()
    reds[0][0].middle()
    reds[1][0].middle()
    reds[2][0].finish()
    reds[2][1].start()
    s_red.finish()
    sgath[me["y"]] = swork[me["y"]]
    s_gat.start()
    reds[2][1].middle()
    reds[2][1].finish()
    reds[2][2].start()
    reds[2][2].middle()
    reds[2][2].finish()
    last = n_port - 1
    rows_last = PORT[last][1]
    gath[me["x"], me["z"], core, me["y"]] = work[last][here + (slice(rows_last - 16, rows_last - 8), slice(None))]
    g_y.start()
    s_gat.middle()
    g_y.middle()
    reds[0][0].finish()
    reds[0][1].start()
    reds[1][0].finish()
    reds[1][1].start()
    g_y.finish()
    g_z.start()
    s_gat.finish()
    reds[0][1].middle()
    reds[1][1].middle()
    g_z.middle()
    reds[0][1].finish()
    reds[0][2].start()
    reds[1][1].finish()
    reds[1][2].start()
    g_z.finish()
    g_x.start()
    reds[0][2].middle()
    reds[1][2].middle()
    g_x.middle()
    reds[0][2].finish()
    reds[1][2].finish()
    g_x.finish()
    g_c = send(gath.at[:, :, core], gath.at[:, :, core], partner)
    for p, (first, rows, half, order) in enumerate(PORT):
        mine[first : first + rows, :] = work[p][here]
    seg_out[...] = sgath[...]
    g_c.wait_recv()
    freq_out[...] = gath[...]
    for c in sent:
        c.wait_send()


def reduce_scratch(owned):
    v = lambda *s: pltpu.VMEM(s, f32)
    out = [v(4, 4, 4, r, 128) for _, r, _, _ in PORT] * 2
    for _, r, h, _ in PORT:
        for k in range(3):
            lead = (4,) * (2 - k)
            out += [v(*lead, h, 128), v(*lead, r - h, 128), v(*lead, r, 128), v(*lead, r, 128)]
    out += [v(4, owned // 4, 128), v(owned // 8, 128), v(owned // 8, 128), v(owned // 4, 128), v(owned // 4, 128), v(4, owned // 4, 128)]
    out += [v(4, 4, 2, 4, 8, 128)]
    out += [pltpu.SemaphoreType.DMA((80,)), pltpu.SemaphoreType.DMA((80,)), pltpu.SemaphoreType.DMA((8,))]
    return out


def reduce_all(both, bias, seg):
    owned = seg.shape[0]
    per = both.shape[0] // 128
    vmem = pl.BlockSpec(memory_space=pltpu.VMEM)
    anyw = pl.BlockSpec(memory_space=pl.ANY)
    mine, freq, seg = pl.pallas_call(
        reduce_kernel,
        out_shape=(
            jax.ShapeDtypeStruct((per + 8, 128), f32),
            jax.ShapeDtypeStruct((4, 4, 2, 4, 8, 128), f32),
            jax.ShapeDtypeStruct((4, owned // 4, 128), f32),
        ),
        in_specs=[anyw, anyw, anyw],
        out_specs=(vmem, vmem, vmem),
        scratch_shapes=reduce_scratch(owned),
        compiler_params=params(collective_id=0, has_side_effects=True),
        name="reduce_kernel",
    )(both.reshape(4, 4, 2, 4, per, 128), bias.reshape(4, 4, 2, 4, 8, 128), seg.reshape(4, owned // 4, 128))
    return mine, freq.reshape(1024, 128), seg.reshape(owned, 128)


def body(cross_in, cotangent, weight_down, weight_up, cross_bias, row_place, frequent_table, frequent_accum, shard_table, shard_accum):
    samples, width = cross_in.shape
    rank = weight_down.shape[1]
    tables = row_place.shape[1]
    emb = frequent_table.shape[1]
    f_count = frequent_table.shape[0]
    owned = shard_table.shape[0]
    shards = lax.axis_size("dp")
    count = shards * lax.axis_size("rep")
    capacity = samples * tables // (2 * shards)
    blocks = width // emb
    per = 3
    steps = blocks // per
    wide = per * emb
    vmem = pl.BlockSpec(memory_space=pltpu.VMEM)

    place_t = row_place.T
    anyw = pl.BlockSpec(memory_space=pl.ANY)
    hidden, back_low, values, bucket = pl.pallas_call(
        functools.partial(front_kernel, f_count, owned),
        out_shape=(
            jax.ShapeDtypeStruct((samples, rank), bf16),
            jax.ShapeDtypeStruct((samples, rank), bf16),
            jax.ShapeDtypeStruct((blocks * samples, emb), f32),
            jax.ShapeDtypeStruct((shards, capacity + 8, emb), f32),
        ),
        in_specs=[vmem, vmem, anyw, anyw, anyw, anyw],
        out_specs=(vmem, vmem, anyw, anyw),
        scratch_shapes=[
            pltpu.VMEM((samples, width), bf16),
            pltpu.VMEM((samples, width), bf16),
            pltpu.VMEM((width, rank), bf16),
            pltpu.VMEM((rank, width), bf16),
            pltpu.VMEM((blocks * samples, emb), f32),
            pltpu.VMEM((shards, capacity + 8, emb), f32),
            pltpu.VMEM((tables * shards, samples), bf16),
            pltpu.VMEM((tables * shards, samples), f32),
            pltpu.VMEM((shards, 256), i32),
            pltpu.VMEM((shards, 128), f32),
            pltpu.VMEM((shards, 128), f32),
            pltpu.SMEM((shards, 256), i32),
            pltpu.VMEM((samples, rank), f32),
            pltpu.VMEM((samples, rank), f32),
            pltpu.SemaphoreType.DMA((steps, 4)),
            pltpu.SemaphoreType.DMA((steps,)),
            pltpu.SemaphoreType.DMA((shards,)),
            pltpu.SemaphoreType.DMA,
        ],
        compiler_params=params(),
        name="front_kernel",
    )(place_t, cross_bias.reshape(1, -1), cross_in, cotangent, weight_down, weight_up)

    values = values.reshape(blocks, samples, emb)
    arrived = lax.all_to_all(bucket, "dp", split_axis=0, concat_axis=0, tiled=True)

    place3 = jnp.concatenate([jnp.full((1, samples), -1, i32), place_t], axis=0).reshape(steps, per, samples)
    block = rank * width // count // 128 * 2 + f_count // count
    both, bias = pl.pallas_call(
        functools.partial(weights_kernel, count, steps),
        grid=(steps,),
        out_shape=(
            jax.ShapeDtypeStruct((count * block, 128), f32),
            jax.ShapeDtypeStruct((1, width), f32),
        ),
        in_specs=[
            pl.BlockSpec((samples, rank), lambda g: (0, 0)),
            pl.BlockSpec((samples, rank), lambda g: (0, 0)),
            pl.BlockSpec((samples, wide), lambda g: (0, g)),
            pl.BlockSpec((samples, wide), lambda g: (0, g)),
            pl.BlockSpec((per, samples, emb), lambda g: (g, 0, 0)),
            pl.BlockSpec((1, per, samples), lambda g: (g, 0, 0)),
        ],
        out_specs=(
            pl.BlockSpec((count * block, 128), lambda g: (0, 0)),
            pl.BlockSpec((1, wide), lambda g: (0, g)),
        ),
        scratch_shapes=[
            pltpu.VMEM((f_count, emb), f32),
            pltpu.VMEM((rank, samples), bf16),
            pltpu.VMEM((rank // 128 * width, 128), f32),
            pltpu.VMEM((per * rank, 128), f32),
        ],
        compiler_params=params(),
        name="weights_kernel",
    )(hidden, back_low, cross_in, cotangent, values, place3)
    bias = jnp.pad(bias.reshape(count, 1, width // count), ((0, 0), (0, 7), (0, 128 - width // count)))

    shard_grad = pl.pallas_call(
        segment_kernel,
        grid=(shards // 4,),
        out_shape=jax.ShapeDtypeStruct((owned, emb), f32),
        in_specs=[pl.BlockSpec((4, capacity + 8, emb), lambda g: (g, 0, 0))],
        out_specs=pl.BlockSpec((owned, emb), lambda g: (0, 0)),
        scratch_shapes=[pltpu.VMEM((owned, 256), f32)],
        compiler_params=params(),
        name="segment_kernel",
    )(arrived)
    mine, freq, shard_grad = reduce_all(both, bias, shard_grad)
    n = rank * width // count // 128
    grad_up = mine[:n].reshape(rank // count, width)
    grad_down = mine[n : 2 * n].reshape(width // count, rank)
    grad_bias = mine[block, : width // count]
    new_shard, new_shard_accum = row_adagrad(shard_table, shard_accum, shard_grad)
    new_frequent, new_frequent_accum = row_adagrad(frequent_table, frequent_accum, freq)
    return (new_frequent, new_frequent_accum, new_shard, new_shard_accum, grad_up, grad_down, grad_bias)


def solution(mesh):
    both = ("dp", "rep")
    in_specs = (P(both, None), P(both, None), P(), P(), P(), P(both, None), P(), P(), P("dp", None), P("dp"))
    out_specs = (P(), P(), P("dp", None), P("dp"), P(both, None), P(both, None), P(both))
    return jax.shard_map(body, mesh=mesh, in_specs=in_specs, out_specs=out_specs, check_vma=False)
```

```python
import functools
import jax
import jax.numpy as jnp
from jax import lax
from jax.experimental import pallas as pl
from jax.experimental.pallas import tpu as pltpu
from jax.sharding import PartitionSpec as P

learn_rate = 0.05
eps_ada = 1e-08
f32, bf16, i32 = jnp.float32, jnp.bfloat16, jnp.int32
VLIM = 60 * 1024 * 1024


def row_adagrad(table, accum, grad):
    accum_new = accum + jnp.mean(grad * grad, axis=1)
    return (table - learn_rate * grad / (jnp.sqrt(accum_new)[:, None] + eps_ada), accum_new)


def dot_nt(a, b):
    return lax.dot_general(a, b, (((1,), (1,)), ((), ())), preferred_element_type=f32)


def dot_tn(a, b):
    return lax.dot_general(a, b, (((0,), (0,)), ((), ())), preferred_element_type=f32)


def hi_lo(v):
    hi = v.astype(bf16)
    lo = (v - hi.astype(f32)).astype(bf16)
    return jnp.concatenate([hi, lo], axis=1)


def one_hot(flags):
    return jnp.where(flags, 1.0, 0.0).astype(bf16)


def index_work(frequent, owned, place, idx, row_a, row_b, hot, cum):
    tables, samples = place.shape
    owners, slots = idx.shape
    at = lax.broadcasted_iota(i32, (1, samples), 1)
    owner_iota = lax.broadcasted_iota(i32, (owners, samples), 0)
    tri = one_hot(
        lax.broadcasted_iota(i32, (samples, samples), 0)
        < lax.broadcasted_iota(i32, (samples, samples), 1)
    )
    shift = owned.bit_length() - 1
    for t in range(tables):
        owner = lax.shift_right_arithmetic(place[t : t + 1, :] - frequent, shift)
        hot[t * owners : (t + 1) * owners, :] = one_hot(owner_iota == owner)
    cum[...] = jnp.dot(hot[...], tri, preferred_element_type=f32)
    base = jnp.zeros((owners, 1), f32)
    total = jnp.zeros((4 * owners, slots), f32)
    slot_iota = lax.broadcasted_iota(i32, (slots, samples), 0)
    at_hi = lax.shift_right_logical(at, 7).astype(f32)
    at_lo = (at & 127).astype(f32)
    blocks = samples // 128
    for t in range(tables):
        mine = hot[t * owners : (t + 1) * owners, :].astype(f32)
        before = cum[t * owners : (t + 1) * owners, :] + base
        rank = jnp.sum(mine * before, axis=0, keepdims=True).astype(i32)
        base = before[:, samples - 1 :] + mine[:, samples - 1 :]
        local = (place[t : t + 1, :] - frequent) & (owned - 1)
        parts = [
            mine * (at_hi + float((t + 1) * blocks)),
            mine * at_lo,
            mine * (lax.shift_right_logical(local, 7) + 1).astype(f32),
            mine * (local & 127).astype(f32),
        ]
        left = jnp.concatenate(parts, axis=0).astype(bf16)
        total = total + dot_nt(left, one_hot(slot_iota == rank))
    idx[...] = (total[:owners] * 128.0 + total[owners : 2 * owners]).astype(i32)
    row = (total[2 * owners : 3 * owners] - 1.0) * 128.0 + total[3 * owners :]
    row_a[...] = row[:, :128]
    row_b[...] = row[:, 128:]


def front_kernel(
    frequent, owned, place, bias, cross_hbm, cot_hbm, down_hbm, up_hbm,
    hidden, back_low, values_hbm, bucket_hbm,
    cross, cot, down, up, values, bucket, hot, cum, idx_v, row_a, row_b, idx, h_acc, b_acc, in_sems, v_sems, b_sems, i_sem,
):
    samples = hidden.shape[0]
    emb = values.shape[1]
    steps = in_sems.shape[0]
    wide = cross.shape[1] // steps
    per = wide // emb
    owners = bucket.shape[0]
    slots = bucket.shape[1] - 8

    def loads(g):
        cols = pl.ds(pl.multiple_of(g * wide, wide), wide)
        return [
            pltpu.make_async_copy(cross_hbm.at[:, cols], cross.at[:, cols], in_sems.at[g, 0]),
            pltpu.make_async_copy(cot_hbm.at[:, cols], cot.at[:, cols], in_sems.at[g, 1]),
            pltpu.make_async_copy(down_hbm.at[cols, :], down.at[cols, :], in_sems.at[g, 2]),
            pltpu.make_async_copy(up_hbm.at[:, cols], up.at[:, cols], in_sems.at[g, 3]),
        ]

    for g in range(steps):
        for c in loads(g):
            c.start()
    index_work(frequent, owned, place, idx_v, row_a, row_b, hot, cum)
    to_scalar = pltpu.make_async_copy(idx_v, idx, i_sem)
    to_scalar.start()
    h_acc[...] = jnp.zeros_like(h_acc)
    b_acc[...] = jnp.zeros_like(b_acc)

    def low(g, _):
        for c in loads(g):
            c.wait()
        cols = pl.ds(pl.multiple_of(g * wide, wide), wide)
        x = cross[:, cols]
        inner = (cot[:, cols].astype(f32) * x.astype(f32)).astype(bf16)
        h_acc[...] += jnp.dot(x, down[cols, :], preferred_element_type=f32)
        b_acc[...] += dot_nt(inner, up[:, cols])
        return 0

    lax.fori_loop(0, steps, low, 0)
    hidden[...] = h_acc[...].astype(bf16)
    back_low[...] = b_acc[...].astype(bf16)

    def store(g):
        part = pl.ds(pl.multiple_of(g * per * samples, 128), per * samples)
        return pltpu.make_async_copy(values.at[part], values_hbm.at[part], v_sems.at[g])

    def high(g, _):
        cols = pl.ds(pl.multiple_of(g * wide, wide), wide)
        scaled = jnp.dot(hidden[...], up[:, cols], preferred_element_type=f32) + bias[:, cols]
        v = cot[:, cols].astype(f32) * (scaled + 1.0) + dot_nt(back_low[...], down[cols, :])
        for k in range(per):
            values[pl.ds(pl.multiple_of((g * per + k) * samples, 128), samples), :] = v[:, k * emb : (k + 1) * emb]
        store(g).start()
        return 0

    lax.fori_loop(0, steps, high, 0)
    to_scalar.wait()

    def ship(o):
        return pltpu.make_async_copy(bucket.at[o], bucket_hbm.at[o], b_sems.at[o])

    def pick(o, _):
        for k in range(slots):
            src = idx[o, k]
            bucket[o, k : k + 1, :] = values[pl.ds(src, 1), :]
        bucket[o, slots : slots + 8, :] = jnp.zeros((8, emb), f32)
        bucket[o, slots : slots + 1, :] = row_a[pl.ds(o, 1), :]
        bucket[o, slots + 1 : slots + 2, :] = row_b[pl.ds(o, 1), :]
        ship(o).start()
        return 0

    lax.fori_loop(0, owners, pick, 0)
    lax.fori_loop(0, steps, lambda g, _: (store(g).wait(), 0)[1], 0)
    lax.fori_loop(0, owners, lambda o, _: (ship(o).wait(), 0)[1], 0)


PORT = ((0, 96, 48, "xzy"), (96, 96, 48, "zxy"), (192, 40, 24, "yxz"))


def mesh_place():
    dp, y = lax.axis_index("dp"), lax.axis_index("rep")
    core = dp % 2
    return {"x": dp // 8, "z": (dp // 2) % 4, "y": y}, core, (dp + 1 - 2 * core, y)


def sender(send_sems, recv_sems, sent):
    used = [0]

    def send(src, dst, to):
        k = used[0]
        used[0] += 1
        copy = pltpu.make_async_remote_copy(
            src_ref=src, dst_ref=dst, send_sem=send_sems.at[k], recv_sem=recv_sems.at[k],
            device_id=to, device_id_type=pl.DeviceIdType.MESH,
        )
        copy.start()
        sent.append(copy)
        return copy

    return send


def weights_kernel(steps, hidden, back_low, cross, cot, values_hbm, place, *rest):
    outs, rest = rest[: len(PORT)], rest[len(PORT) :]
    pair, rest = rest[: len(PORT)], rest[len(PORT) :]
    both, freq, hidden_t, down, up, bias, values, send_sems, recv_sems, local_sems = rest
    g = pl.program_id(0)
    rank = hidden.shape[1]
    wide = cross.shape[1]
    per = wide // 128
    frequent = freq.shape[0]
    samples = hidden.shape[0]
    count = frequent // 8
    width = wide * steps
    cols = per * steps
    up_rows = rank // count
    down_rows = width // count
    base = up_rows * cols
    freq_at = base + down_rows * rank // 128
    _, core, partner = mesh_place()
    load = pltpu.make_async_copy(values_hbm, values, local_sems.at[0])

    @pl.when(g == 0)
    def _():
        barrier = pltpu.get_barrier_semaphore()
        pl.semaphore_signal(barrier, inc=1, device_id=partner, device_id_type=pl.DeviceIdType.MESH)
        pl.semaphore_wait(barrier, 1)
        load.start()
        hidden_t[...] = hidden[...].T
        freq[...] = jnp.zeros_like(freq)

    inner = cot[...].astype(f32) * cross[...].astype(f32)
    bias[:, pl.ds(pl.multiple_of(g * wide, wide), wide)] = jnp.sum(inner, axis=0, keepdims=True)
    u = jnp.dot(hidden_t[...], inner.astype(bf16), preferred_element_type=f32)
    for k in range(per):
        up[k * rank : (k + 1) * rank, :] = u[:, k * 128 : (k + 1) * 128]
    d = dot_tn(cross[...], back_low[...])
    for k in range(rank // 128):
        down[pl.ds(pl.multiple_of(k * width + g * wide, 128), wide), :] = d[:, k * 128 : (k + 1) * 128]

    def put_up(n, _):
        for c in range(2):
            for y in range(4):
                i = n * 8 + c * 4 + y
                for k in range(per):
                    both[n, c, y, pl.ds(g * per + k, up_rows, stride=cols), :] = up[
                        pl.ds(k * rank + i * up_rows, up_rows), :
                    ]
        return 0

    lax.fori_loop(0, count // 8, put_up, 0)

    @pl.when(g == steps - 1)
    def _():
        sent = []
        send = sender(send_sems, recv_sems, sent)

        def part(p, c):
            first, rows = PORT[p][0], PORT[p][1]
            return both.at[:, c, :, pl.ds(first, rows), :]

        got = [send(part(0, 1 - core), pair[0], partner)]

        def put_down(n, _):
            for c in range(2):
                for y in range(4):
                    i = n * 8 + c * 4 + y
                    for k in range(rank // 128):
                        both[n, c, y, pl.ds(base + k, down_rows, stride=rank // 128), :] = down[
                            pl.ds(k * width + i * down_rows, down_rows), :
                        ]
                    both[n, c, y, freq_at + 8 : freq_at + 16, :] = jnp.zeros((8, 128), f32)
            return 0

        lax.fori_loop(0, count // 8, put_down, 0)
        got.append(send(part(1, 1 - core), pair[1], partner))
        for i in range(count):
            both[i // 8, (i // 4) % 2, i % 4, freq_at + 8 : freq_at + 9, 0:down_rows] = bias[
                :, i * down_rows : (i + 1) * down_rows
            ]
        load.wait()
        row_iota = lax.broadcasted_iota(i32, (frequent, samples), 0)

        def tables(t, _):
            hots, parts = [], []
            for k in range(2):
                hots.append(one_hot(row_iota == place[2 * t + k]))
                parts.append(hi_lo(values[pl.ds(pl.multiple_of((2 * t + k + 1) * samples, 128), samples), :]))
            s = jnp.dot(jnp.concatenate(hots, axis=1), jnp.concatenate(parts, axis=0), preferred_element_type=f32)
            freq[...] += s[:, :128] + s[:, 128:]
            return 0

        lax.fori_loop(0, place.shape[0] // 2, tables, 0)

        def put_freq(n, _):
            for c in range(2):
                for y in range(4):
                    both[n, c, y, freq_at : freq_at + 8, :] = freq[
                        pl.ds(pl.multiple_of((n * 8 + c * 4 + y) * 8, 8), 8), :
                    ]
            return 0

        lax.fori_loop(0, count // 8, put_freq, 0)
        got.append(send(part(2, 1 - core), pair[2], partner))
        stores = []
        for p, (first, rows, half, order) in enumerate(PORT):
            got[p].wait_recv()

            def add(n, _):
                for y in range(4):
                    both[n, core, y, first : first + rows, :] = (
                        both[n, core, y, first : first + rows, :] + pair[p][n, y]
                    )
                return 0

            lax.fori_loop(0, count // 8, add, 0)
            stores.append(pltpu.make_async_copy(part(p, core), outs[p], local_sems.at[1 + p]))
            stores[-1].start()
        for c in stores:
            c.wait()
        for c in sent:
            c.wait_send()


def params(**kw):
    return pltpu.CompilerParams(vmem_limit_bytes=VLIM, **kw)


def reduce_kernel(*refs):
    n_port = len(PORT)
    it = iter(refs)
    loads = [next(it) for _ in PORT]
    arrived, mine, freq_out, seg_out = next(it), next(it), next(it), next(it)
    work = [next(it) for _ in PORT]
    land = [[[next(it) for _ in range(4)] for _ in range(3)] for _ in PORT]
    swork = next(it)
    sland = [next(it) for _ in range(4)]
    sgath = next(it)
    gath = next(it)
    ids, right, acc = next(it), next(it), next(it)
    send_sems, recv_sems, local_sems = next(it), next(it), next(it)
    me, core, partner = mesh_place()

    def device(axis, to):
        at = dict(me, **{axis: to})
        return ((at["x"] * 4 + at["z"]) * 2 + core, at["y"])

    up = {a: (me[a] + 1) % 4 for a in "xzy"}
    down = {a: (me[a] + 3) % 4 for a in "xzy"}
    far = {a: (me[a] + 2) % 4 for a in "xzy"}
    peers = [partner] + [device(a, s[a]) for a in "xzy" for s in (up, down)]
    barrier = pltpu.get_barrier_semaphore()
    for peer in peers:
        pl.semaphore_signal(barrier, inc=1, device_id=peer, device_id_type=pl.DeviceIdType.MESH)
    pl.semaphore_wait(barrier, len(peers))

    sent = []
    send = sender(send_sems, recv_sems, sent)

    def place(done, axis, t, rem=None):
        rem = iter(rem) if rem is not None else None
        out = []
        for a in "xzy":
            if a in done:
                out.append(me[a])
            elif a == axis:
                out.append(t)
            else:
                out.append(slice(None) if rem is None else next(rem))
        return tuple(out)

    def each(n_rem, fn):
        if n_rem == 0:
            fn(())
        elif n_rem == 1:
            lax.fori_loop(0, 4, lambda i, _: (fn((i,)), 0)[1], 0)
        else:
            lax.fori_loop(0, 16, lambda i, _: (fn((i // 4, i % 4)), 0)[1], 0)

    class Reduce:
        def __init__(self, ref, done, axis, rows, half, lands, free=2):
            self.ref, self.done, self.axis, self.rows, self.half, self.lands = ref, done, axis, rows, half, lands
            self.n = free

        def at(self, t, lo, hi):
            if self.done is None:
                return self.ref.at[t, pl.ds(lo, hi - lo), :]
            return self.ref.at[place(self.done, self.axis, t) + (pl.ds(lo, hi - lo), slice(None))]

        def add(self, t, lo, hi, *refs):
            def one(rem):
                if self.done is None:
                    step = 128
                    for r in range(lo, hi, step):
                        v = self.ref[t, r : r + step, :]
                        for ref in refs:
                            v = v + ref[r - lo : r - lo + step, :]
                        self.ref[t, r : r + step, :] = v
                    return
                where = place(self.done, self.axis, t, rem)
                v = self.ref[where + (slice(lo, hi), slice(None))]
                for ref in refs:
                    v = v + ref[rem + (slice(None), slice(None))]
                self.ref[where + (slice(lo, hi), slice(None))] = v

            each(self.n, one)

        def start(self):
            a = self.axis
            self.c0 = send(self.at(far[a], 0, self.half), self.lands[0], device(a, up[a]))
            self.c1 = send(self.at(far[a], self.half, self.rows), self.lands[1], device(a, down[a]))

        def middle(self):
            a = self.axis
            self.c0.wait_recv()
            self.add(up[a], 0, self.half, self.lands[0])
            self.c2 = send(self.at(up[a], 0, self.rows), self.lands[2], device(a, up[a]))
            self.c1.wait_recv()
            self.add(down[a], self.half, self.rows, self.lands[1])
            self.c3 = send(self.at(down[a], 0, self.rows), self.lands[3], device(a, down[a]))

        def finish(self):
            self.c2.wait_recv()
            self.c3.wait_recv()
            self.add(me[self.axis], 0, self.rows, self.lands[2], self.lands[3])

    class Gather:
        def __init__(self, axis, at):
            self.axis, self.at = axis, at

        def start(self):
            a = self.axis
            src = self.at(me[a], None)
            self.c0 = send(src, src, device(a, up[a]))
            self.c1 = send(src, src, device(a, down[a]))

        def middle(self):
            a = self.axis
            self.c0.wait_recv()
            src = self.at(down[a], 0)
            self.c2 = send(src, src, device(a, up[a]))
            self.c1.wait_recv()
            src = self.at(up[a], 1)
            self.c3 = None
            if src is not None:
                self.c3 = send(src, src, device(a, down[a]))

        def finish(self):
            self.c2.wait_recv()
            if self.c3 is not None:
                self.c3.wait_recv()

    copies = [pltpu.make_async_copy(loads[p], work[p], local_sems.at[p]) for p in range(n_port)]
    for c in copies:
        c.start()
    owned = swork.shape[1]
    slots = arrived.shape[1] - 8
    some = ids.shape[0]
    each_of = arrived.shape[0] // some
    chunk = each_of * slots

    def prepare(g, _):
        rows = []
        for b in range(each_of):
            n = g * each_of + b
            rows.append(arrived[n, slots : slots + 1, :])
            rows.append(arrived[n, slots + 1 : slots + 2, : slots - 128])
            right[pl.ds(pl.multiple_of(n * slots, 16), slots), :] = hi_lo(arrived[n, :slots, :])
        ids[g] = jnp.concatenate(rows, axis=1).astype(i32)
        return 0

    def seg_block(t):
        acc[...] = jnp.zeros_like(acc)
        first = t * owned

        def one(g, _):
            hot = one_hot(lax.broadcasted_iota(i32, (owned, chunk), 0) + first == ids[g])
            acc[...] += jnp.dot(
                hot, right[pl.ds(pl.multiple_of(g * chunk, 16), chunk), :], preferred_element_type=f32
            )
            return 0

        lax.fori_loop(0, some, one, 0)
        swork[t] = acc[:, :128] + acc[:, 128:]

    s_red = Reduce(swork, None, "y", owned, owned // 2, sland, 0)

    reds = []
    for p, (first, rows, half, order) in enumerate(PORT):
        phases = []
        for k in range(3):
            phases.append(Reduce(work[p], order[:k], order[k], rows, half, land[p][k], 2 - k))
        reds.append(phases)

    def s_half(t, h):
        if h is None:
            return sgath.at[t]
        return sgath.at[t, pl.ds(h * (owned // 2), owned // 2), :]

    s_gat = Gather("y", s_half)

    def y_at(t, h):
        return None if h == 1 else gath.at[me["x"], me["z"], core, t]

    def z_at(t, h):
        return gath.at[me["x"], t, core] if h is None else gath.at[me["x"], t, core, pl.ds(2 * h, 2)]

    def x_at(t, h):
        return gath.at[t, :, core] if h is None else gath.at[t, pl.ds(2 * h, 2), core]

    g_y, g_z, g_x = Gather("y", y_at), Gather("z", z_at), Gather("x", x_at)
    here = (me["x"], me["z"], me["y"])

    lax.fori_loop(0, some, prepare, 0)
    for p in (2, 0, 1):
        copies[p].wait()
        reds[p][0].start()
    seg_block(far["y"])
    s_red.start()
    reds[2][0].middle()
    seg_block(up["y"])
    reds[0][0].middle()
    reds[1][0].middle()
    seg_block(down["y"])
    s_red.middle()
    seg_block(me["y"])
    reds[2][0].finish()
    reds[2][1].start()
    s_red.finish()
    sgath[me["y"]] = swork[me["y"]]
    s_gat.start()
    reds[2][1].middle()
    reds[2][1].finish()
    reds[2][2].start()
    reds[2][2].middle()
    reds[2][2].finish()
    last = n_port - 1
    rows_last = PORT[last][1]
    gath[me["x"], me["z"], core, me["y"]] = work[last][here + (slice(rows_last - 16, rows_last - 8), slice(None))]
    g_y.start()
    s_gat.middle()
    g_y.middle()
    reds[0][0].finish()
    reds[0][1].start()
    reds[1][0].finish()
    reds[1][1].start()
    g_y.finish()
    g_z.start()
    s_gat.finish()
    reds[0][1].middle()
    reds[1][1].middle()
    g_z.middle()
    reds[0][1].finish()
    reds[0][2].start()
    reds[1][1].finish()
    reds[1][2].start()
    g_z.finish()
    g_x.start()
    reds[0][2].middle()
    reds[1][2].middle()
    g_x.middle()
    reds[0][2].finish()
    reds[1][2].finish()
    g_x.finish()
    g_c = send(gath.at[:, :, core], gath.at[:, :, core], partner)
    for p, (first, rows, half, order) in enumerate(PORT):
        mine[first : first + rows, :] = work[p][here]
    seg_out[...] = sgath[...]
    g_c.wait_recv()
    freq_out[...] = gath[...]
    for c in sent:
        c.wait_send()


def reduce_scratch(owned, arrived):
    v = lambda *s: pltpu.VMEM(s, f32)
    out = [v(4, 4, 4, r, 128) for _, r, _, _ in PORT]
    for _, r, h, _ in PORT:
        for k in range(3):
            lead = (4,) * (2 - k)
            out += [v(*lead, h, 128), v(*lead, r - h, 128), v(*lead, r, 128), v(*lead, r, 128)]
    out += [v(4, owned // 4, 128), v(owned // 8, 128), v(owned // 8, 128), v(owned // 4, 128), v(owned // 4, 128), v(4, owned // 4, 128)]
    out += [v(4, 4, 2, 4, 8, 128)]
    n = arrived.shape[0] // 4
    flat = arrived.shape[0] * (arrived.shape[1] - 8)
    out += [pltpu.VMEM((n, 1, flat // n), i32), pltpu.VMEM((flat, 256), bf16), v(owned // 4, 256)]
    out += [pltpu.SemaphoreType.DMA((80,)), pltpu.SemaphoreType.DMA((80,)), pltpu.SemaphoreType.DMA((8,))]
    return out


def reduce_all(parts, arrived, owned):
    vmem = pl.BlockSpec(memory_space=pltpu.VMEM)
    anyw = pl.BlockSpec(memory_space=pl.ANY)
    total = PORT[-1][0] + PORT[-1][1]
    mine, freq, seg = pl.pallas_call(
        reduce_kernel,
        out_shape=(
            jax.ShapeDtypeStruct((total, 128), f32),
            jax.ShapeDtypeStruct((4, 4, 2, 4, 8, 128), f32),
            jax.ShapeDtypeStruct((4, owned // 4, 128), f32),
        ),
        in_specs=[anyw] * len(PORT) + [vmem],
        out_specs=(vmem, vmem, vmem),
        scratch_shapes=reduce_scratch(owned, arrived),
        compiler_params=params(collective_id=0, has_side_effects=True),
        name="reduce_kernel",
    )(*[w.reshape(4, 4, 4, w.shape[2], 128) for w in parts], arrived)
    return mine, freq.reshape(1024, 128), seg.reshape(owned, 128)


def body(cross_in, cotangent, weight_down, weight_up, cross_bias, row_place, frequent_table, frequent_accum, shard_table, shard_accum):
    samples, width = cross_in.shape
    rank = weight_down.shape[1]
    tables = row_place.shape[1]
    emb = frequent_table.shape[1]
    f_count = frequent_table.shape[0]
    owned = shard_table.shape[0]
    shards = lax.axis_size("dp")
    count = shards * lax.axis_size("rep")
    capacity = samples * tables // (2 * shards)
    blocks = width // emb
    per = 3
    steps = blocks // per
    wide = per * emb
    vmem = pl.BlockSpec(memory_space=pltpu.VMEM)

    place_t = row_place.T
    anyw = pl.BlockSpec(memory_space=pl.ANY)
    hidden, back_low, values, bucket = pl.pallas_call(
        functools.partial(front_kernel, f_count, owned),
        out_shape=(
            jax.ShapeDtypeStruct((samples, rank), bf16),
            jax.ShapeDtypeStruct((samples, rank), bf16),
            jax.ShapeDtypeStruct((blocks * samples, emb), f32),
            jax.ShapeDtypeStruct((shards, capacity + 8, emb), f32),
        ),
        in_specs=[vmem, vmem, anyw, anyw, anyw, anyw],
        out_specs=(vmem, vmem, anyw, anyw),
        scratch_shapes=[
            pltpu.VMEM((samples, width), bf16),
            pltpu.VMEM((samples, width), bf16),
            pltpu.VMEM((width, rank), bf16),
            pltpu.VMEM((rank, width), bf16),
            pltpu.VMEM((blocks * samples, emb), f32),
            pltpu.VMEM((shards, capacity + 8, emb), f32),
            pltpu.VMEM((tables * shards, samples), bf16),
            pltpu.VMEM((tables * shards, samples), f32),
            pltpu.VMEM((shards, 256), i32),
            pltpu.VMEM((shards, 128), f32),
            pltpu.VMEM((shards, 128), f32),
            pltpu.SMEM((shards, 256), i32),
            pltpu.VMEM((samples, rank), f32),
            pltpu.VMEM((samples, rank), f32),
            pltpu.SemaphoreType.DMA((steps, 4)),
            pltpu.SemaphoreType.DMA((steps,)),
            pltpu.SemaphoreType.DMA((shards,)),
            pltpu.SemaphoreType.DMA,
        ],
        compiler_params=params(),
        name="front_kernel",
    )(place_t, cross_bias.reshape(1, -1), cross_in, cotangent, weight_down, weight_up)

    arrived = lax.all_to_all(bucket, "dp", split_axis=0, concat_axis=0, tiled=True)

    parts = pl.pallas_call(
        functools.partial(weights_kernel, steps),
        grid=(steps,),
        out_shape=tuple(jax.ShapeDtypeStruct((16, 4, r, 128), f32) for _, r, _, _ in PORT),
        in_specs=[
            pl.BlockSpec((samples, rank), lambda g: (0, 0)),
            pl.BlockSpec((samples, rank), lambda g: (0, 0)),
            pl.BlockSpec((samples, wide), lambda g: (0, g)),
            pl.BlockSpec((samples, wide), lambda g: (0, g)),
            anyw,
            pl.BlockSpec((tables, 1, samples), lambda g: (0, 0, 0)),
        ],
        out_specs=(anyw,) * len(PORT),
        scratch_shapes=[pltpu.VMEM((16, 4, r, 128), f32) for _, r, _, _ in PORT]
        + [
            pltpu.VMEM((16, 2, 4, PORT[-1][0] + PORT[-1][1], 128), f32),
            pltpu.VMEM((f_count, emb), f32),
            pltpu.VMEM((rank, samples), bf16),
            pltpu.VMEM((rank // 128 * width, 128), f32),
            pltpu.VMEM((per * rank, 128), f32),
            pltpu.VMEM((1, width), f32),
            pltpu.VMEM((blocks * samples, emb), f32),
            pltpu.SemaphoreType.DMA((len(PORT),)),
            pltpu.SemaphoreType.DMA((len(PORT),)),
            pltpu.SemaphoreType.DMA((1 + len(PORT),)),
        ],
        compiler_params=params(collective_id=1, has_side_effects=True),
        name="weights_kernel",
    )(hidden, back_low, cross_in, cotangent, values, place_t.reshape(tables, 1, samples))

    mine, freq, shard_grad = reduce_all(parts, arrived, owned)
    n = rank * width // count // 128
    grad_up = mine[:n].reshape(rank // count, width)
    grad_down = mine[n : 2 * n].reshape(width // count, rank)
    grad_bias = mine[2 * n + f_count // count, : width // count]
    new_shard, new_shard_accum = row_adagrad(shard_table, shard_accum, shard_grad)
    new_frequent, new_frequent_accum = row_adagrad(frequent_table, frequent_accum, freq)
    return (new_frequent, new_frequent_accum, new_shard, new_shard_accum, grad_up, grad_down, grad_bias)


def solution(mesh):
    both = ("dp", "rep")
    in_specs = (P(both, None), P(both, None), P(), P(), P(), P(both, None), P(), P(), P("dp", None), P("dp"))
    out_specs = (P(), P(), P("dp", None), P("dp"), P(both, None), P(both, None), P(both))
    return jax.shard_map(body, mesh=mesh, in_specs=in_specs, out_specs=out_specs, check_vma=False)
```

```python
import functools
import jax
import jax.numpy as jnp
from jax import lax
from jax.experimental import pallas as pl
from jax.experimental.pallas import tpu as pltpu
from jax.sharding import PartitionSpec as P

learn_rate = 0.05
eps_ada = 1e-08
f32, bf16, i32 = jnp.float32, jnp.bfloat16, jnp.int32
VLIM = 60 * 1024 * 1024


def row_adagrad(table, accum, grad):
    accum_new = accum + jnp.mean(grad * grad, axis=1)
    return (table - learn_rate * grad / (jnp.sqrt(accum_new)[:, None] + eps_ada), accum_new)


def dot_nt(a, b):
    return lax.dot_general(a, b, (((1,), (1,)), ((), ())), preferred_element_type=f32)


def dot_tn(a, b):
    return lax.dot_general(a, b, (((0,), (0,)), ((), ())), preferred_element_type=f32)


def hi_lo(v):
    hi = v.astype(bf16)
    lo = (v - hi.astype(f32)).astype(bf16)
    return jnp.concatenate([hi, lo], axis=1)


def one_hot(flags):
    return jnp.where(flags, 1.0, 0.0).astype(bf16)


def index_work(frequent, owned, place, idx, row_a, row_b, hot, cum):
    tables, samples = place.shape
    owners, slots = idx.shape
    at = lax.broadcasted_iota(i32, (1, samples), 1)
    owner_iota = lax.broadcasted_iota(i32, (owners, samples), 0)
    tri = one_hot(
        lax.broadcasted_iota(i32, (samples, samples), 0)
        < lax.broadcasted_iota(i32, (samples, samples), 1)
    )
    shift = owned.bit_length() - 1
    for t in range(tables):
        owner = lax.shift_right_arithmetic(place[t : t + 1, :] - frequent, shift)
        hot[t * owners : (t + 1) * owners, :] = one_hot(owner_iota == owner)
    cum[...] = jnp.dot(hot[...], tri, preferred_element_type=f32)
    base = jnp.zeros((owners, 1), f32)
    total = jnp.zeros((4 * owners, slots), f32)
    slot_iota = lax.broadcasted_iota(i32, (slots, samples), 0)
    at_hi = lax.shift_right_logical(at, 7).astype(f32)
    at_lo = (at & 127).astype(f32)
    blocks = samples // 128
    for t in range(tables):
        mine = hot[t * owners : (t + 1) * owners, :].astype(f32)
        before = cum[t * owners : (t + 1) * owners, :] + base
        rank = jnp.sum(mine * before, axis=0, keepdims=True).astype(i32)
        base = before[:, samples - 1 :] + mine[:, samples - 1 :]
        local = (place[t : t + 1, :] - frequent) & (owned - 1)
        parts = [
            mine * (at_hi + float((t + 1) * blocks)),
            mine * at_lo,
            mine * (lax.shift_right_logical(local, 7) + 1).astype(f32),
            mine * (local & 127).astype(f32),
        ]
        left = jnp.concatenate(parts, axis=0).astype(bf16)
        total = total + dot_nt(left, one_hot(slot_iota == rank))
    idx[...] = (total[:owners] * 128.0 + total[owners : 2 * owners]).astype(i32)
    row = (total[2 * owners : 3 * owners] - 1.0) * 128.0 + total[3 * owners :]
    row_a[...] = row[:, :128]
    row_b[...] = row[:, 128:]


def front_kernel(
    frequent, owned, place, bias, cross_hbm, cot_hbm, down_hbm, up_hbm,
    hidden, back_low, values_hbm, bucket_hbm,
    cross, cot, down, up, values, bucket, hot, cum, idx_v, row_a, row_b, idx, h_acc, b_acc, in_sems, v_sems, b_sems, i_sem,
):
    samples = hidden.shape[0]
    emb = values.shape[1]
    steps = in_sems.shape[0]
    wide = cross.shape[1] // steps
    per = wide // emb
    owners = bucket.shape[0]
    slots = bucket.shape[1] - 8

    def loads(g):
        cols = pl.ds(pl.multiple_of(g * wide, wide), wide)
        return [
            pltpu.make_async_copy(cross_hbm.at[:, cols], cross.at[:, cols], in_sems.at[g, 0]),
            pltpu.make_async_copy(cot_hbm.at[:, cols], cot.at[:, cols], in_sems.at[g, 1]),
            pltpu.make_async_copy(down_hbm.at[cols, :], down.at[cols, :], in_sems.at[g, 2]),
            pltpu.make_async_copy(up_hbm.at[:, cols], up.at[:, cols], in_sems.at[g, 3]),
        ]

    for g in range(steps):
        for c in loads(g):
            c.start()
    index_work(frequent, owned, place, idx_v, row_a, row_b, hot, cum)
    to_scalar = pltpu.make_async_copy(idx_v, idx, i_sem)
    to_scalar.start()
    h_acc[...] = jnp.zeros_like(h_acc)
    b_acc[...] = jnp.zeros_like(b_acc)

    def low(g, _):
        for c in loads(g):
            c.wait()
        cols = pl.ds(pl.multiple_of(g * wide, wide), wide)
        x = cross[:, cols]
        inner = (cot[:, cols].astype(f32) * x.astype(f32)).astype(bf16)
        h_acc[...] += jnp.dot(x, down[cols, :], preferred_element_type=f32)
        b_acc[...] += dot_nt(inner, up[:, cols])
        return 0

    lax.fori_loop(0, steps, low, 0)
    hidden[...] = h_acc[...].astype(bf16)
    back_low[...] = b_acc[...].astype(bf16)

    def store(g):
        part = pl.ds(pl.multiple_of(g * per * samples, 128), per * samples)
        return pltpu.make_async_copy(values.at[part], values_hbm.at[part], v_sems.at[g])

    def high(g, _):
        cols = pl.ds(pl.multiple_of(g * wide, wide), wide)
        scaled = jnp.dot(hidden[...], up[:, cols], preferred_element_type=f32) + bias[:, cols]
        v = cot[:, cols].astype(f32) * (scaled + 1.0) + dot_nt(back_low[...], down[cols, :])
        for k in range(per):
            values[pl.ds(pl.multiple_of((g * per + k) * samples, 128), samples), :] = v[:, k * emb : (k + 1) * emb]
        store(g).start()
        return 0

    lax.fori_loop(0, steps, high, 0)
    to_scalar.wait()

    def ship(o):
        return pltpu.make_async_copy(bucket.at[o], bucket_hbm.at[o], b_sems.at[o])

    def pick(o, _):
        for k in range(slots):
            src = idx[o, k]
            bucket[o, k : k + 1, :] = values[pl.ds(src, 1), :]
        bucket[o, slots : slots + 8, :] = jnp.zeros((8, emb), f32)
        bucket[o, slots : slots + 1, :] = row_a[pl.ds(o, 1), :]
        bucket[o, slots + 1 : slots + 2, :] = row_b[pl.ds(o, 1), :]
        ship(o).start()
        return 0

    lax.fori_loop(0, owners, pick, 0)
    lax.fori_loop(0, steps, lambda g, _: (store(g).wait(), 0)[1], 0)
    lax.fori_loop(0, owners, lambda o, _: (ship(o).wait(), 0)[1], 0)


PORT = ((72, 72, 40, "xzy"), (144, 80, 40, "zxy"), (0, 72, 40, "yxz"))


def mesh_place():
    dp, y = lax.axis_index("dp"), lax.axis_index("rep")
    core = dp % 2
    return {"x": dp // 8, "z": (dp // 2) % 4, "y": y}, core, (dp + 1 - 2 * core, y)


def sender(send_sems, recv_sems, sent):
    used = [0]

    def send(src, dst, to):
        k = used[0]
        used[0] += 1
        copy = pltpu.make_async_remote_copy(
            src_ref=src, dst_ref=dst, send_sem=send_sems.at[k], recv_sem=recv_sems.at[k],
            device_id=to, device_id_type=pl.DeviceIdType.MESH,
        )
        copy.start()
        sent.append(copy)
        return copy

    return send


class Reduce:
    def __init__(self, send, near, at, add, rows, half, lands):
        self.send, self.near, self.at, self.add = send, near, at, add
        self.rows, self.half, self.lands = rows, half, lands

    def start(self):
        (_, up, far, down), to = self.near
        self.c0 = self.send(self.at(far, 0, self.half), self.lands[0], to[up])
        self.c1 = self.send(self.at(far, self.half, self.rows), self.lands[1], to[down])

    def middle(self):
        (_, up, far, down), to = self.near
        self.c0.wait_recv()
        self.add(up, 0, self.half, self.lands[:1])
        self.c2 = self.send(self.at(up, 0, self.rows), self.lands[2], to[up])
        self.c1.wait_recv()
        self.add(down, self.half, self.rows, self.lands[1:2])
        self.c3 = self.send(self.at(down, 0, self.rows), self.lands[3], to[down])

    def finish(self):
        self.c2.wait_recv()
        self.c3.wait_recv()
        self.add(self.near[0][0], 0, self.rows, self.lands[2:4])


class Direct:
    def __init__(self, send, near, at, add, lands):
        self.send, self.near, self.at, self.add, self.lands = send, near, at, add, lands

    def start(self):
        places, to = self.near
        self.got = [self.send(self.at(places[d]), self.lands[d - 1], to[places[d]]) for d in (1, 3, 2)]

    def finish(self):
        for c in self.got:
            c.wait_recv()
        self.add(self.near[0][0], self.lands)


class Spread:
    def __init__(self, send, near, at):
        self.send, self.near, self.at = send, near, at

    def start(self):
        places, to = self.near
        src = self.at(places[0])
        self.got = [self.send(src, src, to[places[d]]) for d in (1, 3, 2)]

    def finish(self):
        for c in self.got:
            c.wait_recv()


class Ids:
    def __init__(self, make):
        self.make = make

    def __getitem__(self, t):
        return self.make(t)


def neighbours(me, core, axis):
    def device(to):
        at = dict(me, **{axis: to})
        return ((at["x"] * 4 + at["z"]) * 2 + core, at["y"])

    return [(me[axis] + d) % 4 for d in range(4)], Ids(device)


def greet(peers):
    barrier = pltpu.get_barrier_semaphore()
    for peer in peers:
        pl.semaphore_signal(barrier, inc=1, device_id=peer, device_id_type=pl.DeviceIdType.MESH)
    pl.semaphore_wait(barrier, len(peers))


def weights_kernel(steps, hidden, back_low, cross, cot, values_hbm, place, *rest):
    outs, rest = rest[: len(PORT)], rest[len(PORT) :]
    freq_out, rest = rest[0], rest[1:]
    pair, rest = rest[: len(PORT)], rest[len(PORT) :]
    y_land, rest = rest[:4], rest[4:]
    f_both, f_pair, f_land, rest = rest[0], rest[1], rest[2:5], rest[5:]
    both, freq, hidden_t, down, up, bias, values, send_sems, recv_sems, local_sems = rest
    g = pl.program_id(0)
    rank = hidden.shape[1]
    wide = cross.shape[1]
    per = wide // 128
    frequent = freq.shape[0]
    samples = hidden.shape[0]
    count = frequent // 8
    width = wide * steps
    cols = per * steps
    up_rows = rank // count
    down_rows = width // count
    base = up_rows * cols
    bias_at = base + down_rows * rank // 128
    me, core, partner = mesh_place()
    near = neighbours(me, core, "y")
    load = pltpu.make_async_copy(values_hbm, values, local_sems.at[0])

    @pl.when(g == 0)
    def _():
        greet([partner] + [near[1][t] for t in near[0][1:]])
        load.start()
        hidden_t[...] = hidden[...].T
        freq[...] = jnp.zeros_like(freq)

    inner = cot[...].astype(f32) * cross[...].astype(f32)
    bias[:, pl.ds(pl.multiple_of(g * wide, wide), wide)] = jnp.sum(inner, axis=0, keepdims=True)
    u = jnp.dot(hidden_t[...], inner.astype(bf16), preferred_element_type=f32)
    for k in range(per):
        up[k * rank : (k + 1) * rank, :] = u[:, k * 128 : (k + 1) * 128]
    d = dot_tn(cross[...], back_low[...])
    for k in range(rank // 128):
        down[pl.ds(pl.multiple_of(k * width + g * wide, 128), wide), :] = d[:, k * 128 : (k + 1) * 128]

    def put_up(n, _):
        for c in range(2):
            for y in range(4):
                i = n * 8 + c * 4 + y
                for k in range(per):
                    both[n, c, y, pl.ds(g * per + k, up_rows, stride=cols), :] = up[
                        pl.ds(k * rank + i * up_rows, up_rows), :
                    ]
        return 0

    lax.fori_loop(0, count // 8, put_up, 0)

    @pl.when(g == steps - 1)
    def _():
        sent = []
        send = sender(send_sems, recv_sems, sent)

        def part(p, c):
            first, rows = PORT[p][0], PORT[p][1]
            return both.at[:, c, :, pl.ds(first, rows), :]

        got = {2: send(part(2, 1 - core), pair[2], partner)}

        def put_down(n, _):
            for c in range(2):
                for y in range(4):
                    i = n * 8 + c * 4 + y
                    for k in range(rank // 128):
                        both[n, c, y, pl.ds(base + k, down_rows, stride=rank // 128), :] = down[
                            pl.ds(k * width + i * down_rows, down_rows), :
                        ]
                    both[n, c, y, bias_at : bias_at + 8, :] = jnp.zeros((8, 128), f32)
            return 0

        lax.fori_loop(0, count // 8, put_down, 0)
        for i in range(count):
            both[i // 8, (i // 4) % 2, i % 4, bias_at : bias_at + 1, 0:down_rows] = bias[
                :, i * down_rows : (i + 1) * down_rows
            ]
        for p in (0, 1):
            got[p] = send(part(p, 1 - core), pair[p], partner)
        load.wait()
        row_iota = lax.broadcasted_iota(i32, (frequent, samples), 0)

        def tables(t, _):
            hots, parts = [], []
            for k in range(2):
                hots.append(one_hot(row_iota == place[2 * t + k]))
                parts.append(hi_lo(values[pl.ds(pl.multiple_of((2 * t + k + 1) * samples, 128), samples), :]))
            s = jnp.dot(jnp.concatenate(hots, axis=1), jnp.concatenate(parts, axis=0), preferred_element_type=f32)
            freq[...] += s[:, :128] + s[:, 128:]
            return 0

        def add_pair(p):
            first, rows = PORT[p][0], PORT[p][1]
            got[p].wait_recv()

            def add(n, _):
                for y in range(4):
                    both[n, core, y, first : first + rows, :] = (
                        both[n, core, y, first : first + rows, :] + pair[p][n, y]
                    )
                return 0

            lax.fori_loop(0, count // 8, add, 0)

        first, rows, half, _ = PORT[2]

        def y_at(t, lo, hi):
            return both.at[:, core, t, pl.ds(first + lo, hi - lo), :]

        def y_add(t, lo, hi, lands):
            def add(n, _):
                v = both[n, core, t, first + lo : first + hi, :]
                for ref in lands:
                    v = v + ref[n]
                both[n, core, t, first + lo : first + hi, :] = v
                return 0

            lax.fori_loop(0, count // 8, add, 0)

        def f_add(t, lands):
            v = f_both[:, core, t]
            for ref in lands:
                v = v + ref[...]
            f_both[:, core, t] = v

        y_sum = Reduce(send, near, y_at, y_add, rows, half, y_land)
        f_sum = Direct(send, near, lambda t: f_both.at[:, core, t], f_add, f_land)
        pairs = place.shape[0] // 2
        cut = pairs // 3
        lax.fori_loop(0, cut, tables, 0)
        add_pair(2)
        y_sum.start()
        lax.fori_loop(cut, pairs, tables, 0)
        y_sum.middle()

        def put_freq(n, _):
            for c in range(2):
                for y in range(4):
                    f_both[n, c, y] = freq[pl.ds(pl.multiple_of((n * 8 + c * 4 + y) * 8, 8), 8), :]
            return 0

        lax.fori_loop(0, count // 8, put_freq, 0)
        f_got = send(f_both.at[:, 1 - core], f_pair, partner)
        stores = []
        for p in (0, 1):
            add_pair(p)
            stores.append(pltpu.make_async_copy(part(p, core), outs[p], local_sems.at[1 + p]))
            stores[-1].start()
        f_got.wait_recv()
        f_both[:, core] = f_both[:, core] + f_pair[...]
        f_sum.start()
        y_sum.finish()
        stores.append(pltpu.make_async_copy(y_at(me["y"], 0, rows), outs[2], local_sems.at[3]))
        stores[-1].start()
        f_sum.finish()
        stores.append(pltpu.make_async_copy(f_both.at[:, core, me["y"]], freq_out, local_sems.at[4]))
        stores[-1].start()
        for c in stores:
            c.wait()
        for c in sent:
            c.wait_send()


def params(**kw):
    return pltpu.CompilerParams(vmem_limit_bytes=VLIM, **kw)


def reduce_kernel(*refs):
    it = iter(refs)
    take = lambda n: [next(it) for _ in range(n)]
    loads, (load_f, arrived), (mine, freq_out, seg_out) = take(3), take(2), take(3)
    work = take(3)
    land = {p: {k: take(4) for k in range(1 if p == 2 else 0, 3)} for p in range(3)}
    swork, sland, sgath = next(it), take(4), next(it)
    f_work, fx_land, fz_land, gath = next(it), take(3), take(3), next(it)
    arr, ids, right, acc = take(4)
    send_sems, recv_sems, local_sems = take(3)
    me, core, partner = mesh_place()
    near = {a: neighbours(me, core, a) for a in "xzy"}
    greet([partner] + [near[a][1][t] for a in "xzy" for t in near[a][0][1:]])
    sent = []
    send = sender(send_sems, recv_sems, sent)

    def where(dims, done, axis, t, rem=None):
        rem = iter(rem) if rem is not None else None
        out = []
        for a in dims:
            if a in done:
                out.append(me[a])
            elif a == axis:
                out.append(t)
            else:
                out.append(slice(None) if rem is None else next(rem))
        return tuple(out)

    def phase(p, k):
        _, rows, half, order = PORT[p]
        dims = "xz" if p == 2 else "xzy"
        done, axis = order[:k].replace("y", "") if p == 2 else order[:k], order[k]
        ref, left = work[p], 2 - k

        def at(t, lo, hi):
            return ref.at[where(dims, done, axis, t) + (pl.ds(lo, hi - lo), slice(None))]

        def add(t, lo, hi, lands):
            def one(rem):
                spot = where(dims, done, axis, t, rem) + (slice(lo, hi), slice(None))
                v = ref[spot]
                for x in lands:
                    v = v + x[rem + (slice(None), slice(None))]
                ref[spot] = v

            if left == 0:
                one(())
            elif left == 1:
                lax.fori_loop(0, 4, lambda i, _: (one((i,)), 0)[1], 0)
            else:
                lax.fori_loop(0, 16, lambda i, _: (one((i // 4, i % 4)), 0)[1], 0)

        return Reduce(send, near[axis], at, add, rows, half, land[p][k])

    sums = {(p, k): phase(p, k) for p in range(3) for k in range(1 if p == 2 else 0, 3)}

    owned = swork.shape[1]

    def s_add(t, lo, hi, lands):
        for r in range(lo, hi, 128):
            v = swork[t, r : r + 128, :]
            for ref in lands:
                v = v + ref[r - lo : r - lo + 128, :]
            swork[t, r : r + 128, :] = v

    s_red = Reduce(
        send, near["y"], lambda t, lo, hi: swork.at[t, pl.ds(lo, hi - lo), :], s_add, owned, owned // 2, sland
    )

    def f_add(spot, lands):
        v = f_work[spot]
        for ref in lands:
            v = v + ref[...]
        f_work[spot] = v

    f_x = Direct(send, near["x"], lambda t: f_work.at[t], lambda t, l: f_add((t,), l), fx_land)
    f_z = Direct(
        send, near["z"], lambda t: f_work.at[me["x"], t], lambda t, l: f_add((me["x"], t), l), fz_land
    )
    g_z = Spread(send, near["z"], lambda t: gath.at[me["x"], t, core, me["y"]])
    g_x = Spread(send, near["x"], lambda t: gath.at[t, :, core, me["y"]])
    g_y = Spread(send, near["y"], lambda t: gath.at[:, :, core, t])

    class SegGather:
        def start(self):
            (here, up, far, down), to = near["y"]
            src = sgath.at[here]
            self.c0, self.c1 = send(src, src, to[up]), send(src, src, to[down])

        def middle(self):
            (here, up, far, down), to = near["y"]
            self.c0.wait_recv()
            src = sgath.at[down, pl.ds(0, owned // 2), :]
            self.c2 = send(src, src, to[up])
            self.c1.wait_recv()
            src = sgath.at[up, pl.ds(owned // 2, owned // 2), :]
            self.c3 = send(src, src, to[down])

        def finish(self):
            self.c2.wait_recv()
            self.c3.wait_recv()

    s_gat = SegGather()
    copies = [pltpu.make_async_copy(loads[p], work[p], local_sems.at[p]) for p in range(3)]
    copy_f = pltpu.make_async_copy(load_f, f_work, local_sems.at[3])
    copy_a = pltpu.make_async_copy(arrived, arr, local_sems.at[4])
    for c in [copy_f, copies[0], copies[1], copy_a, copies[2]]:
        c.start()
    slots = arr.shape[1] - 8
    some = ids.shape[0]
    each_of = arr.shape[0] // some
    chunk = each_of * slots

    def prepare(g, _):
        rows = []
        for b in range(each_of):
            n = g * each_of + b
            rows.append(arr[n, slots : slots + 1, :])
            rows.append(arr[n, slots + 1 : slots + 2, : slots - 128])
            right[pl.ds(pl.multiple_of(n * slots, 16), slots), :] = hi_lo(arr[n, :slots, :])
        ids[g] = jnp.concatenate(rows, axis=1).astype(i32)
        return 0

    def seg_block(t):
        acc[...] = jnp.zeros_like(acc)
        first = t * owned

        def one(g, _):
            hot = one_hot(lax.broadcasted_iota(i32, (owned, chunk), 0) + first == ids[g])
            acc[...] += jnp.dot(
                hot, right[pl.ds(pl.multiple_of(g * chunk, 16), chunk), :], preferred_element_type=f32
            )
            return 0

        lax.fori_loop(0, some, one, 0)
        swork[t] = acc[:, :128] + acc[:, 128:]

    _, y_up, y_far, y_down = near["y"][0]
    copy_f.wait()
    f_x.start()
    copies[0].wait()
    sums[0, 0].start()
    copies[1].wait()
    sums[1, 0].start()
    copy_a.wait()
    lax.fori_loop(0, some, prepare, 0)
    f_x.finish()
    f_z.start()
    seg_block(y_far)
    s_red.start()
    copies[2].wait()
    seg_block(y_up)
    sums[0, 0].middle()
    sums[1, 0].middle()
    sums[2, 1].start()
    seg_block(y_down)
    s_red.middle()
    f_z.finish()
    gath[me["x"], me["z"], core, me["y"]] = f_work[me["x"], me["z"]]
    g_z.start()
    seg_block(me["y"])
    s_red.finish()
    sgath[me["y"]] = swork[me["y"]]
    s_gat.start()
    sums[0, 0].finish()
    sums[0, 1].start()
    sums[1, 0].finish()
    sums[1, 1].start()
    sums[2, 1].middle()
    g_z.finish()
    g_x.start()
    s_gat.middle()
    sums[0, 1].middle()
    sums[1, 1].middle()
    sums[2, 1].finish()
    sums[2, 2].start()
    g_x.finish()
    g_y.start()
    sums[0, 1].finish()
    sums[0, 2].start()
    sums[1, 1].finish()
    sums[1, 2].start()
    s_gat.finish()
    seg_out[...] = sgath[...]
    sums[2, 2].middle()
    g_y.finish()
    g_c = send(gath.at[:, :, core], gath.at[:, :, core], partner)
    sums[0, 2].middle()
    sums[1, 2].middle()
    g_c.wait_recv()
    freq_out[...] = gath[...]
    sums[2, 2].finish()
    sums[0, 2].finish()
    sums[1, 2].finish()
    here = (me["x"], me["z"], me["y"])
    for p, (first, rows, _, _) in enumerate(PORT):
        mine[first : first + rows, :] = work[p][here[:2] if p == 2 else here]
    for c in sent:
        c.wait_send()


def reduce_scratch(owned, arrived):
    v = lambda *s: pltpu.VMEM(s, f32)
    out = [v(*((4, 4) if p == 2 else (4, 4, 4)), PORT[p][1], 128) for p in range(3)]
    for p, (_, r, h, _) in enumerate(PORT):
        for k in range(1 if p == 2 else 0, 3):
            lead = (4,) * (2 - k)
            out += [v(*lead, h, 128), v(*lead, r - h, 128), v(*lead, r, 128), v(*lead, r, 128)]
    q = owned // 4
    out += [v(4, q, 128), v(q // 2, 128), v(q // 2, 128), v(q, 128), v(q, 128), v(4, q, 128)]
    out += [v(4, 4, 8, 128)] + [v(4, 8, 128)] * 3 + [v(8, 128)] * 3 + [v(4, 4, 2, 4, 8, 128)]
    n = arrived.shape[0] // 4
    flat = arrived.shape[0] * (arrived.shape[1] - 8)
    out += [v(*arrived.shape), pltpu.VMEM((n, 1, flat // n), i32), pltpu.VMEM((flat, 256), bf16), v(q, 256)]
    out += [pltpu.SemaphoreType.DMA((64,)), pltpu.SemaphoreType.DMA((64,)), pltpu.SemaphoreType.DMA((8,))]
    return out


def reduce_all(parts, arrived, owned):
    vmem = pl.BlockSpec(memory_space=pltpu.VMEM)
    anyw = pl.BlockSpec(memory_space=pl.ANY)
    total = max(a + r for a, r, _, _ in PORT)
    mine, freq, seg = pl.pallas_call(
        reduce_kernel,
        out_shape=(
            jax.ShapeDtypeStruct((total, 128), f32),
            jax.ShapeDtypeStruct((4, 4, 2, 4, 8, 128), f32),
            jax.ShapeDtypeStruct((4, owned // 4, 128), f32),
        ),
        in_specs=[anyw] * (len(PORT) + 2),
        out_specs=(vmem, vmem, vmem),
        scratch_shapes=reduce_scratch(owned, arrived),
        compiler_params=params(collective_id=0, has_side_effects=True),
        name="reduce_kernel",
    )(*[w.reshape(4, 4, *w.shape[1:]) for w in parts], arrived)
    return mine, freq.reshape(1024, 128), seg.reshape(owned, 128)


def body(cross_in, cotangent, weight_down, weight_up, cross_bias, row_place, frequent_table, frequent_accum, shard_table, shard_accum):
    samples, width = cross_in.shape
    rank = weight_down.shape[1]
    tables = row_place.shape[1]
    emb = frequent_table.shape[1]
    f_count = frequent_table.shape[0]
    owned = shard_table.shape[0]
    shards = lax.axis_size("dp")
    count = shards * lax.axis_size("rep")
    capacity = samples * tables // (2 * shards)
    blocks = width // emb
    per = 3
    steps = blocks // per
    wide = per * emb
    vmem = pl.BlockSpec(memory_space=pltpu.VMEM)

    place_t = row_place.T
    anyw = pl.BlockSpec(memory_space=pl.ANY)
    hidden, back_low, values, bucket = pl.pallas_call(
        functools.partial(front_kernel, f_count, owned),
        out_shape=(
            jax.ShapeDtypeStruct((samples, rank), bf16),
            jax.ShapeDtypeStruct((samples, rank), bf16),
            jax.ShapeDtypeStruct((blocks * samples, emb), f32),
            jax.ShapeDtypeStruct((shards, capacity + 8, emb), f32),
        ),
        in_specs=[vmem, vmem, anyw, anyw, anyw, anyw],
        out_specs=(vmem, vmem, anyw, anyw),
        scratch_shapes=[
            pltpu.VMEM((samples, width), bf16),
            pltpu.VMEM((samples, width), bf16),
            pltpu.VMEM((width, rank), bf16),
            pltpu.VMEM((rank, width), bf16),
            pltpu.VMEM((blocks * samples, emb), f32),
            pltpu.VMEM((shards, capacity + 8, emb), f32),
            pltpu.VMEM((tables * shards, samples), bf16),
            pltpu.VMEM((tables * shards, samples), f32),
            pltpu.VMEM((shards, 256), i32),
            pltpu.VMEM((shards, 128), f32),
            pltpu.VMEM((shards, 128), f32),
            pltpu.SMEM((shards, 256), i32),
            pltpu.VMEM((samples, rank), f32),
            pltpu.VMEM((samples, rank), f32),
            pltpu.SemaphoreType.DMA((steps, 4)),
            pltpu.SemaphoreType.DMA((steps,)),
            pltpu.SemaphoreType.DMA((shards,)),
            pltpu.SemaphoreType.DMA,
        ],
        compiler_params=params(),
        name="front_kernel",
    )(place_t, cross_bias.reshape(1, -1), cross_in, cotangent, weight_down, weight_up)

    arrived = lax.all_to_all(bucket, "dp", split_axis=0, concat_axis=0, tiled=True)

    parts = pl.pallas_call(
        functools.partial(weights_kernel, steps),
        grid=(steps,),
        out_shape=tuple(
            jax.ShapeDtypeStruct(shape, f32)
            for shape in ((16, 4, PORT[0][1], 128), (16, 4, PORT[1][1], 128), (16, PORT[2][1], 128), (16, 8, 128))
        ),
        in_specs=[
            pl.BlockSpec((samples, rank), lambda g: (0, 0)),
            pl.BlockSpec((samples, rank), lambda g: (0, 0)),
            pl.BlockSpec((samples, wide), lambda g: (0, g)),
            pl.BlockSpec((samples, wide), lambda g: (0, g)),
            anyw,
            pl.BlockSpec((tables, 1, samples), lambda g: (0, 0, 0)),
        ],
        out_specs=(anyw,) * (len(PORT) + 1),
        scratch_shapes=[pltpu.VMEM((16, 4, r, 128), f32) for _, r, _, _ in PORT]
        + [pltpu.VMEM((16, r, 128), f32) for r in (PORT[2][2], PORT[2][1] - PORT[2][2], PORT[2][1], PORT[2][1])]
        + [pltpu.VMEM((16, 2, 4, 8, 128), f32), pltpu.VMEM((16, 4, 8, 128), f32)]
        + [pltpu.VMEM((16, 8, 128), f32)] * 3
        + [
            pltpu.VMEM((16, 2, 4, max(a + r for a, r, _, _ in PORT), 128), f32),
            pltpu.VMEM((f_count, emb), f32),
            pltpu.VMEM((rank, samples), bf16),
            pltpu.VMEM((rank // 128 * width, 128), f32),
            pltpu.VMEM((per * rank, 128), f32),
            pltpu.VMEM((1, width), f32),
            pltpu.VMEM((blocks * samples, emb), f32),
            pltpu.SemaphoreType.DMA((16,)),
            pltpu.SemaphoreType.DMA((16,)),
            pltpu.SemaphoreType.DMA((8,)),
        ],
        compiler_params=params(collective_id=1, has_side_effects=True),
        name="weights_kernel",
    )(hidden, back_low, cross_in, cotangent, values, place_t.reshape(tables, 1, samples))

    mine, freq, shard_grad = reduce_all(parts, arrived, owned)
    n = rank * width // count // 128
    grad_up = mine[:n].reshape(rank // count, width)
    grad_down = mine[n : 2 * n].reshape(width // count, rank)
    grad_bias = mine[2 * n, : width // count]
    new_shard, new_shard_accum = row_adagrad(shard_table, shard_accum, shard_grad)
    new_frequent, new_frequent_accum = row_adagrad(frequent_table, frequent_accum, freq)
    return (new_frequent, new_frequent_accum, new_shard, new_shard_accum, grad_up, grad_down, grad_bias)


def solution(mesh):
    both = ("dp", "rep")
    in_specs = (P(both, None), P(both, None), P(), P(), P(), P(both, None), P(), P(), P("dp", None), P("dp"))
    out_specs = (P(), P(), P("dp", None), P("dp"), P(both, None), P(both, None), P(both))
    return jax.shard_map(body, mesh=mesh, in_specs=in_specs, out_specs=out_specs, check_vma=False)
```

```python
import functools
import jax
import jax.numpy as jnp
from jax import lax
from jax.experimental import pallas as pl
from jax.experimental.pallas import tpu as pltpu
from jax.sharding import PartitionSpec as P

learn_rate = 0.05
eps_ada = 1e-08
f32, bf16, i32 = jnp.float32, jnp.bfloat16, jnp.int32
VLIM = 66 * 1000 * 1000


def row_adagrad(table, accum, grad, new, new_accum):
    rows = table.shape[0]

    def chunk(n, _):
        at = pl.ds(pl.multiple_of(n * 128, 128), 128)
        g = grad[at, :]
        before = jnp.broadcast_to(accum[pl.ds(n, 1), :], (128, 128)).T
        after = before + jnp.mean(g * g, axis=1, keepdims=True)
        new[at, :] = table[at, :] - learn_rate * g / (jnp.sqrt(after) + eps_ada)
        new_accum[pl.ds(n, 1), :] = after.T[0:1, :]
        return 0

    lax.fori_loop(0, rows // 128, chunk, 0)


def finish_kernel(mine, freq, seg, f_table, f_accum, s_table, s_accum, new_f, new_fa, new_s, new_sa, g_up, g_down, g_bias):
    row_adagrad(s_table, s_accum, seg, new_s, new_sa)
    row_adagrad(f_table, f_accum, freq, new_f, new_fa)
    up_rows, down_rows = g_up.shape[0], g_down.shape[0]
    cols = g_up.shape[1] // 128
    for c in range(cols):
        g_up[:, c * 128 : (c + 1) * 128] = mine[pl.ds(c, up_rows, stride=cols), :]
    first, cols = up_rows * cols, g_down.shape[1] // 128
    for c in range(cols):
        g_down[:, c * 128 : (c + 1) * 128] = mine[pl.ds(first + c, down_rows, stride=cols), :]
    g_bias[...] = mine[first + down_rows * cols : first + down_rows * cols + 1, 0:down_rows]


def dot_nt(a, b):
    return lax.dot_general(a, b, (((1,), (1,)), ((), ())), preferred_element_type=f32)


def dot_tn(a, b):
    return lax.dot_general(a, b, (((0,), (0,)), ((), ())), preferred_element_type=f32)


def hi_lo(v):
    hi = v.astype(bf16)
    lo = (v - hi.astype(f32)).astype(bf16)
    return jnp.concatenate([hi, lo], axis=1)


def one_hot(flags):
    return jnp.where(flags, 1.0, 0.0).astype(bf16)


def index_work(frequent, owned, place, idx, row_a, row_b, hot, cum):
    tables, samples = place.shape
    owners, slots = idx.shape
    at = lax.broadcasted_iota(i32, (1, samples), 1)
    owner_iota = lax.broadcasted_iota(i32, (owners, samples), 0)
    tri = one_hot(
        lax.broadcasted_iota(i32, (samples, samples), 0)
        < lax.broadcasted_iota(i32, (samples, samples), 1)
    )
    shift = owned.bit_length() - 1
    for t in range(tables):
        owner = lax.shift_right_arithmetic(place[t : t + 1, :] - frequent, shift)
        hot[t * owners : (t + 1) * owners, :] = one_hot(owner_iota == owner)
    cum[...] = jnp.dot(hot[...], tri, preferred_element_type=f32)
    base = jnp.zeros((owners, 1), f32)
    total = jnp.zeros((4 * owners, slots), f32)
    slot_iota = lax.broadcasted_iota(i32, (slots, samples), 0)
    at_hi = lax.shift_right_logical(at, 7).astype(f32)
    at_lo = (at & 127).astype(f32)
    blocks = samples // 128
    for t in range(tables):
        mine = hot[t * owners : (t + 1) * owners, :].astype(f32)
        before = cum[t * owners : (t + 1) * owners, :] + base
        rank = jnp.sum(mine * before, axis=0, keepdims=True).astype(i32)
        base = before[:, samples - 1 :] + mine[:, samples - 1 :]
        local = (place[t : t + 1, :] - frequent) & (owned - 1)
        parts = [
            mine * (at_hi + float((t + 1) * blocks)),
            mine * at_lo,
            mine * (lax.shift_right_logical(local, 7) + 1).astype(f32),
            mine * (local & 127).astype(f32),
        ]
        left = jnp.concatenate(parts, axis=0).astype(bf16)
        total = total + dot_nt(left, one_hot(slot_iota == rank))
    idx[...] = (total[:owners] * 128.0 + total[owners : 2 * owners]).astype(i32)
    row = (total[2 * owners : 3 * owners] - 1.0) * 128.0 + total[3 * owners :]
    row_a[...] = row[:, :128]
    row_b[...] = row[:, 128:]


def front_kernel(
    frequent, owned, place, bias, cross_hbm, cot_hbm, down_hbm, up_hbm,
    hidden, back_low, values_hbm, bucket_hbm,
    cross, cot, down, up, values, bucket, hot, cum, idx_v, row_a, row_b, idx, h_acc, b_acc, in_sems, v_sems, b_sems, i_sem,
):
    samples = hidden.shape[0]
    emb = values.shape[1]
    pieces = in_sems.shape[0]
    steps = v_sems.shape[0]
    wide = cross.shape[1] // steps
    thin = cross.shape[1] // pieces
    per = wide // emb
    owners = bucket.shape[0]
    slots = bucket.shape[1] - 8

    def loads(g):
        cols = pl.ds(pl.multiple_of(g * thin, 128), thin)
        return [
            pltpu.make_async_copy(cross_hbm.at[:, cols], cross.at[:, cols], in_sems.at[g, 0]),
            pltpu.make_async_copy(cot_hbm.at[:, cols], cot.at[:, cols], in_sems.at[g, 1]),
            pltpu.make_async_copy(down_hbm.at[cols, :], down.at[cols, :], in_sems.at[g, 2]),
            pltpu.make_async_copy(up_hbm.at[:, cols], up.at[:, cols], in_sems.at[g, 3]),
        ]

    for g in range(pieces):
        for c in loads(g):
            c.start()
    index_work(frequent, owned, place, idx_v, row_a, row_b, hot, cum)
    to_scalar = pltpu.make_async_copy(idx_v, idx, i_sem)
    to_scalar.start()
    h_acc[...] = jnp.zeros_like(h_acc)
    b_acc[...] = jnp.zeros_like(b_acc)

    def low(g, _):
        for n in range(pieces // steps):
            for c in loads(g * (pieces // steps) + n):
                c.wait()
        cols = pl.ds(pl.multiple_of(g * wide, wide), wide)
        x = cross[:, cols]
        inner = (cot[:, cols].astype(f32) * x.astype(f32)).astype(bf16)
        h_acc[...] += jnp.dot(x, down[cols, :], preferred_element_type=f32)
        b_acc[...] += dot_nt(inner, up[:, cols])
        return 0

    lax.fori_loop(0, steps, low, 0)
    hidden[...] = h_acc[...].astype(bf16)
    back_low[...] = b_acc[...].astype(bf16)

    def store(g):
        part = pl.ds(pl.multiple_of(g * per * samples, 128), per * samples)
        return pltpu.make_async_copy(values.at[part], values_hbm.at[part], v_sems.at[g])

    def high(g, _):
        cols = pl.ds(pl.multiple_of(g * wide, wide), wide)
        scaled = jnp.dot(hidden[...], up[:, cols], preferred_element_type=f32) + bias[cols].reshape(1, wide)
        v = cot[:, cols].astype(f32) * (scaled + 1.0) + dot_nt(back_low[...], down[cols, :])
        for k in range(per):
            values[pl.ds(pl.multiple_of((g * per + k) * samples, 128), samples), :] = v[:, k * emb : (k + 1) * emb]
        store(g).start()
        return 0

    lax.fori_loop(0, steps, high, 0)
    to_scalar.wait()

    def ship(o):
        return pltpu.make_async_copy(bucket.at[o], bucket_hbm.at[o], b_sems.at[o])

    def pick(o, _):
        for k in range(slots):
            src = idx[o, k]
            bucket[o, k : k + 1, :] = values[pl.ds(src, 1), :]
        bucket[o, slots : slots + 8, :] = jnp.zeros((8, emb), f32)
        bucket[o, slots : slots + 1, :] = row_a[pl.ds(o, 1), :]
        bucket[o, slots + 1 : slots + 2, :] = row_b[pl.ds(o, 1), :]
        ship(o).start()
        return 0

    lax.fori_loop(0, owners, pick, 0)
    lax.fori_loop(0, steps, lambda g, _: (store(g).wait(), 0)[1], 0)
    lax.fori_loop(0, owners, lambda o, _: (ship(o).wait(), 0)[1], 0)


PORT = ((72, 72, 40, "xzy"), (144, 80, 40, "zxy"), (0, 72, 40, "yxz"))


def mesh_place():
    dp, y = lax.axis_index("dp"), lax.axis_index("rep")
    core = dp % 2
    return {"x": dp // 8, "z": (dp // 2) % 4, "y": y}, core, (dp + 1 - 2 * core, y)


def sender(send_sems, recv_sems, sent):
    used = [0]

    def send(src, dst, to):
        k = used[0]
        used[0] += 1
        copy = pltpu.make_async_remote_copy(
            src_ref=src, dst_ref=dst, send_sem=send_sems.at[k], recv_sem=recv_sems.at[k],
            device_id=to, device_id_type=pl.DeviceIdType.MESH,
        )
        copy.start()
        sent.append(copy)
        return copy

    return send


class Reduce:
    def __init__(self, send, near, at, add, rows, half, lands):
        self.send, self.near, self.at, self.add = send, near, at, add
        self.rows, self.half, self.lands = rows, half, lands

    def start(self):
        (_, up, far, down), to = self.near
        self.c0 = self.send(self.at(far, 0, self.half), self.lands[0], to[up])
        self.c1 = self.send(self.at(far, self.half, self.rows), self.lands[1], to[down])

    def middle(self):
        (_, up, far, down), to = self.near
        self.c0.wait_recv()
        self.add(up, 0, self.half, self.lands[:1])
        self.c2 = self.send(self.at(up, 0, self.rows), self.lands[2], to[up])
        self.c1.wait_recv()
        self.add(down, self.half, self.rows, self.lands[1:2])
        self.c3 = self.send(self.at(down, 0, self.rows), self.lands[3], to[down])

    def finish(self):
        self.c2.wait_recv()
        self.c3.wait_recv()
        self.add(self.near[0][0], 0, self.rows, self.lands[2:4])


class Direct:
    def __init__(self, send, near, at, add, lands):
        self.send, self.near, self.at, self.add, self.lands = send, near, at, add, lands

    def start(self):
        places, to = self.near
        self.got = [self.send(self.at(places[d]), self.lands[d - 1], to[places[d]]) for d in (1, 3, 2)]

    def finish(self):
        for c in self.got:
            c.wait_recv()
        self.add(self.near[0][0], self.lands)


class Spread:
    def __init__(self, send, near, at):
        self.send, self.near, self.at = send, near, at

    def start(self):
        places, to = self.near
        src = self.at(places[0])
        self.got = [self.send(src, src, to[places[d]]) for d in (1, 3, 2)]

    def finish(self):
        for c in self.got:
            c.wait_recv()


class Ids:
    def __init__(self, make):
        self.make = make

    def __getitem__(self, t):
        return self.make(t)


def neighbours(me, core, axis):
    def device(to):
        at = dict(me, **{axis: to})
        return ((at["x"] * 4 + at["z"]) * 2 + core, at["y"])

    return [(me[axis] + d) % 4 for d in range(4)], Ids(device)


def greet(peers):
    barrier = pltpu.get_barrier_semaphore()
    for peer in peers:
        pl.semaphore_signal(barrier, inc=1, device_id=peer, device_id_type=pl.DeviceIdType.MESH)
    pl.semaphore_wait(barrier, len(peers))


def weights_kernel(steps, hidden, back_low, cross, cot, values_hbm, place_in, *rest):
    outs, rest = rest[: len(PORT)], rest[len(PORT) :]
    freq_out, rest = rest[0], rest[1:]
    pair, rest = rest[: len(PORT)], rest[len(PORT) :]
    y_land, rest = rest[:4], rest[4:]
    f_both, f_pair, f_land, rest = rest[0], rest[1], rest[2:5], rest[5:]
    both, freq, hidden_t, down, up, bias, values, place, send_sems, recv_sems, local_sems = rest
    g = pl.program_id(0)
    rank = hidden.shape[1]
    wide = cross.shape[1]
    per = wide // 128
    frequent = freq.shape[0]
    samples = hidden.shape[0]
    count = frequent // 8
    width = wide * steps
    cols = per * steps
    up_rows = rank // count
    down_rows = width // count
    base = up_rows * cols
    bias_at = base + down_rows * rank // 128
    me, core, partner = mesh_place()
    near = neighbours(me, core, "y")
    load = pltpu.make_async_copy(values_hbm, values, local_sems.at[0])

    @pl.when(g == 0)
    def _():
        greet([partner] + [near[1][t] for t in near[0][1:]])
        load.start()
        hidden_t[...] = hidden[...].T
        for t in range(place.shape[0]):
            place[t] = place_in[t : t + 1, :]
        freq[...] = jnp.zeros_like(freq)

    inner = cot[...].astype(f32) * cross[...].astype(f32)
    bias[:, pl.ds(pl.multiple_of(g * wide, wide), wide)] = jnp.sum(inner, axis=0, keepdims=True)
    u = jnp.dot(hidden_t[...], inner.astype(bf16), preferred_element_type=f32)
    for k in range(per):
        up[k * rank : (k + 1) * rank, :] = u[:, k * 128 : (k + 1) * 128]
    d = dot_tn(cross[...], back_low[...])
    for k in range(rank // 128):
        down[pl.ds(pl.multiple_of(k * width + g * wide, 128), wide), :] = d[:, k * 128 : (k + 1) * 128]

    def put_up(n, _):
        for c in range(2):
            for y in range(4):
                i = n * 8 + c * 4 + y
                for k in range(per):
                    both[n, c, y, pl.ds(g * per + k, up_rows, stride=cols), :] = up[
                        pl.ds(k * rank + i * up_rows, up_rows), :
                    ]
        return 0

    lax.fori_loop(0, count // 8, put_up, 0)

    @pl.when(g == steps - 1)
    def _():
        sent = []
        send = sender(send_sems, recv_sems, sent)

        def part(p, c):
            first, rows = PORT[p][0], PORT[p][1]
            return both.at[:, c, :, pl.ds(first, rows), :]

        got = {2: send(part(2, 1 - core), pair[2], partner)}

        def put_down(n, _):
            for c in range(2):
                for y in range(4):
                    i = n * 8 + c * 4 + y
                    for k in range(rank // 128):
                        both[n, c, y, pl.ds(base + k, down_rows, stride=rank // 128), :] = down[
                            pl.ds(k * width + i * down_rows, down_rows), :
                        ]
                    both[n, c, y, bias_at : bias_at + 8, :] = jnp.zeros((8, 128), f32)
            return 0

        lax.fori_loop(0, count // 8, put_down, 0)
        for i in range(count):
            both[i // 8, (i // 4) % 2, i % 4, bias_at : bias_at + 1, 0:down_rows] = bias[
                :, i * down_rows : (i + 1) * down_rows
            ]
        for p in (0, 1):
            got[p] = send(part(p, 1 - core), pair[p], partner)
        load.wait()
        row_iota = lax.broadcasted_iota(i32, (frequent, samples), 0)

        def tables(t, _):
            hots, parts = [], []
            for k in range(2):
                hots.append(one_hot(row_iota == place[2 * t + k]))
                parts.append(hi_lo(values[pl.ds(pl.multiple_of((2 * t + k + 1) * samples, 128), samples), :]))
            s = jnp.dot(jnp.concatenate(hots, axis=1), jnp.concatenate(parts, axis=0), preferred_element_type=f32)
            freq[...] += s[:, :128] + s[:, 128:]
            return 0

        def add_pair(p):
            first, rows = PORT[p][0], PORT[p][1]
            got[p].wait_recv()

            def add(n, _):
                for y in range(4):
                    both[n, core, y, first : first + rows, :] = (
                        both[n, core, y, first : first + rows, :] + pair[p][n, y]
                    )
                return 0

            lax.fori_loop(0, count // 8, add, 0)

        first, rows, half, _ = PORT[2]

        def y_at(t, lo, hi):
            return both.at[:, core, t, pl.ds(first + lo, hi - lo), :]

        def y_add(t, lo, hi, lands):
            def add(n, _):
                v = both[n, core, t, first + lo : first + hi, :]
                for ref in lands:
                    v = v + ref[n]
                both[n, core, t, first + lo : first + hi, :] = v
                return 0

            lax.fori_loop(0, count // 8, add, 0)

        def f_add(t, lands):
            v = f_both[:, core, t]
            for ref in lands:
                v = v + ref[...]
            f_both[:, core, t] = v

        y_sum = Reduce(send, near, y_at, y_add, rows, half, y_land)
        f_sum = Direct(send, near, lambda t: f_both.at[:, core, t], f_add, f_land)
        pairs = place.shape[0] // 2
        cut = pairs // 3
        lax.fori_loop(0, cut, tables, 0)
        add_pair(2)
        y_sum.start()
        lax.fori_loop(cut, pairs, tables, 0)
        y_sum.middle()

        def put_freq(n, _):
            for c in range(2):
                for y in range(4):
                    f_both[n, c, y] = freq[pl.ds(pl.multiple_of((n * 8 + c * 4 + y) * 8, 8), 8), :]
            return 0

        lax.fori_loop(0, count // 8, put_freq, 0)
        f_got = send(f_both.at[:, 1 - core], f_pair, partner)
        stores = []
        for p in (0, 1):
            add_pair(p)
            stores.append(pltpu.make_async_copy(part(p, core), outs[p], local_sems.at[1 + p]))
            stores[-1].start()
        f_got.wait_recv()
        f_both[:, core] = f_both[:, core] + f_pair[...]
        f_sum.start()
        y_sum.finish()
        stores.append(pltpu.make_async_copy(y_at(me["y"], 0, rows), outs[2], local_sems.at[3]))
        stores[-1].start()
        f_sum.finish()
        stores.append(pltpu.make_async_copy(f_both.at[:, core, me["y"]], freq_out, local_sems.at[4]))
        stores[-1].start()
        for c in stores:
            c.wait()
        for c in sent:
            c.wait_send()


def params(**kw):
    return pltpu.CompilerParams(vmem_limit_bytes=VLIM, **kw)


def reduce_kernel(*refs):
    it = iter(refs)
    take = lambda n: [next(it) for _ in range(n)]
    loads, (load_f, arrived), (mine, freq_out, seg_out) = take(3), take(2), take(3)
    work = take(3)
    land = {p: {k: take(4) for k in range(1 if p == 2 else 0, 3)} for p in range(3)}
    swork, sland, sgath = next(it), take(4), next(it)
    f_work, fx_land, fz_land, gath = next(it), take(3), take(3), next(it)
    arr, ids, right, acc = take(4)
    send_sems, recv_sems, local_sems = take(3)
    me, core, partner = mesh_place()
    near = {a: neighbours(me, core, a) for a in "xzy"}
    greet([partner] + [near[a][1][t] for a in "xzy" for t in near[a][0][1:]])
    sent = []
    send = sender(send_sems, recv_sems, sent)

    def where(dims, done, axis, t, rem=None):
        rem = iter(rem) if rem is not None else None
        out = []
        for a in dims:
            if a in done:
                out.append(me[a])
            elif a == axis:
                out.append(t)
            else:
                out.append(slice(None) if rem is None else next(rem))
        return tuple(out)

    def phase(p, k):
        _, rows, half, order = PORT[p]
        dims = "xz" if p == 2 else "xzy"
        done, axis = order[:k].replace("y", "") if p == 2 else order[:k], order[k]
        ref, left = work[p], 2 - k

        def at(t, lo, hi):
            return ref.at[where(dims, done, axis, t) + (pl.ds(lo, hi - lo), slice(None))]

        def add(t, lo, hi, lands):
            def one(rem):
                spot = where(dims, done, axis, t, rem) + (slice(lo, hi), slice(None))
                v = ref[spot]
                for x in lands:
                    v = v + x[rem + (slice(None), slice(None))]
                ref[spot] = v

            if left == 0:
                one(())
            elif left == 1:
                lax.fori_loop(0, 4, lambda i, _: (one((i,)), 0)[1], 0)
            else:
                lax.fori_loop(0, 16, lambda i, _: (one((i // 4, i % 4)), 0)[1], 0)

        return Reduce(send, near[axis], at, add, rows, half, land[p][k])

    sums = {(p, k): phase(p, k) for p in range(3) for k in range(1 if p == 2 else 0, 3)}

    owned = swork.shape[1]

    def s_add(t, lo, hi, lands):
        for r in range(lo, hi, 128):
            v = swork[t, r : r + 128, :]
            for ref in lands:
                v = v + ref[r - lo : r - lo + 128, :]
            swork[t, r : r + 128, :] = v

    s_red = Reduce(
        send, near["y"], lambda t, lo, hi: swork.at[t, pl.ds(lo, hi - lo), :], s_add, owned, owned // 2, sland
    )

    def f_add(spot, lands):
        v = f_work[spot]
        for ref in lands:
            v = v + ref[...]
        f_work[spot] = v

    f_x = Direct(send, near["x"], lambda t: f_work.at[t], lambda t, l: f_add((t,), l), fx_land)
    f_z = Direct(
        send, near["z"], lambda t: f_work.at[me["x"], t], lambda t, l: f_add((me["x"], t), l), fz_land
    )
    g_z = Spread(send, near["z"], lambda t: gath.at[me["x"], t, core, me["y"]])
    g_x = Spread(send, near["x"], lambda t: gath.at[t, :, core, me["y"]])
    g_y = Spread(send, near["y"], lambda t: gath.at[:, :, core, t])

    class SegGather:
        def start(self):
            (here, up, far, down), to = near["y"]
            src = sgath.at[here]
            self.c0, self.c1 = send(src, src, to[up]), send(src, src, to[down])

        def middle(self):
            (here, up, far, down), to = near["y"]
            self.c0.wait_recv()
            src = sgath.at[down, pl.ds(0, owned // 2), :]
            self.c2 = send(src, src, to[up])
            self.c1.wait_recv()
            src = sgath.at[up, pl.ds(owned // 2, owned // 2), :]
            self.c3 = send(src, src, to[down])

        def finish(self):
            self.c2.wait_recv()
            self.c3.wait_recv()

    s_gat = SegGather()
    copies = [pltpu.make_async_copy(loads[p], work[p], local_sems.at[p]) for p in range(3)]
    copy_f = pltpu.make_async_copy(load_f, f_work, local_sems.at[3])
    copy_a = pltpu.make_async_copy(arrived, arr, local_sems.at[4])
    for c in [copy_f, copies[0], copies[1], copy_a, copies[2]]:
        c.start()
    slots = arr.shape[1] - 8
    some = ids.shape[0]
    each_of = arr.shape[0] // some
    chunk = each_of * slots

    def prepare(g, _):
        rows = []
        for b in range(each_of):
            n = g * each_of + b
            rows.append(arr[n, slots : slots + 1, :])
            rows.append(arr[n, slots + 1 : slots + 2, : slots - 128])
            right[pl.ds(pl.multiple_of(n * slots, 16), slots), :] = hi_lo(arr[n, :slots, :])
        ids[g] = jnp.concatenate(rows, axis=1).astype(i32)
        return 0

    def seg_block(t):
        acc[...] = jnp.zeros_like(acc)
        first = t * owned

        def one(g, _):
            hot = one_hot(lax.broadcasted_iota(i32, (owned, chunk), 0) + first == ids[g])
            acc[...] += jnp.dot(
                hot, right[pl.ds(pl.multiple_of(g * chunk, 16), chunk), :], preferred_element_type=f32
            )
            return 0

        lax.fori_loop(0, some, one, 0)
        swork[t] = acc[:, :128] + acc[:, 128:]

    _, y_up, y_far, y_down = near["y"][0]
    copy_f.wait()
    f_x.start()
    copies[0].wait()
    sums[0, 0].start()
    copies[1].wait()
    sums[1, 0].start()
    copy_a.wait()
    lax.fori_loop(0, some, prepare, 0)
    f_x.finish()
    f_z.start()
    seg_block(y_far)
    s_red.start()
    copies[2].wait()
    seg_block(y_up)
    sums[0, 0].middle()
    sums[1, 0].middle()
    sums[2, 1].start()
    seg_block(y_down)
    s_red.middle()
    f_z.finish()
    gath[me["x"], me["z"], core, me["y"]] = f_work[me["x"], me["z"]]
    g_z.start()
    seg_block(me["y"])
    s_red.finish()
    sgath[me["y"]] = swork[me["y"]]
    s_gat.start()
    sums[0, 0].finish()
    sums[0, 1].start()
    sums[1, 0].finish()
    sums[1, 1].start()
    sums[2, 1].middle()
    g_z.finish()
    g_x.start()
    s_gat.middle()
    sums[0, 1].middle()
    sums[1, 1].middle()
    sums[2, 1].finish()
    sums[2, 2].start()
    g_x.finish()
    g_y.start()
    sums[0, 1].finish()
    sums[0, 2].start()
    sums[1, 1].finish()
    sums[1, 2].start()
    s_gat.finish()
    seg_out[...] = sgath[...]
    sums[2, 2].middle()
    g_y.finish()
    g_c = send(gath.at[:, :, core], gath.at[:, :, core], partner)
    sums[0, 2].middle()
    sums[1, 2].middle()
    g_c.wait_recv()
    freq_out[...] = gath[...]
    sums[2, 2].finish()
    sums[0, 2].finish()
    sums[1, 2].finish()
    here = (me["x"], me["z"], me["y"])
    for p, (first, rows, _, _) in enumerate(PORT):
        mine[first : first + rows, :] = work[p][here[:2] if p == 2 else here]
    for c in sent:
        c.wait_send()


def reduce_scratch(owned, arrived):
    v = lambda *s: pltpu.VMEM(s, f32)
    out = [v(*((4, 4) if p == 2 else (4, 4, 4)), PORT[p][1], 128) for p in range(3)]
    for p, (_, r, h, _) in enumerate(PORT):
        for k in range(1 if p == 2 else 0, 3):
            lead = (4,) * (2 - k)
            out += [v(*lead, h, 128), v(*lead, r - h, 128), v(*lead, r, 128), v(*lead, r, 128)]
    q = owned // 4
    out += [v(4, q, 128), v(q // 2, 128), v(q // 2, 128), v(q, 128), v(q, 128), v(4, q, 128)]
    out += [v(4, 4, 8, 128)] + [v(4, 8, 128)] * 3 + [v(8, 128)] * 3 + [v(4, 4, 2, 4, 8, 128)]
    n = arrived.shape[0] // 4
    flat = arrived.shape[0] * (arrived.shape[1] - 8)
    out += [v(*arrived.shape), pltpu.VMEM((n, 1, flat // n), i32), pltpu.VMEM((flat, 256), bf16), v(q, 256)]
    out += [pltpu.SemaphoreType.DMA((64,)), pltpu.SemaphoreType.DMA((64,)), pltpu.SemaphoreType.DMA((8,))]
    return out


def reduce_all(parts, arrived, owned):
    vmem = pl.BlockSpec(memory_space=pltpu.VMEM)
    anyw = pl.BlockSpec(memory_space=pl.ANY)
    total = max(a + r for a, r, _, _ in PORT)
    mine, freq, seg = pl.pallas_call(
        reduce_kernel,
        out_shape=(
            jax.ShapeDtypeStruct((total, 128), f32),
            jax.ShapeDtypeStruct((4, 4, 2, 4, 8, 128), f32),
            jax.ShapeDtypeStruct((4, owned // 4, 128), f32),
        ),
        in_specs=[anyw] * (len(PORT) + 2),
        out_specs=(vmem, vmem, vmem),
        scratch_shapes=reduce_scratch(owned, arrived),
        compiler_params=params(collective_id=0, has_side_effects=True),
        name="reduce_kernel",
    )(*[w.reshape(4, 4, *w.shape[1:]) for w in parts], arrived)
    return mine, freq.reshape(1024, 128), seg.reshape(owned, 128)


def body(cross_in, cotangent, weight_down, weight_up, cross_bias, row_place, frequent_table, frequent_accum, shard_table, shard_accum):
    samples, width = cross_in.shape
    rank = weight_down.shape[1]
    tables = row_place.shape[1]
    emb = frequent_table.shape[1]
    f_count = frequent_table.shape[0]
    owned = shard_table.shape[0]
    shards = lax.axis_size("dp")
    count = shards * lax.axis_size("rep")
    capacity = samples * tables // (2 * shards)
    blocks = width // emb
    per = 3
    steps = blocks // per
    wide = per * emb
    vmem = pl.BlockSpec(memory_space=pltpu.VMEM)

    place_t = row_place.T
    anyw = pl.BlockSpec(memory_space=pl.ANY)
    hidden, back_low, values, bucket = pl.pallas_call(
        functools.partial(front_kernel, f_count, owned),
        out_shape=(
            jax.ShapeDtypeStruct((samples, rank), bf16),
            jax.ShapeDtypeStruct((samples, rank), bf16),
            jax.ShapeDtypeStruct((blocks * samples, emb), f32),
            jax.ShapeDtypeStruct((shards, capacity + 8, emb), f32),
        ),
        in_specs=[vmem, vmem, anyw, anyw, anyw, anyw],
        out_specs=(vmem, vmem, anyw, anyw),
        scratch_shapes=[
            pltpu.VMEM((samples, width), bf16),
            pltpu.VMEM((samples, width), bf16),
            pltpu.VMEM((width, rank), bf16),
            pltpu.VMEM((rank, width), bf16),
            pltpu.VMEM((blocks * samples, emb), f32),
            pltpu.VMEM((shards, capacity + 8, emb), f32),
            pltpu.VMEM((tables * shards, samples), bf16),
            pltpu.VMEM((tables * shards, samples), f32),
            pltpu.VMEM((shards, 256), i32),
            pltpu.VMEM((shards, 128), f32),
            pltpu.VMEM((shards, 128), f32),
            pltpu.SMEM((shards, 256), i32),
            pltpu.VMEM((samples, rank), f32),
            pltpu.VMEM((samples, rank), f32),
            pltpu.SemaphoreType.DMA((steps, 4)),
            pltpu.SemaphoreType.DMA((3,)),
            pltpu.SemaphoreType.DMA((shards,)),
            pltpu.SemaphoreType.DMA,
        ],
        compiler_params=params(),
        name="front_kernel",
    )(place_t, cross_bias, cross_in, cotangent, weight_down, weight_up)

    arrived = lax.all_to_all(bucket, "dp", split_axis=0, concat_axis=0, tiled=True)

    parts = pl.pallas_call(
        functools.partial(weights_kernel, steps),
        grid=(steps,),
        out_shape=tuple(
            jax.ShapeDtypeStruct(shape, f32)
            for shape in ((16, 4, PORT[0][1], 128), (16, 4, PORT[1][1], 128), (16, PORT[2][1], 128), (16, 8, 128))
        ),
        in_specs=[
            pl.BlockSpec((samples, rank), lambda g: (0, 0)),
            pl.BlockSpec((samples, rank), lambda g: (0, 0)),
            pl.BlockSpec((samples, wide), lambda g: (0, g)),
            pl.BlockSpec((samples, wide), lambda g: (0, g)),
            anyw,
            pl.BlockSpec((tables, samples), lambda g: (0, 0)),
        ],
        out_specs=(anyw,) * (len(PORT) + 1),
        scratch_shapes=[pltpu.VMEM((16, 4, r, 128), f32) for _, r, _, _ in PORT]
        + [pltpu.VMEM((16, r, 128), f32) for r in (PORT[2][2], PORT[2][1] - PORT[2][2], PORT[2][1], PORT[2][1])]
        + [pltpu.VMEM((16, 2, 4, 8, 128), f32), pltpu.VMEM((16, 4, 8, 128), f32)]
        + [pltpu.VMEM((16, 8, 128), f32)] * 3
        + [
            pltpu.VMEM((16, 2, 4, max(a + r for a, r, _, _ in PORT), 128), f32),
            pltpu.VMEM((f_count, emb), f32),
            pltpu.VMEM((rank, samples), bf16),
            pltpu.VMEM((rank // 128 * width, 128), f32),
            pltpu.VMEM((per * rank, 128), f32),
            pltpu.VMEM((1, width), f32),
            pltpu.VMEM((blocks * samples, emb), f32),
            pltpu.VMEM((tables, 1, samples), i32),
            pltpu.SemaphoreType.DMA((16,)),
            pltpu.SemaphoreType.DMA((16,)),
            pltpu.SemaphoreType.DMA((8,)),
        ],
        compiler_params=params(collective_id=1, has_side_effects=True),
        name="weights_kernel",
    )(hidden, back_low, cross_in, cotangent, values, place_t)

    mine, freq, shard_grad = reduce_all(parts, arrived, owned)
    n = width // count
    new_frequent, new_frequent_accum, new_shard, new_shard_accum, grad_up, grad_down, grad_bias = pl.pallas_call(
        finish_kernel,
        out_shape=(
            jax.ShapeDtypeStruct((f_count, emb), f32),
            jax.ShapeDtypeStruct((f_count // 128, 128), f32),
            jax.ShapeDtypeStruct((owned, emb), f32),
            jax.ShapeDtypeStruct((owned // 128, 128), f32),
            jax.ShapeDtypeStruct((rank // count, width), f32),
            jax.ShapeDtypeStruct((n, rank), f32),
            jax.ShapeDtypeStruct((1, n), f32),
        ),
        in_specs=[vmem] * 7,
        out_specs=(vmem,) * 7,
        compiler_params=pltpu.CompilerParams(vmem_limit_bytes=16 * 1024 * 1024),
        name="finish_kernel",
    )(
        mine, freq, shard_grad, frequent_table, frequent_accum.reshape(-1, 128),
        shard_table, shard_accum.reshape(-1, 128),
    )
    new_frequent_accum, new_shard_accum = new_frequent_accum.reshape(-1), new_shard_accum.reshape(-1)
    grad_bias = grad_bias.reshape(-1)
    return (new_frequent, new_frequent_accum, new_shard, new_shard_accum, grad_up, grad_down, grad_bias)


def solution(mesh):
    both = ("dp", "rep")
    in_specs = (P(both, None), P(both, None), P(), P(), P(), P(both, None), P(), P(), P("dp", None), P("dp"))
    out_specs = (P(), P(), P("dp", None), P("dp"), P(both, None), P(both, None), P(both))
    return jax.shard_map(body, mesh=mesh, in_specs=in_specs, out_specs=out_specs, check_vma=False)
```

```python
import functools
import jax
import jax.numpy as jnp
from jax import lax
from jax.experimental import pallas as pl
from jax.experimental.pallas import tpu as pltpu
from jax.sharding import PartitionSpec as P

learn_rate = 0.05
eps_ada = 1e-08
f32, bf16, i32 = jnp.float32, jnp.bfloat16, jnp.int32
VLIM = 66 * 1000 * 1000


def row_adagrad(table, accum, grad_of, new, new_accum):
    def chunk(n, _):
        at = pl.ds(pl.multiple_of(n * 128, 128), 128)
        g = grad_of(n)
        before = jnp.broadcast_to(accum[pl.ds(n, 1), :], (128, 128)).T
        after = before + jnp.mean(g * g, axis=1, keepdims=True)
        new[at, :] = table[at, :] - learn_rate * g / (jnp.sqrt(after) + eps_ada)
        new_accum[pl.ds(n, 1), :] = after.T[0:1, :]
        return 0

    lax.fori_loop(0, table.shape[0] // 128, chunk, 0)


def move_kernel(*refs):
    n = len(refs) // 3
    src, dst, held, sems = refs[:n], refs[n : 2 * n], refs[2 * n : 3 * n], refs[3 * n]
    takes = [pltpu.make_async_copy(a, b, sems.at[0, i]) for i, (a, b) in enumerate(zip(src, held))]
    gives = [pltpu.make_async_copy(a, b, sems.at[1, i]) for i, (a, b) in enumerate(zip(held, dst))]
    for c in takes:
        c.start()
    for c, d in zip(takes, gives):
        c.wait()
        d.start()
    for d in gives:
        d.wait()


def dot_nt(a, b):
    return lax.dot_general(a, b, (((1,), (1,)), ((), ())), preferred_element_type=f32)


def dot_tn(a, b):
    return lax.dot_general(a, b, (((0,), (0,)), ((), ())), preferred_element_type=f32)


def hi_lo(v):
    hi = v.astype(bf16)
    lo = (v - hi.astype(f32)).astype(bf16)
    return jnp.concatenate([hi, lo], axis=1)


def one_hot(flags):
    return jnp.where(flags, 1.0, 0.0).astype(bf16)


def index_work(frequent, owned, place, idx, row_a, row_b, hot, cum):
    tables, samples = place.shape
    owners, slots = idx.shape
    at = lax.broadcasted_iota(i32, (1, samples), 1)
    owner_iota = lax.broadcasted_iota(i32, (owners, samples), 0)
    tri = one_hot(
        lax.broadcasted_iota(i32, (samples, samples), 0)
        < lax.broadcasted_iota(i32, (samples, samples), 1)
    )
    shift = owned.bit_length() - 1
    for t in range(tables):
        owner = lax.shift_right_arithmetic(place[t : t + 1, :] - frequent, shift)
        hot[t * owners : (t + 1) * owners, :] = one_hot(owner_iota == owner)
    cum[...] = jnp.dot(hot[...], tri, preferred_element_type=f32)
    base = jnp.zeros((owners, 1), f32)
    total = jnp.zeros((4 * owners, slots), f32)
    slot_iota = lax.broadcasted_iota(i32, (slots, samples), 0)
    at_hi = lax.shift_right_logical(at, 7).astype(f32)
    at_lo = (at & 127).astype(f32)
    blocks = samples // 128
    for t in range(tables):
        mine = hot[t * owners : (t + 1) * owners, :].astype(f32)
        before = cum[t * owners : (t + 1) * owners, :] + base
        rank = jnp.sum(mine * before, axis=0, keepdims=True).astype(i32)
        base = before[:, samples - 1 :] + mine[:, samples - 1 :]
        local = (place[t : t + 1, :] - frequent) & (owned - 1)
        parts = [
            mine * (at_hi + float((t + 1) * blocks)),
            mine * at_lo,
            mine * (lax.shift_right_logical(local, 7) + 1).astype(f32),
            mine * (local & 127).astype(f32),
        ]
        left = jnp.concatenate(parts, axis=0).astype(bf16)
        total = total + dot_nt(left, one_hot(slot_iota == rank))
    idx[...] = (total[:owners] * 128.0 + total[owners : 2 * owners]).astype(i32)
    row = (total[2 * owners : 3 * owners] - 1.0) * 128.0 + total[3 * owners :]
    row_a[...] = row[:, :128]
    row_b[...] = row[:, 128:]


def front_kernel(
    frequent, owned, place, bias, cross_hbm, cot_hbm, down_hbm, up_hbm,
    hidden, back_low, values_hbm, bucket_hbm,
    cross, cot, down, up, values, bucket, hot, cum, idx_v, row_a, row_b, idx, h_acc, b_acc, in_sems, v_sems, b_sems, i_sem,
):
    samples = hidden.shape[0]
    emb = values.shape[1]
    pieces = in_sems.shape[0]
    steps = v_sems.shape[0]
    wide = cross.shape[1] // steps
    thin = cross.shape[1] // pieces
    per = wide // emb
    owners = bucket.shape[0]
    slots = bucket.shape[1] - 8

    def loads(g):
        cols = pl.ds(pl.multiple_of(g * thin, 128), thin)
        return [
            pltpu.make_async_copy(cross_hbm.at[:, cols], cross.at[:, cols], in_sems.at[g, 0]),
            pltpu.make_async_copy(cot_hbm.at[:, cols], cot.at[:, cols], in_sems.at[g, 1]),
            pltpu.make_async_copy(down_hbm.at[cols, :], down.at[cols, :], in_sems.at[g, 2]),
            pltpu.make_async_copy(up_hbm.at[:, cols], up.at[:, cols], in_sems.at[g, 3]),
        ]

    for g in range(pieces):
        for c in loads(g):
            c.start()
    index_work(frequent, owned, place, idx_v, row_a, row_b, hot, cum)
    to_scalar = pltpu.make_async_copy(idx_v, idx, i_sem)
    to_scalar.start()
    h_acc[...] = jnp.zeros_like(h_acc)
    b_acc[...] = jnp.zeros_like(b_acc)

    def low(g, _):
        for n in range(pieces // steps):
            for c in loads(g * (pieces // steps) + n):
                c.wait()
        cols = pl.ds(pl.multiple_of(g * wide, wide), wide)
        x = cross[:, cols]
        inner = (cot[:, cols].astype(f32) * x.astype(f32)).astype(bf16)
        h_acc[...] += jnp.dot(x, down[cols, :], preferred_element_type=f32)
        b_acc[...] += dot_nt(inner, up[:, cols])
        return 0

    lax.fori_loop(0, steps, low, 0)
    hidden[...] = h_acc[...].astype(bf16)
    back_low[...] = b_acc[...].astype(bf16)

    def store(g):
        part = pl.ds(pl.multiple_of(g * per * samples, 128), per * samples)
        return pltpu.make_async_copy(values.at[part], values_hbm.at[part], v_sems.at[g])

    def high(g, _):
        cols = pl.ds(pl.multiple_of(g * wide, wide), wide)
        scaled = jnp.dot(hidden[...], up[:, cols], preferred_element_type=f32) + bias[cols].reshape(1, wide)
        v = cot[:, cols].astype(f32) * (scaled + 1.0) + dot_nt(back_low[...], down[cols, :])
        for k in range(per):
            values[pl.ds(pl.multiple_of((g * per + k) * samples, 128), samples), :] = v[:, k * emb : (k + 1) * emb]
        store(g).start()
        return 0

    lax.fori_loop(0, steps, high, 0)
    to_scalar.wait()

    def ship(o):
        return pltpu.make_async_copy(bucket.at[o], bucket_hbm.at[o], b_sems.at[o])

    def pick(o, _):
        for k in range(slots):
            src = idx[o, k]
            bucket[o, k : k + 1, :] = values[pl.ds(src, 1), :]
        bucket[o, slots : slots + 8, :] = jnp.zeros((8, emb), f32)
        bucket[o, slots : slots + 1, :] = row_a[pl.ds(o, 1), :]
        bucket[o, slots + 1 : slots + 2, :] = row_b[pl.ds(o, 1), :]
        ship(o).start()
        return 0

    lax.fori_loop(0, owners, pick, 0)
    lax.fori_loop(0, steps, lambda g, _: (store(g).wait(), 0)[1], 0)
    lax.fori_loop(0, owners, lambda o, _: (ship(o).wait(), 0)[1], 0)


PORT = (
    (72, 40, 24, "xzy"),
    (112, 32, 16, "xzy"),
    (144, 40, 24, "zxy"),
    (184, 40, 24, "zxy"),
    (0, 40, 24, "yxz"),
    (40, 32, 16, "yzx"),
)
N_BULK = 4


def mesh_place():
    dp, y = lax.axis_index("dp"), lax.axis_index("rep")
    core = dp % 2
    return {"x": dp // 8, "z": (dp // 2) % 4, "y": y}, core, (dp + 1 - 2 * core, y)


def sender(send_sems, recv_sems, sent):
    used = [0]

    def send(src, dst, to):
        k = used[0]
        used[0] += 1
        copy = pltpu.make_async_remote_copy(
            src_ref=src, dst_ref=dst, send_sem=send_sems.at[k], recv_sem=recv_sems.at[k],
            device_id=to, device_id_type=pl.DeviceIdType.MESH,
        )
        copy.start()
        sent.append(copy)
        return copy

    return send


class Reduce:
    def __init__(self, send, near, at, add, rows, half, lands):
        self.send, self.near, self.at, self.add = send, near, at, add
        self.rows, self.half, self.lands = rows, half, lands

    def start(self):
        (_, up, far, down), to = self.near
        self.c0 = self.send(self.at(far, 0, self.half), self.lands[0], to[up])
        self.c1 = self.send(self.at(far, self.half, self.rows), self.lands[1], to[down])

    def middle(self):
        (_, up, far, down), to = self.near
        self.c0.wait_recv()
        self.add(up, 0, self.half, self.lands[:1])
        self.c2 = self.send(self.at(up, 0, self.rows), self.lands[2], to[up])
        self.c1.wait_recv()
        self.add(down, self.half, self.rows, self.lands[1:2])
        self.c3 = self.send(self.at(down, 0, self.rows), self.lands[3], to[down])

    def finish(self):
        self.c2.wait_recv()
        self.c3.wait_recv()
        self.add(self.near[0][0], 0, self.rows, self.lands[2:4])


class Direct:
    def __init__(self, send, near, at, add, lands):
        self.send, self.near, self.at, self.add, self.lands = send, near, at, add, lands

    def start(self):
        places, to = self.near
        self.got = [self.send(self.at(places[d]), self.lands[d - 1], to[places[d]]) for d in (1, 3, 2)]

    def finish(self):
        for c in self.got:
            c.wait_recv()
        self.add(self.near[0][0], self.lands)


class Spread:
    def __init__(self, send, near, at):
        self.send, self.near, self.at = send, near, at

    def start(self):
        places, to = self.near
        src = self.at(places[0])
        self.got = [self.send(src, src, to[places[d]]) for d in (1, 3, 2)]

    def finish(self):
        for c in self.got:
            c.wait_recv()


class Ids:
    def __init__(self, make):
        self.make = make

    def __getitem__(self, t):
        return self.make(t)


def neighbours(me, core, axis):
    def device(to):
        at = dict(me, **{axis: to})
        return ((at["x"] * 4 + at["z"]) * 2 + core, at["y"])

    return [(me[axis] + d) % 4 for d in range(4)], Ids(device)


def greet(peers):
    barrier = pltpu.get_barrier_semaphore()
    for peer in peers:
        pl.semaphore_signal(barrier, inc=1, device_id=peer, device_id_type=pl.DeviceIdType.MESH)
    pl.semaphore_wait(barrier, len(peers))


def weights_kernel(steps, hidden, back_low, cross, cot, values_hbm, place_in, *rest):
    outs, rest = rest[: len(PORT)], rest[len(PORT) :]
    freq_out, rest = rest[0], rest[1:]
    pair, rest = rest[: len(PORT)], rest[len(PORT) :]
    y_land, rest = [rest[:4], rest[4:8]], rest[8:]
    f_both, f_pair, f_land, rest = rest[0], rest[1], rest[2:5], rest[5:]
    both, freq, hidden_t, down, up, bias, values, place, send_sems, recv_sems, local_sems = rest
    g = pl.program_id(0)
    rank = hidden.shape[1]
    wide = cross.shape[1]
    per = wide // 128
    frequent = freq.shape[0]
    samples = hidden.shape[0]
    count = frequent // 8
    width = wide * steps
    cols = per * steps
    up_rows = rank // count
    down_rows = width // count
    base = up_rows * cols
    bias_at = base + down_rows * rank // 128
    me, core, partner = mesh_place()
    near = neighbours(me, core, "y")
    load = pltpu.make_async_copy(values_hbm, values, local_sems.at[0])

    @pl.when(g == 0)
    def _():
        greet([partner] + [near[1][t] for t in near[0][1:]])
        load.start()
        hidden_t[...] = hidden[...].T
        for t in range(place.shape[0]):
            place[t] = place_in[t : t + 1, :]
        freq[...] = jnp.zeros_like(freq)

    inner = cot[...].astype(f32) * cross[...].astype(f32)
    bias[:, pl.ds(pl.multiple_of(g * wide, wide), wide)] = jnp.sum(inner, axis=0, keepdims=True)
    u = jnp.dot(hidden_t[...], inner.astype(bf16), preferred_element_type=f32)
    for k in range(per):
        up[k * rank : (k + 1) * rank, :] = u[:, k * 128 : (k + 1) * 128]
    d = dot_tn(cross[...], back_low[...])
    for k in range(rank // 128):
        down[pl.ds(pl.multiple_of(k * width + g * wide, 128), wide), :] = d[:, k * 128 : (k + 1) * 128]

    def put_up(n, _):
        for c in range(2):
            for y in range(4):
                i = n * 8 + c * 4 + y
                for k in range(per):
                    both[n, c, y, pl.ds(g * per + k, up_rows, stride=cols), :] = up[
                        pl.ds(k * rank + i * up_rows, up_rows), :
                    ]
        return 0

    lax.fori_loop(0, count // 8, put_up, 0)

    @pl.when(g == steps - 1)
    def _():
        sent = []
        send = sender(send_sems, recv_sems, sent)

        def part(p, c):
            first, rows = PORT[p][0], PORT[p][1]
            return both.at[:, c, :, pl.ds(first, rows), :]

        firsts = range(N_BULK, len(PORT))
        got = {p: send(part(p, 1 - core), pair[p], partner) for p in firsts}

        def put_down(n, _):
            for c in range(2):
                for y in range(4):
                    i = n * 8 + c * 4 + y
                    for k in range(rank // 128):
                        both[n, c, y, pl.ds(base + k, down_rows, stride=rank // 128), :] = down[
                            pl.ds(k * width + i * down_rows, down_rows), :
                        ]
                    both[n, c, y, bias_at : bias_at + 8, :] = jnp.zeros((8, 128), f32)
            return 0

        lax.fori_loop(0, count // 8, put_down, 0)
        for i in range(count):
            both[i // 8, (i // 4) % 2, i % 4, bias_at : bias_at + 1, 0:down_rows] = bias[
                :, i * down_rows : (i + 1) * down_rows
            ]
        for p in range(N_BULK):
            got[p] = send(part(p, 1 - core), pair[p], partner)
        load.wait()
        row_iota = lax.broadcasted_iota(i32, (frequent, samples), 0)

        def tables(t, _):
            hots, parts = [], []
            for k in range(2):
                hots.append(one_hot(row_iota == place[2 * t + k]))
                parts.append(hi_lo(values[pl.ds(pl.multiple_of((2 * t + k + 1) * samples, 128), samples), :]))
            s = jnp.dot(jnp.concatenate(hots, axis=1), jnp.concatenate(parts, axis=0), preferred_element_type=f32)
            freq[...] += s[:, :128] + s[:, 128:]
            return 0

        def add_pair(p):
            first, rows = PORT[p][0], PORT[p][1]
            got[p].wait_recv()

            def add(n, _):
                for y in range(4):
                    both[n, core, y, first : first + rows, :] = (
                        both[n, core, y, first : first + rows, :] + pair[p][n, y]
                    )
                return 0

            lax.fori_loop(0, count // 8, add, 0)

        def y_phase(p):
            first, rows, half, _ = PORT[p]

            def at(t, lo, hi):
                return both.at[:, core, t, pl.ds(first + lo, hi - lo), :]

            def y_add(t, lo, hi, lands):
                def add(n, _):
                    v = both[n, core, t, first + lo : first + hi, :]
                    for ref in lands:
                        v = v + ref[n]
                    both[n, core, t, first + lo : first + hi, :] = v
                    return 0

                lax.fori_loop(0, count // 8, add, 0)

            return Reduce(send, near, at, y_add, rows, half, y_land[p - N_BULK])

        def f_add(t, lands):
            v = f_both[:, core, t]
            for ref in lands:
                v = v + ref[...]
            f_both[:, core, t] = v

        y_sums = {p: y_phase(p) for p in firsts}
        f_sum = Direct(send, near, lambda t: f_both.at[:, core, t], f_add, f_land)
        pairs = place.shape[0] // 2
        lax.fori_loop(0, 2, tables, 0)
        for p in firsts:
            add_pair(p)
            y_sums[p].start()
        lax.fori_loop(2, pairs // 2 + 2, tables, 0)
        y_sums[N_BULK].middle()
        lax.fori_loop(pairs // 2 + 2, pairs, tables, 0)
        y_sums[N_BULK + 1].middle()

        def put_freq(n, _):
            for c in range(2):
                for y in range(4):
                    f_both[n, c, y] = freq[pl.ds(pl.multiple_of((n * 8 + c * 4 + y) * 8, 8), 8), :]
            return 0

        lax.fori_loop(0, count // 8, put_freq, 0)
        f_got = send(f_both.at[:, 1 - core], f_pair, partner)
        stores = []
        for p in range(N_BULK):
            add_pair(p)
            stores.append(pltpu.make_async_copy(part(p, core), outs[p], local_sems.at[1 + p]))
            stores[-1].start()
        f_got.wait_recv()
        f_both[:, core] = f_both[:, core] + f_pair[...]
        f_sum.start()
        for p in firsts:
            y_sums[p].finish()
            stores.append(pltpu.make_async_copy(y_sums[p].at(me["y"], 0, PORT[p][1]), outs[p], local_sems.at[1 + p]))
            stores[-1].start()
        f_sum.finish()
        stores.append(pltpu.make_async_copy(f_both.at[:, core, me["y"]], freq_out, local_sems.at[1 + len(PORT)]))
        stores[-1].start()
        for c in stores:
            c.wait()
        for c in sent:
            c.wait_send()


def params(**kw):
    return pltpu.CompilerParams(vmem_limit_bytes=VLIM, **kw)


def reduce_kernel(*refs):
    it = iter(refs)
    take = lambda n: [next(it) for _ in range(n)]
    pieces = range(len(PORT))
    begins = [1 if PORT[p][3][0] == "y" else 0 for p in pieces]
    loads, (load_f, arrived), given = take(len(PORT)), take(2), take(4)
    new_f, new_fa, new_s, new_sa, g_up, g_down, g_bias = take(7)
    work = take(len(PORT))
    land = {p: {k: take(4) for k in range(begins[p], 3)} for p in pieces}
    swork, sland, sgath = next(it), [take(4), take(4)], next(it)
    f_work, fx_land, fz_land, gath = next(it), take(3), take(3), next(it)
    mine, arr, ids, right, acc = take(5)
    f_table, f_accum, s_table, s_accum = held = take(4)
    send_sems, recv_sems, local_sems = take(3)
    me, core, partner = mesh_place()
    near = {a: neighbours(me, core, a) for a in "xzy"}
    greet([partner] + [near[a][1][t] for a in "xzy" for t in near[a][0][1:]])
    sent = []
    send = sender(send_sems, recv_sems, sent)

    def where(dims, done, axis, t, rem=None):
        rem = iter(rem) if rem is not None else None
        out = []
        for a in dims:
            if a in done:
                out.append(me[a])
            elif a == axis:
                out.append(t)
            else:
                out.append(slice(None) if rem is None else next(rem))
        return tuple(out)

    def phase(p, k):
        _, rows, half, order = PORT[p]
        dims = "xz" if begins[p] else "xzy"
        done, axis = order[begins[p] : k], order[k]
        ref, left = work[p], 2 - k

        def at(t, lo, hi):
            return ref.at[where(dims, done, axis, t) + (pl.ds(lo, hi - lo), slice(None))]

        def add(t, lo, hi, lands):
            def one(rem):
                spot = where(dims, done, axis, t, rem) + (slice(lo, hi), slice(None))
                v = ref[spot]
                for x in lands:
                    v = v + x[rem + (slice(None), slice(None))]
                ref[spot] = v

            if left == 0:
                one(())
            elif left == 1:
                lax.fori_loop(0, 4, lambda i, _: (one((i,)), 0)[1], 0)
            else:
                lax.fori_loop(0, 16, lambda i, _: (one((i // 4, i % 4)), 0)[1], 0)

        return Reduce(send, near[axis], at, add, rows, half, land[p][k])

    sums = {(p, k): phase(p, k) for p in pieces for k in range(begins[p], 3)}

    owned = swork.shape[1]

    part = owned // 2

    def s_phase(h):
        def at(t, lo, hi):
            return swork.at[t, pl.ds(h * part + lo, hi - lo), :]

        def add(t, lo, hi, lands):
            for r in range(lo, hi, 128):
                v = swork[t, h * part + r : h * part + r + 128, :]
                for ref in lands:
                    v = v + ref[r - lo : r - lo + 128, :]
                swork[t, h * part + r : h * part + r + 128, :] = v

        return Reduce(send, near["y"], at, add, part, part // 2, sland[h])

    s_red = [s_phase(0), s_phase(1)]

    def f_add(spot, lands):
        v = f_work[spot]
        for ref in lands:
            v = v + ref[...]
        f_work[spot] = v

    f_x = Direct(send, near["x"], lambda t: f_work.at[t], lambda t, l: f_add((t,), l), fx_land)
    f_z = Direct(
        send, near["z"], lambda t: f_work.at[me["x"], t], lambda t, l: f_add((me["x"], t), l), fz_land
    )
    g_z = Spread(send, near["z"], lambda t: gath.at[me["x"], t, core, me["y"]])
    g_x = Spread(send, near["x"], lambda t: gath.at[t, :, core, me["y"]])
    g_y = Spread(send, near["y"], lambda t: gath.at[:, :, core, t])

    class SegGather:
        def __init__(self, h):
            self.first = h * part

        def at(self, t, lo, hi):
            return sgath.at[t, pl.ds(self.first + lo, hi - lo), :]

        def start(self):
            (here, up, far, down), to = near["y"]
            spot = (here, slice(self.first, self.first + part), slice(None))
            sgath[spot] = swork[spot]
            src = self.at(here, 0, part)
            self.c0, self.c1 = send(src, src, to[up]), send(src, src, to[down])

        def middle(self):
            (here, up, far, down), to = near["y"]
            self.c0.wait_recv()
            src = self.at(down, 0, part // 2)
            self.c2 = send(src, src, to[up])
            self.c1.wait_recv()
            src = self.at(up, part // 2, part)
            self.c3 = send(src, src, to[down])

        def finish(self):
            self.c2.wait_recv()
            self.c3.wait_recv()

    s_gat = [SegGather(0), SegGather(1)]
    copies = [pltpu.make_async_copy(loads[p], work[p], local_sems.at[p]) for p in pieces]
    more = [(load_f, f_work), (arrived, arr)] + list(zip(given, held))
    copy_f, copy_a, *rest = [
        pltpu.make_async_copy(a, b, local_sems.at[len(PORT) + i]) for i, (a, b) in enumerate(more)
    ]
    for c in [copy_f, copies[0], copies[2], copies[1], copies[3], copy_a, copies[4], copies[5]] + rest:
        c.start()
    slots = arr.shape[1] - 8
    some = ids.shape[0]
    each_of = arr.shape[0] // some
    chunk = each_of * slots

    def prepare(g, _):
        rows = []
        for b in range(each_of):
            n = g * each_of + b
            rows.append(arr[n, slots : slots + 1, :])
            rows.append(arr[n, slots + 1 : slots + 2, : slots - 128])
            right[pl.ds(pl.multiple_of(n * slots, 16), slots), :] = hi_lo(arr[n, :slots, :])
        ids[g] = jnp.concatenate(rows, axis=1).astype(i32)
        return 0

    def seg_block(t):
        acc[...] = jnp.zeros_like(acc)
        first = t * owned

        def one(g, _):
            hot = one_hot(lax.broadcasted_iota(i32, (owned, chunk), 0) + first == ids[g])
            acc[...] += jnp.dot(
                hot, right[pl.ds(pl.multiple_of(g * chunk, 16), chunk), :], preferred_element_type=f32
            )
            return 0

        lax.fori_loop(0, some, one, 0)
        swork[t] = acc[:, :128] + acc[:, 128:]

    _, y_up, y_far, y_down = near["y"][0]
    def done(p, k):
        sums[p, k].finish()
        if k < 2:
            sums[p, k + 1].start()

    copy_f.wait()
    f_x.start()
    for p in (0, 2, 1, 3):
        copies[p].wait()
        sums[p, 0].start()
    copy_a.wait()
    lax.fori_loop(0, some, prepare, 0)
    f_x.finish()
    f_z.start()
    seg_block(y_far)
    s_red[0].start()
    s_red[1].start()
    sums[0, 0].middle()
    sums[2, 0].middle()
    seg_block(y_up)
    sums[1, 0].middle()
    sums[3, 0].middle()
    for p in (4, 5):
        copies[p].wait()
        sums[p, 1].start()
    seg_block(y_down)
    s_red[0].middle()
    s_red[1].middle()
    f_z.finish()
    gath[me["x"], me["z"], core, me["y"]] = f_work[me["x"], me["z"]]
    g_z.start()
    seg_block(me["y"])
    done(0, 0)
    done(2, 0)
    s_red[0].finish()
    s_gat[0].start()
    s_red[1].finish()
    s_gat[1].start()
    done(1, 0)
    done(3, 0)
    sums[4, 1].middle()
    sums[5, 1].middle()
    g_z.finish()
    g_x.start()
    sums[0, 1].middle()
    sums[2, 1].middle()
    s_gat[0].middle()
    s_gat[1].middle()
    done(4, 1)
    done(5, 1)
    sums[1, 1].middle()
    sums[3, 1].middle()
    g_x.finish()
    g_y.start()
    done(0, 1)
    done(2, 1)
    done(1, 1)
    done(3, 1)
    for c in rest:
        c.wait()
    s_gat[0].finish()
    s_gat[1].finish()
    row_adagrad(s_table, s_accum, lambda n: sgath[n // 4, pl.ds(pl.multiple_of(n % 4 * 128, 128), 128), :], new_s, new_sa)
    sums[4, 2].middle()
    sums[5, 2].middle()
    g_y.finish()
    g_c = send(gath.at[:, :, core], gath.at[:, :, core], partner)
    for p in (0, 2, 1, 3):
        sums[p, 2].middle()
    g_c.wait_recv()
    row_adagrad(f_table, f_accum, lambda n: gath[n // 2, pl.ds(n % 2 * 2, 2)].reshape(128, 128), new_f, new_fa)
    here = (me["x"], me["z"], me["y"])
    for p in (4, 5, 0, 2, 1, 3):
        sums[p, 2].finish()
        first, rows = PORT[p][:2]
        mine[first : first + rows, :] = work[p][here[:2] if begins[p] else here]
    up_rows, down_rows = g_up.shape[0], g_down.shape[0]
    cols = g_up.shape[1] // 128
    for c in range(cols):
        g_up[:, c * 128 : (c + 1) * 128] = mine[pl.ds(c, up_rows, stride=cols), :]
    first, cols = up_rows * cols, g_down.shape[1] // 128
    for c in range(cols):
        g_down[:, c * 128 : (c + 1) * 128] = mine[pl.ds(first + c, down_rows, stride=cols), :]
    g_bias[...] = mine[first + down_rows * cols : first + down_rows * cols + 1, 0:down_rows]
    for c in sent:
        c.wait_send()


def reduce_scratch(owned, frequent, arrived):
    v = lambda *s: pltpu.VMEM(s, f32)
    begins = [1 if order[0] == "y" else 0 for _, _, _, order in PORT]
    out = [v(*(4,) * (3 - b), r, 128) for b, (_, r, _, _) in zip(begins, PORT)]
    for b, (_, r, h, _) in zip(begins, PORT):
        for k in range(b, 3):
            lead = (4,) * (2 - k)
            out += [v(*lead, h, 128), v(*lead, r - h, 128), v(*lead, r, 128), v(*lead, r, 128)]
    q = owned // 4
    out += [v(4, q, 128)] + [v(q // 4, 128), v(q // 4, 128), v(q // 2, 128), v(q // 2, 128)] * 2 + [v(4, q, 128)]
    out += [v(4, 4, 8, 128)] + [v(4, 8, 128)] * 3 + [v(8, 128)] * 3 + [v(4, 4, 2, 4, 8, 128)]
    n = arrived.shape[0] // 4
    flat = arrived.shape[0] * (arrived.shape[1] - 8)
    out += [v(max(a + r for a, r, _, _ in PORT), 128)]
    out += [v(*arrived.shape), pltpu.VMEM((n, 1, flat // n), i32), pltpu.VMEM((flat, 256), bf16), v(q, 256)]
    out += [v(frequent, 128), v(frequent // 128, 128), v(owned, 128), v(owned // 128, 128)]
    out += [pltpu.SemaphoreType.DMA((112,)), pltpu.SemaphoreType.DMA((112,)), pltpu.SemaphoreType.DMA((16,))]
    return out


def reduce_all(parts, arrived, f_table, f_accum, s_table, s_accum, count, width, rank):
    vmem = pl.BlockSpec(memory_space=pltpu.VMEM)
    anyw = pl.BlockSpec(memory_space=pl.ANY)
    frequent, owned = f_table.shape[0], s_table.shape[0]
    given = [f_table, f_accum.reshape(-1, 128), s_table, s_accum.reshape(-1, 128)]
    shapes = [g.shape for g in given] + [(rank // count, width), (width // count, rank), (1, width // count)]
    shapes = [jax.ShapeDtypeStruct(shape, f32) for shape in shapes]
    outs = pl.pallas_call(
        reduce_kernel,
        out_shape=tuple(shapes),
        in_specs=[anyw] * (len(PORT) + 6),
        out_specs=(vmem,) * 7,
        scratch_shapes=reduce_scratch(owned, frequent, arrived),
        compiler_params=params(collective_id=0, has_side_effects=True),
        name="reduce_kernel",
    )(*[w.reshape(4, 4, *w.shape[1:]) for w in parts], arrived, *given)
    return pl.pallas_call(
        move_kernel,
        out_shape=tuple(shapes),
        in_specs=[anyw] * 7,
        out_specs=(anyw,) * 7,
        scratch_shapes=[pltpu.VMEM(x.shape, f32) for x in shapes] + [pltpu.SemaphoreType.DMA((2, 7))],
        compiler_params=params(),
        name="move_kernel",
    )(*outs)


def body(cross_in, cotangent, weight_down, weight_up, cross_bias, row_place, frequent_table, frequent_accum, shard_table, shard_accum):
    samples, width = cross_in.shape
    rank = weight_down.shape[1]
    tables = row_place.shape[1]
    emb = frequent_table.shape[1]
    f_count = frequent_table.shape[0]
    owned = shard_table.shape[0]
    shards = lax.axis_size("dp")
    count = shards * lax.axis_size("rep")
    capacity = samples * tables // (2 * shards)
    blocks = width // emb
    per = 3
    steps = blocks // per
    wide = per * emb
    vmem = pl.BlockSpec(memory_space=pltpu.VMEM)

    place_t = row_place.T
    anyw = pl.BlockSpec(memory_space=pl.ANY)
    hidden, back_low, values, bucket = pl.pallas_call(
        functools.partial(front_kernel, f_count, owned),
        out_shape=(
            jax.ShapeDtypeStruct((samples, rank), bf16),
            jax.ShapeDtypeStruct((samples, rank), bf16),
            jax.ShapeDtypeStruct((blocks * samples, emb), f32),
            jax.ShapeDtypeStruct((shards, capacity + 8, emb), f32),
        ),
        in_specs=[vmem, vmem, anyw, anyw, anyw, anyw],
        out_specs=(vmem, vmem, anyw, anyw),
        scratch_shapes=[
            pltpu.VMEM((samples, width), bf16),
            pltpu.VMEM((samples, width), bf16),
            pltpu.VMEM((width, rank), bf16),
            pltpu.VMEM((rank, width), bf16),
            pltpu.VMEM((blocks * samples, emb), f32),
            pltpu.VMEM((shards, capacity + 8, emb), f32),
            pltpu.VMEM((tables * shards, samples), bf16),
            pltpu.VMEM((tables * shards, samples), f32),
            pltpu.VMEM((shards, 256), i32),
            pltpu.VMEM((shards, 128), f32),
            pltpu.VMEM((shards, 128), f32),
            pltpu.SMEM((shards, 256), i32),
            pltpu.VMEM((samples, rank), f32),
            pltpu.VMEM((samples, rank), f32),
            pltpu.SemaphoreType.DMA((steps, 4)),
            pltpu.SemaphoreType.DMA((3,)),
            pltpu.SemaphoreType.DMA((shards,)),
            pltpu.SemaphoreType.DMA,
        ],
        compiler_params=params(),
        name="front_kernel",
    )(place_t, cross_bias, cross_in, cotangent, weight_down, weight_up)

    arrived = lax.all_to_all(bucket, "dp", split_axis=0, concat_axis=0, tiled=True)

    parts = pl.pallas_call(
        functools.partial(weights_kernel, steps),
        grid=(steps,),
        out_shape=tuple(
            jax.ShapeDtypeStruct(shape, f32)
            for shape in [(16, 4, r, 128) for _, r, _, _ in PORT[:N_BULK]]
            + [(16, r, 128) for _, r, _, _ in PORT[N_BULK:]]
            + [(16, 8, 128)]
        ),
        in_specs=[
            pl.BlockSpec((samples, rank), lambda g: (0, 0)),
            pl.BlockSpec((samples, rank), lambda g: (0, 0)),
            pl.BlockSpec((samples, wide), lambda g: (0, g)),
            pl.BlockSpec((samples, wide), lambda g: (0, g)),
            anyw,
            pl.BlockSpec((tables, samples), lambda g: (0, 0)),
        ],
        out_specs=(anyw,) * (len(PORT) + 1),
        scratch_shapes=[pltpu.VMEM((16, 4, r, 128), f32) for _, r, _, _ in PORT]
        + [pltpu.VMEM((16, n, 128), f32) for _, r, h, _ in PORT[N_BULK:] for n in (h, r - h, r, r)]
        + [pltpu.VMEM((16, 2, 4, 8, 128), f32), pltpu.VMEM((16, 4, 8, 128), f32)]
        + [pltpu.VMEM((16, 8, 128), f32)] * 3
        + [
            pltpu.VMEM((16, 2, 4, max(a + r for a, r, _, _ in PORT), 128), f32),
            pltpu.VMEM((f_count, emb), f32),
            pltpu.VMEM((rank, samples), bf16),
            pltpu.VMEM((rank // 128 * width, 128), f32),
            pltpu.VMEM((per * rank, 128), f32),
            pltpu.VMEM((1, width), f32),
            pltpu.VMEM((blocks * samples, emb), f32),
            pltpu.VMEM((tables, 1, samples), i32),
            pltpu.SemaphoreType.DMA((24,)),
            pltpu.SemaphoreType.DMA((24,)),
            pltpu.SemaphoreType.DMA((16,)),
        ],
        compiler_params=params(collective_id=1, has_side_effects=True),
        name="weights_kernel",
    )(hidden, back_low, cross_in, cotangent, values, place_t)

    new_frequent, new_frequent_accum, new_shard, new_shard_accum, grad_up, grad_down, grad_bias = reduce_all(
        parts, arrived, frequent_table, frequent_accum, shard_table, shard_accum, count, width, rank
    )
    new_frequent_accum, new_shard_accum = new_frequent_accum.reshape(-1), new_shard_accum.reshape(-1)
    grad_bias = grad_bias.reshape(-1)
    return (new_frequent, new_frequent_accum, new_shard, new_shard_accum, grad_up, grad_down, grad_bias)


def solution(mesh):
    both = ("dp", "rep")
    in_specs = (P(both, None), P(both, None), P(), P(), P(), P(both, None), P(), P(), P("dp", None), P("dp"))
    out_specs = (P(), P(), P("dp", None), P("dp"), P(both, None), P(both, None), P(both))
    return jax.shard_map(body, mesh=mesh, in_specs=in_specs, out_specs=out_specs, check_vma=False)
```

```python
import functools
import jax
import jax.numpy as jnp
from jax import lax
from jax.experimental import pallas as pl
from jax.experimental.pallas import tpu as pltpu
from jax.sharding import PartitionSpec as P

learn_rate = 0.05
eps_ada = 1e-08
f32, bf16, i32 = jnp.float32, jnp.bfloat16, jnp.int32
VLIM = 66 * 1000 * 1000


def row_adagrad(table, accum, grad_of, new, new_accum):
    def chunk(n, _):
        at = pl.ds(pl.multiple_of(n * 128, 128), 128)
        g = grad_of(n)
        before = jnp.broadcast_to(accum[pl.ds(n, 1), :], (128, 128)).T
        after = before + jnp.mean(g * g, axis=1, keepdims=True)
        new[at, :] = table[at, :] - learn_rate * g / (jnp.sqrt(after) + eps_ada)
        new_accum[pl.ds(n, 1), :] = after.T[0:1, :]
        return 0

    lax.fori_loop(0, table.shape[0] // 128, chunk, 0)


def move_kernel(*refs):
    n = len(refs) // 3
    src, dst, held, sems = refs[:n], refs[n : 2 * n], refs[2 * n : 3 * n], refs[3 * n]
    takes = [pltpu.make_async_copy(a, b, sems.at[0, i]) for i, (a, b) in enumerate(zip(src, held))]
    gives = [pltpu.make_async_copy(a, b, sems.at[1, i]) for i, (a, b) in enumerate(zip(held, dst))]
    for c in takes:
        c.start()
    for c, d in zip(takes, gives):
        c.wait()
        d.start()
    for d in gives:
        d.wait()


def dot_nt(a, b):
    return lax.dot_general(a, b, (((1,), (1,)), ((), ())), preferred_element_type=f32)


def dot_tn(a, b):
    return lax.dot_general(a, b, (((0,), (0,)), ((), ())), preferred_element_type=f32)


def hi_lo(v):
    hi = v.astype(bf16)
    lo = (v - hi.astype(f32)).astype(bf16)
    return jnp.concatenate([hi, lo], axis=1)


def one_hot(flags):
    return jnp.where(flags, 1.0, 0.0).astype(bf16)


def index_work(frequent, owned, place, idx, row_a, row_b, hot, cum):
    tables, samples = place.shape
    owners, slots = idx.shape
    at = lax.broadcasted_iota(i32, (1, samples), 1)
    owner_iota = lax.broadcasted_iota(i32, (owners, samples), 0)
    tri = one_hot(
        lax.broadcasted_iota(i32, (samples, samples), 0)
        < lax.broadcasted_iota(i32, (samples, samples), 1)
    )
    shift = owned.bit_length() - 1
    for t in range(tables):
        owner = lax.shift_right_arithmetic(place[t : t + 1, :] - frequent, shift)
        hot[t * owners : (t + 1) * owners, :] = one_hot(owner_iota == owner)
    cum[...] = jnp.dot(hot[...], tri, preferred_element_type=f32)
    base = jnp.zeros((owners, 1), f32)
    total = jnp.zeros((4 * owners, slots), f32)
    slot_iota = lax.broadcasted_iota(i32, (slots, samples), 0)
    at_hi = lax.shift_right_logical(at, 7).astype(f32)
    at_lo = (at & 127).astype(f32)
    blocks = samples // 128
    for t in range(tables):
        mine = hot[t * owners : (t + 1) * owners, :].astype(f32)
        before = cum[t * owners : (t + 1) * owners, :] + base
        rank = jnp.sum(mine * before, axis=0, keepdims=True).astype(i32)
        base = before[:, samples - 1 :] + mine[:, samples - 1 :]
        local = (place[t : t + 1, :] - frequent) & (owned - 1)
        parts = [
            mine * (at_hi + float((t + 1) * blocks)),
            mine * at_lo,
            mine * (lax.shift_right_logical(local, 7) + 1).astype(f32),
            mine * (local & 127).astype(f32),
        ]
        left = jnp.concatenate(parts, axis=0).astype(bf16)
        total = total + dot_nt(left, one_hot(slot_iota == rank))
    idx[...] = (total[:owners] * 128.0 + total[owners : 2 * owners]).astype(i32)
    row = (total[2 * owners : 3 * owners] - 1.0) * 128.0 + total[3 * owners :]
    row_a[...] = row[:, :128]
    row_b[...] = row[:, 128:]


def front_kernel(
    frequent, owned, place, bias, cross_hbm, cot_hbm, down_hbm, up_hbm,
    hidden, back_low, values_hbm, bucket_hbm,
    cross, cot, down, up, values, bucket, hot, cum, idx_v, row_a, row_b, idx, h_acc, b_acc, in_sems, v_sems, b_sems, i_sem,
):
    samples = hidden.shape[0]
    emb = values.shape[1]
    pieces = in_sems.shape[0]
    steps = v_sems.shape[0]
    wide = cross.shape[1] // steps
    thin = cross.shape[1] // pieces
    per = wide // emb
    owners = bucket.shape[0]
    slots = bucket.shape[1] - 8

    def loads(g):
        cols = pl.ds(pl.multiple_of(g * thin, 128), thin)
        return [
            pltpu.make_async_copy(cross_hbm.at[:, cols], cross.at[:, cols], in_sems.at[g, 0]),
            pltpu.make_async_copy(cot_hbm.at[:, cols], cot.at[:, cols], in_sems.at[g, 1]),
            pltpu.make_async_copy(down_hbm.at[cols, :], down.at[cols, :], in_sems.at[g, 2]),
            pltpu.make_async_copy(up_hbm.at[:, cols], up.at[:, cols], in_sems.at[g, 3]),
        ]

    for g in range(pieces):
        for c in loads(g):
            c.start()
    index_work(frequent, owned, place, idx_v, row_a, row_b, hot, cum)
    to_scalar = pltpu.make_async_copy(idx_v, idx, i_sem)
    to_scalar.start()
    h_acc[...] = jnp.zeros_like(h_acc)
    b_acc[...] = jnp.zeros_like(b_acc)

    def low(g, _):
        for n in range(pieces // steps):
            for c in loads(g * (pieces // steps) + n):
                c.wait()
        cols = pl.ds(pl.multiple_of(g * wide, wide), wide)
        x = cross[:, cols]
        inner = (cot[:, cols].astype(f32) * x.astype(f32)).astype(bf16)
        h_acc[...] += jnp.dot(x, down[cols, :], preferred_element_type=f32)
        b_acc[...] += dot_nt(inner, up[:, cols])
        return 0

    lax.fori_loop(0, steps, low, 0)
    hidden[...] = h_acc[...].astype(bf16)
    back_low[...] = b_acc[...].astype(bf16)

    def store(g):
        part = pl.ds(pl.multiple_of(g * per * samples, 128), per * samples)
        return pltpu.make_async_copy(values.at[part], values_hbm.at[part], v_sems.at[g])

    def high(g, _):
        cols = pl.ds(pl.multiple_of(g * wide, wide), wide)
        scaled = jnp.dot(hidden[...], up[:, cols], preferred_element_type=f32) + bias[cols].reshape(1, wide)
        v = cot[:, cols].astype(f32) * (scaled + 1.0) + dot_nt(back_low[...], down[cols, :])
        for k in range(per):
            values[pl.ds(pl.multiple_of((g * per + k) * samples, 128), samples), :] = v[:, k * emb : (k + 1) * emb]
        store(g).start()
        return 0

    lax.fori_loop(0, steps, high, 0)
    to_scalar.wait()

    def ship(o):
        return pltpu.make_async_copy(bucket.at[o], bucket_hbm.at[o], b_sems.at[o])

    def pick(o, _):
        for k in range(slots):
            src = idx[o, k]
            bucket[o, k : k + 1, :] = values[pl.ds(src, 1), :]
        bucket[o, slots : slots + 8, :] = jnp.zeros((8, emb), f32)
        bucket[o, slots : slots + 1, :] = row_a[pl.ds(o, 1), :]
        bucket[o, slots + 1 : slots + 2, :] = row_b[pl.ds(o, 1), :]
        ship(o).start()
        return 0

    lax.fori_loop(0, owners, pick, 0)
    lax.fori_loop(0, steps, lambda g, _: (store(g).wait(), 0)[1], 0)
    lax.fori_loop(0, owners, lambda o, _: (ship(o).wait(), 0)[1], 0)


PORT = (
    (128, 24, 16, "xzy"),
    (152, 24, 16, "xzy"),
    (176, 24, 16, "zxy"),
    (200, 24, 16, "zxy"),
    (96, 32, 16, "yxz"),
    (0, 48, 24, "yxz"),
    (48, 48, 24, "yzx"),
)
N_BULK = 5
BEGINS = [1 if p >= N_BULK else 0 for p in range(len(PORT))]


def mesh_place():
    dp, y = lax.axis_index("dp"), lax.axis_index("rep")
    core = dp % 2
    return {"x": dp // 8, "z": (dp // 2) % 4, "y": y}, core, (dp + 1 - 2 * core, y)


class Links:
    def __init__(self, send_sems, recv_sems):
        self.sems, self.used, self.sent = (send_sems, recv_sems), 0, []

    def base(self, n):
        self.used += n
        return self.used - n

    def make(self, k, src, dst, to):
        return pltpu.make_async_remote_copy(
            src_ref=src, dst_ref=dst, send_sem=self.sems[0].at[k], recv_sem=self.sems[1].at[k],
            device_id=to, device_id_type=pl.DeviceIdType.MESH,
        )

    def go(self, k, src, dst, to):
        copy = self.make(k, src(), dst, to())
        copy.start()
        self.sent.append(lambda: self.make(k, src(), dst, to()))
        return copy

    def __call__(self, src, dst, to):
        return self.go(self.base(1), lambda: src, dst, lambda: to)


class Reduce:
    def __init__(self, links, near, at, add, rows, half, lands):
        (_, up, far, down), to = near
        self.links, self.here, self.up, self.down = links, near[0][0], up, down
        self.at, self.add, self.rows, self.half, self.lands = at, add, rows, half, lands
        k = links.base(4)
        self.args = [
            (k, lambda: at(far, 0, half), lands[0], lambda: to[up]),
            (k + 1, lambda: at(far, half, rows), lands[1], lambda: to[down]),
            (k + 2, lambda: at(up, 0, rows), lands[2], lambda: to[up]),
            (k + 3, lambda: at(down, 0, rows), lands[3], lambda: to[down]),
        ]

    def go(self, i):
        k, src, dst, to = self.args[i]
        self.links.go(k, src, dst, to)

    def got(self, i):
        k, src, dst, to = self.args[i]
        self.links.make(k, src(), dst, to()).wait_recv()

    def start(self):
        self.go(0)
        self.go(1)

    def middle(self):
        self.got(0)
        self.add(self.up, 0, self.half, self.lands[:1])
        self.go(2)
        self.got(1)
        self.add(self.down, self.half, self.rows, self.lands[1:2])
        self.go(3)

    def finish(self):
        self.got(2)
        self.got(3)
        self.add(self.here, 0, self.rows, self.lands[2:4])


class Direct:
    def __init__(self, send, near, at, add, lands):
        self.send, self.near, self.at, self.add, self.lands = send, near, at, add, lands

    def start(self):
        places, to = self.near
        self.got = [self.send(self.at(places[d]), self.lands[d - 1], to[places[d]]) for d in (1, 3, 2)]

    def finish(self):
        for c in self.got:
            c.wait_recv()
        self.add(self.near[0][0], self.lands)


class Spread:
    def __init__(self, send, near, at):
        self.send, self.near, self.at = send, near, at

    def start(self):
        places, to = self.near
        src = self.at(places[0])
        self.got = [self.send(src, src, to[places[d]]) for d in (1, 3, 2)]

    def finish(self):
        for c in self.got:
            c.wait_recv()


class Ids:
    def __init__(self, make):
        self.make = make

    def __getitem__(self, t):
        return self.make(t)


def neighbours(me, core, axis):
    def device(to):
        at = dict(me, **{axis: to})
        return ((at["x"] * 4 + at["z"]) * 2 + core, at["y"])

    return [(me[axis] + d) % 4 for d in range(4)], Ids(device)


def greet(peers):
    barrier = pltpu.get_barrier_semaphore()
    for peer in peers:
        pl.semaphore_signal(barrier, inc=1, device_id=peer, device_id_type=pl.DeviceIdType.MESH)
    pl.semaphore_wait(barrier, len(peers))


def weights_kernel(steps, hidden, back_low, cross, cot, values_hbm, place_in, *rest):
    outs, rest = rest[: len(PORT)], rest[len(PORT) :]
    freq_out, rest = rest[0], rest[1:]
    pair, rest = rest[: len(PORT)], rest[len(PORT) :]
    y_land, rest = [rest[:4], rest[4:8]], rest[8:]
    f_both, f_pair, f_land, rest = rest[0], rest[1], rest[2:5], rest[5:]
    both, freq, hidden_t, down, up, bias, values, place, send_sems, recv_sems, local_sems = rest
    g = pl.program_id(0)
    rank = hidden.shape[1]
    wide = cross.shape[1]
    per = wide // 128
    frequent = freq.shape[0]
    samples = hidden.shape[0]
    count = frequent // 8
    width = wide * steps
    cols = per * steps
    up_rows = rank // count
    down_rows = width // count
    base = up_rows * cols
    bias_at = base + down_rows * rank // 128
    me, core, partner = mesh_place()
    near = neighbours(me, core, "y")
    load = pltpu.make_async_copy(values_hbm, values, local_sems.at[0])

    send = Links(send_sems, recv_sems)
    firsts = range(N_BULK, len(PORT))

    def part(p, c):
        first, rows = PORT[p][0], PORT[p][1]
        return both.at[:, c, :, pl.ds(first, rows), :]

    pair_base = send.base(len(PORT))
    pair_args = lambda p: (pair_base + p, lambda: part(p, 1 - core), pair[p], lambda: partner)

    def add_pair(p):
        first, rows = PORT[p][0], PORT[p][1]
        k, src, dst, to = pair_args(p)
        send.make(k, src(), dst, to()).wait_recv()

        def add(n, _):
            for y in range(4):
                both[n, core, y, first : first + rows, :] = both[n, core, y, first : first + rows, :] + pair[p][n, y]
            return 0

        lax.fori_loop(0, count // 8, add, 0)

    def y_phase(p):
        first, rows, half, _ = PORT[p]

        def at(t, lo, hi):
            return both.at[:, core, t, pl.ds(first + lo, hi - lo), :]

        def y_add(t, lo, hi, lands):
            def add(n, _):
                v = both[n, core, t, first + lo : first + hi, :]
                for ref in lands:
                    v = v + ref[n]
                both[n, core, t, first + lo : first + hi, :] = v
                return 0

            lax.fori_loop(0, count // 8, add, 0)

        return Reduce(send, near, at, y_add, rows, half, y_land[p - N_BULK])

    y_sums = {p: y_phase(p) for p in firsts}

    @pl.when(g == 0)
    def _():
        greet([partner] + [near[1][t] for t in near[0][1:]])
        load.start()
        hidden_t[...] = hidden[...].T
        for t in range(place.shape[0]):
            place[t] = place_in[t : t + 1, :]
        freq[...] = jnp.zeros_like(freq)

    @pl.when(g < steps)
    def _():
        inner = cot[...].astype(f32) * cross[...].astype(f32)
        bias[:, pl.ds(pl.multiple_of(g * wide, wide), wide)] = jnp.sum(inner, axis=0, keepdims=True)
        u = jnp.dot(hidden_t[...], inner.astype(bf16), preferred_element_type=f32)
        for k in range(per):
            up[k * rank : (k + 1) * rank, :] = u[:, k * 128 : (k + 1) * 128]

        def put_up(n, _):
            for c in range(2):
                for y in range(4):
                    i = n * 8 + c * 4 + y
                    for k in range(per):
                        both[n, c, y, pl.ds(g * per + k, up_rows, stride=cols), :] = up[
                            pl.ds(k * rank + i * up_rows, up_rows), :
                        ]
            return 0

        lax.fori_loop(0, count // 8, put_up, 0)

    @pl.when(g == steps)
    def _():
        for p in firsts:
            send.go(*pair_args(p))

    @pl.when(g >= steps)
    def _():
        d = dot_tn(cross[...], back_low[...])
        for k in range(rank // 128):
            down[pl.ds(pl.multiple_of(k * width + (g - steps) * wide, 128), wide), :] = d[:, k * 128 : (k + 1) * 128]

    @pl.when(g == 2 * steps - 2)
    def _():
        for p in firsts:
            add_pair(p)
            y_sums[p].start()

    @pl.when(g == 2 * steps - 1)
    def _():
        def put_down(n, _):
            for c in range(2):
                for y in range(4):
                    i = n * 8 + c * 4 + y
                    for k in range(rank // 128):
                        both[n, c, y, pl.ds(base + k, down_rows, stride=rank // 128), :] = down[
                            pl.ds(k * width + i * down_rows, down_rows), :
                        ]
                    both[n, c, y, bias_at : bias_at + 8, :] = jnp.zeros((8, 128), f32)
            return 0

        lax.fori_loop(0, count // 8, put_down, 0)
        for i in range(count):
            both[i // 8, (i // 4) % 2, i % 4, bias_at : bias_at + 1, 0:down_rows] = bias[
                :, i * down_rows : (i + 1) * down_rows
            ]
        for p in range(N_BULK):
            send.go(*pair_args(p))
        y_sums[N_BULK].middle()
        load.wait()
        row_iota = lax.broadcasted_iota(i32, (frequent, samples), 0)

        def tables(t, _):
            hots, parts = [], []
            for k in range(2):
                hots.append(one_hot(row_iota == place[2 * t + k]))
                parts.append(hi_lo(values[pl.ds(pl.multiple_of((2 * t + k + 1) * samples, 128), samples), :]))
            s = jnp.dot(jnp.concatenate(hots, axis=1), jnp.concatenate(parts, axis=0), preferred_element_type=f32)
            freq[...] += s[:, :128] + s[:, 128:]
            return 0

        def f_add(t, lands):
            v = f_both[:, core, t]
            for ref in lands:
                v = v + ref[...]
            f_both[:, core, t] = v

        f_sum = Direct(send, near, lambda t: f_both.at[:, core, t], f_add, f_land)
        pairs = place.shape[0] // 2
        lax.fori_loop(0, pairs // 3, tables, 0)
        y_sums[N_BULK + 1].middle()
        lax.fori_loop(pairs // 3, pairs, tables, 0)

        def put_freq(n, _):
            for c in range(2):
                for y in range(4):
                    f_both[n, c, y] = freq[pl.ds(pl.multiple_of((n * 8 + c * 4 + y) * 8, 8), 8), :]
            return 0

        lax.fori_loop(0, count // 8, put_freq, 0)
        f_got = send(f_both.at[:, 1 - core], f_pair, partner)
        stores = []
        for p in range(N_BULK):
            add_pair(p)
            stores.append(pltpu.make_async_copy(part(p, core), outs[p], local_sems.at[1 + p]))
            stores[-1].start()
        f_got.wait_recv()
        f_both[:, core] = f_both[:, core] + f_pair[...]
        f_sum.start()
        for p in firsts:
            y_sums[p].finish()
            stores.append(pltpu.make_async_copy(y_sums[p].at(me["y"], 0, PORT[p][1]), outs[p], local_sems.at[1 + p]))
            stores[-1].start()
        f_sum.finish()
        stores.append(pltpu.make_async_copy(f_both.at[:, core, me["y"]], freq_out, local_sems.at[1 + len(PORT)]))
        stores[-1].start()
        for c in stores:
            c.wait()
        for c in send.sent:
            c().wait_send()


def params(**kw):
    return pltpu.CompilerParams(vmem_limit_bytes=VLIM, **kw)


def reduce_kernel(*refs):
    it = iter(refs)
    take = lambda n: [next(it) for _ in range(n)]
    pieces = range(len(PORT))
    begins = BEGINS
    loads, (load_f, arrived), given = take(len(PORT)), take(2), take(4)
    new_f, new_fa, new_s, new_sa, g_up, g_down, g_bias = take(7)
    work = take(len(PORT))
    land = {p: {k: take(3 if k == 2 else 4) for k in range(begins[p], 3)} for p in pieces}
    swork, sland, sgath = next(it), [take(4), take(4)], next(it)
    f_work, fx_land, fz_land, gath = next(it), take(3), take(3), next(it)
    mine, arr, ids, right, acc = take(5)
    f_table, f_accum, s_table, s_accum = held = take(4)
    send_sems, recv_sems, local_sems = take(3)
    me, core, partner = mesh_place()
    near = {a: neighbours(me, core, a) for a in "xzy"}
    greet([partner] + [near[a][1][t] for a in "xzy" for t in near[a][0][1:]])
    send = Links(send_sems, recv_sems)

    def where(dims, done, axis, t, rem=None):
        rem = iter(rem) if rem is not None else None
        out = []
        for a in dims:
            if a in done:
                out.append(me[a])
            elif a == axis:
                out.append(t)
            else:
                out.append(slice(None) if rem is None else next(rem))
        return tuple(out)

    def phase(p, k):
        _, rows, half, order = PORT[p]
        dims = "xz" if begins[p] else "xzy"
        done, axis = order[begins[p] : k], order[k]
        ref, left = work[p], 2 - k

        def at(t, lo, hi):
            return ref.at[where(dims, done, axis, t) + (pl.ds(lo, hi - lo), slice(None))]

        def add(t, lo, hi, lands):
            def one(rem):
                spot = where(dims, done, axis, t, rem) + (slice(lo, hi), slice(None))
                v = ref[spot]
                for x in lands:
                    v = v + x[rem + (slice(None), slice(None))]
                ref[spot] = v

            if left == 0:
                one(())
            elif left == 1:
                lax.fori_loop(0, 4, lambda i, _: (one((i,)), 0)[1], 0)
            else:
                lax.fori_loop(0, 16, lambda i, _: (one((i // 4, i % 4)), 0)[1], 0)

        if k == 2:
            whole = lambda t: at(t, 0, rows)
            return Direct(send, near[axis], whole, lambda t, lands: add(t, 0, rows, lands), land[p][k])
        return Reduce(send, near[axis], at, add, rows, half, land[p][k])

    sums = {(p, k): phase(p, k) for p in pieces for k in range(begins[p], 3)}

    owned = swork.shape[1]

    part = owned // 2

    def s_phase(h):
        def at(t, lo, hi):
            return swork.at[t, pl.ds(h * part + lo, hi - lo), :]

        def add(t, lo, hi, lands):
            for r in range(lo, hi, 128):
                v = swork[t, h * part + r : h * part + r + 128, :]
                for ref in lands:
                    v = v + ref[r - lo : r - lo + 128, :]
                swork[t, h * part + r : h * part + r + 128, :] = v

        return Reduce(send, near["y"], at, add, part, part // 2, sland[h])

    s_red = [s_phase(0), s_phase(1)]

    def f_add(spot, lands):
        v = f_work[spot]
        for ref in lands:
            v = v + ref[...]
        f_work[spot] = v

    f_x = Direct(send, near["x"], lambda t: f_work.at[t], lambda t, l: f_add((t,), l), fx_land)
    f_z = Direct(
        send, near["z"], lambda t: f_work.at[me["x"], t], lambda t, l: f_add((me["x"], t), l), fz_land
    )
    g_z = Spread(send, near["z"], lambda t: gath.at[me["x"], t, core, me["y"]])
    g_x = Spread(send, near["x"], lambda t: gath.at[t, :, core, me["y"]])
    g_y = Spread(send, near["y"], lambda t: gath.at[:, :, core, t])

    class SegGather:
        def __init__(self, h):
            self.first = h * part

        def at(self, t, lo, hi):
            return sgath.at[t, pl.ds(self.first + lo, hi - lo), :]

        def start(self):
            (here, up, far, down), to = near["y"]
            spot = (here, slice(self.first, self.first + part), slice(None))
            sgath[spot] = swork[spot]
            src = self.at(here, 0, part)
            self.c0, self.c1 = send(src, src, to[up]), send(src, src, to[down])

        def middle(self):
            (here, up, far, down), to = near["y"]
            self.c0.wait_recv()
            src = self.at(down, 0, part // 2)
            self.c2 = send(src, src, to[up])
            self.c1.wait_recv()
            src = self.at(up, part // 2, part)
            self.c3 = send(src, src, to[down])

        def finish(self):
            self.c2.wait_recv()
            self.c3.wait_recv()

    s_gat = [SegGather(0), SegGather(1)]
    copies = [pltpu.make_async_copy(loads[p], work[p], local_sems.at[p]) for p in pieces]
    more = [(load_f, f_work), (arrived, arr)] + list(zip(given, held))
    copy_f, copy_a, *rest = [
        pltpu.make_async_copy(a, b, local_sems.at[len(PORT) + i]) for i, (a, b) in enumerate(more)
    ]
    for c in [copy_f, copies[0], copies[2], copies[4], copies[1], copies[3], copy_a, copies[5], copies[6]] + rest:
        c.start()
    slots = arr.shape[1] - 8
    some = ids.shape[0]
    each_of = arr.shape[0] // some
    chunk = each_of * slots

    def prepare(g, _):
        rows = []
        for b in range(each_of):
            n = g * each_of + b
            rows.append(arr[n, slots : slots + 1, :])
            rows.append(arr[n, slots + 1 : slots + 2, : slots - 128])
            right[pl.ds(pl.multiple_of(n * slots, 16), slots), :] = hi_lo(arr[n, :slots, :])
        ids[g] = jnp.concatenate(rows, axis=1).astype(i32)
        return 0

    def seg_block(t):
        acc[...] = jnp.zeros_like(acc)
        first = t * owned

        def one(g, _):
            hot = one_hot(lax.broadcasted_iota(i32, (owned, chunk), 0) + first == ids[g])
            acc[...] += jnp.dot(
                hot, right[pl.ds(pl.multiple_of(g * chunk, 16), chunk), :], preferred_element_type=f32
            )
            return 0

        lax.fori_loop(0, some, one, 0)
        swork[t] = acc[:, :128] + acc[:, 128:]

    _, y_up, y_far, y_down = near["y"][0]
    def done(p, k):
        sums[p, k].finish()
        if k < 2:
            sums[p, k + 1].start()

    copy_f.wait()
    f_x.start()
    for p in (0, 2, 4, 1, 3):
        copies[p].wait()
        sums[p, 0].start()
    copy_a.wait()
    lax.fori_loop(0, some, prepare, 0)
    f_x.finish()
    f_z.start()
    sums[4, 0].middle()
    seg_block(y_far)
    s_red[0].start()
    s_red[1].start()
    sums[0, 0].middle()
    sums[2, 0].middle()
    sums[1, 0].middle()
    sums[3, 0].middle()
    for p in (5, 6):
        copies[p].wait()
        sums[p, 1].start()
    seg_block(y_up)
    f_z.finish()
    gath[me["x"], me["z"], core, me["y"]] = f_work[me["x"], me["z"]]
    g_z.start()
    seg_block(y_down)
    s_red[0].middle()
    s_red[1].middle()
    done(4, 0)
    seg_block(me["y"])
    done(0, 0)
    done(2, 0)
    done(1, 0)
    done(3, 0)
    sums[5, 1].middle()
    sums[6, 1].middle()
    s_red[0].finish()
    s_gat[0].start()
    s_red[1].finish()
    s_gat[1].start()
    g_z.finish()
    g_x.start()
    for p in (4, 0, 2, 1, 3):
        sums[p, 1].middle()
    s_gat[0].middle()
    s_gat[1].middle()
    done(5, 1)
    done(6, 1)
    g_x.finish()
    g_y.start()
    for p in (4, 0, 2, 1, 3):
        done(p, 1)
    for c in rest:
        c.wait()
    s_gat[0].finish()
    s_gat[1].finish()
    row_adagrad(s_table, s_accum, lambda n: sgath[n // 4, pl.ds(pl.multiple_of(n % 4 * 128, 128), 128), :], new_s, new_sa)
    g_y.finish()
    g_c = send(gath.at[:, :, core], gath.at[:, :, core], partner)
    here = (me["x"], me["z"], me["y"])
    for p in (5, 6, 4, 0, 2, 1, 3):
        sums[p, 2].finish()
        first, rows = PORT[p][:2]
        mine[first : first + rows, :] = work[p][here[:2] if begins[p] else here]
    g_c.wait_recv()
    row_adagrad(f_table, f_accum, lambda n: gath[n // 2, pl.ds(n % 2 * 2, 2)].reshape(128, 128), new_f, new_fa)
    up_rows, down_rows = g_up.shape[0], g_down.shape[0]
    cols = g_up.shape[1] // 128
    for c in range(cols):
        g_up[:, c * 128 : (c + 1) * 128] = mine[pl.ds(c, up_rows, stride=cols), :]
    first, cols = up_rows * cols, g_down.shape[1] // 128
    for c in range(cols):
        g_down[:, c * 128 : (c + 1) * 128] = mine[pl.ds(first + c, down_rows, stride=cols), :]
    g_bias[...] = mine[first + down_rows * cols : first + down_rows * cols + 1, 0:down_rows]
    for c in send.sent:
        c().wait_send()


def reduce_scratch(owned, frequent, arrived):
    v = lambda *s: pltpu.VMEM(s, f32)
    begins = BEGINS
    out = [v(*(4,) * (3 - b), r, 128) for b, (_, r, _, _) in zip(begins, PORT)]
    for b, (_, r, h, _) in zip(begins, PORT):
        for k in range(b, 3):
            lead = (4,) * (2 - k)
            out += [v(*lead, n, 128) for n in ((r, r, r) if k == 2 else (h, r - h, r, r))]
    q = owned // 4
    out += [v(4, q, 128)] + [v(q // 4, 128), v(q // 4, 128), v(q // 2, 128), v(q // 2, 128)] * 2 + [v(4, q, 128)]
    out += [v(4, 4, 8, 128)] + [v(4, 8, 128)] * 3 + [v(8, 128)] * 3 + [v(4, 4, 2, 4, 8, 128)]
    n = arrived.shape[0] // 4
    flat = arrived.shape[0] * (arrived.shape[1] - 8)
    out += [v(max(a + r for a, r, _, _ in PORT), 128)]
    out += [v(*arrived.shape), pltpu.VMEM((n, 1, flat // n), i32), pltpu.VMEM((flat, 256), bf16), v(q, 256)]
    out += [v(frequent, 128), v(frequent // 128, 128), v(owned, 128), v(owned // 128, 128)]
    out += [pltpu.SemaphoreType.DMA((112,)), pltpu.SemaphoreType.DMA((112,)), pltpu.SemaphoreType.DMA((16,))]
    return out


def reduce_all(parts, arrived, f_table, f_accum, s_table, s_accum, count, width, rank):
    vmem = pl.BlockSpec(memory_space=pltpu.VMEM)
    anyw = pl.BlockSpec(memory_space=pl.ANY)
    frequent, owned = f_table.shape[0], s_table.shape[0]
    given = [f_table, f_accum.reshape(-1, 128), s_table, s_accum.reshape(-1, 128)]
    shapes = [g.shape for g in given] + [(rank // count, width), (width // count, rank), (1, width // count)]
    shapes = [jax.ShapeDtypeStruct(shape, f32) for shape in shapes]
    outs = pl.pallas_call(
        reduce_kernel,
        out_shape=tuple(shapes),
        in_specs=[anyw] * (len(PORT) + 6),
        out_specs=(vmem,) * 7,
        scratch_shapes=reduce_scratch(owned, frequent, arrived),
        compiler_params=params(collective_id=0, has_side_effects=True),
        name="reduce_kernel",
    )(*[w.reshape(4, 4, *w.shape[1:]) for w in parts], arrived, *given)
    return pl.pallas_call(
        move_kernel,
        out_shape=tuple(shapes),
        in_specs=[anyw] * 7,
        out_specs=(anyw,) * 7,
        scratch_shapes=[pltpu.VMEM(x.shape, f32) for x in shapes] + [pltpu.SemaphoreType.DMA((2, 7))],
        compiler_params=params(),
        name="move_kernel",
    )(*outs)


def body(cross_in, cotangent, weight_down, weight_up, cross_bias, row_place, frequent_table, frequent_accum, shard_table, shard_accum):
    samples, width = cross_in.shape
    rank = weight_down.shape[1]
    tables = row_place.shape[1]
    emb = frequent_table.shape[1]
    f_count = frequent_table.shape[0]
    owned = shard_table.shape[0]
    shards = lax.axis_size("dp")
    count = shards * lax.axis_size("rep")
    capacity = samples * tables // (2 * shards)
    blocks = width // emb
    per = 3
    steps = blocks // per
    wide = per * emb
    vmem = pl.BlockSpec(memory_space=pltpu.VMEM)

    place_t = row_place.T
    anyw = pl.BlockSpec(memory_space=pl.ANY)
    hidden, back_low, values, bucket = pl.pallas_call(
        functools.partial(front_kernel, f_count, owned),
        out_shape=(
            jax.ShapeDtypeStruct((samples, rank), bf16),
            jax.ShapeDtypeStruct((samples, rank), bf16),
            jax.ShapeDtypeStruct((blocks * samples, emb), f32),
            jax.ShapeDtypeStruct((shards, capacity + 8, emb), f32),
        ),
        in_specs=[vmem, vmem, anyw, anyw, anyw, anyw],
        out_specs=(vmem, vmem, anyw, anyw),
        scratch_shapes=[
            pltpu.VMEM((samples, width), bf16),
            pltpu.VMEM((samples, width), bf16),
            pltpu.VMEM((width, rank), bf16),
            pltpu.VMEM((rank, width), bf16),
            pltpu.VMEM((blocks * samples, emb), f32),
            pltpu.VMEM((shards, capacity + 8, emb), f32),
            pltpu.VMEM((tables * shards, samples), bf16),
            pltpu.VMEM((tables * shards, samples), f32),
            pltpu.VMEM((shards, 256), i32),
            pltpu.VMEM((shards, 128), f32),
            pltpu.VMEM((shards, 128), f32),
            pltpu.SMEM((shards, 256), i32),
            pltpu.VMEM((samples, rank), f32),
            pltpu.VMEM((samples, rank), f32),
            pltpu.SemaphoreType.DMA((steps, 4)),
            pltpu.SemaphoreType.DMA((3,)),
            pltpu.SemaphoreType.DMA((shards,)),
            pltpu.SemaphoreType.DMA,
        ],
        compiler_params=params(),
        name="front_kernel",
    )(place_t, cross_bias, cross_in, cotangent, weight_down, weight_up)

    arrived = lax.all_to_all(bucket, "dp", split_axis=0, concat_axis=0, tiled=True)

    parts = pl.pallas_call(
        functools.partial(weights_kernel, steps),
        grid=(2 * steps,),
        out_shape=tuple(
            jax.ShapeDtypeStruct(shape, f32)
            for shape in [(16, 4, r, 128) for _, r, _, _ in PORT[:N_BULK]]
            + [(16, r, 128) for _, r, _, _ in PORT[N_BULK:]]
            + [(16, 8, 128)]
        ),
        in_specs=[
            pl.BlockSpec((samples, rank), lambda g: (0, 0)),
            pl.BlockSpec((samples, rank), lambda g: (0, 0)),
            pl.BlockSpec((samples, wide), lambda g: (0, lax.rem(g, steps))),
            pl.BlockSpec((samples, wide), lambda g: (0, jnp.minimum(g, steps - 1))),
            anyw,
            pl.BlockSpec((tables, samples), lambda g: (0, 0)),
        ],
        out_specs=(anyw,) * (len(PORT) + 1),
        scratch_shapes=[pltpu.VMEM((16, 4, r, 128), f32) for _, r, _, _ in PORT]
        + [pltpu.VMEM((16, n, 128), f32) for _, r, h, _ in PORT[N_BULK:] for n in (h, r - h, r, r)]
        + [pltpu.VMEM((16, 2, 4, 8, 128), f32), pltpu.VMEM((16, 4, 8, 128), f32)]
        + [pltpu.VMEM((16, 8, 128), f32)] * 3
        + [
            pltpu.VMEM((16, 2, 4, max(a + r for a, r, _, _ in PORT), 128), f32),
            pltpu.VMEM((f_count, emb), f32),
            pltpu.VMEM((rank, samples), bf16),
            pltpu.VMEM((rank // 128 * width, 128), f32),
            pltpu.VMEM((per * rank, 128), f32),
            pltpu.VMEM((1, width), f32),
            pltpu.VMEM((blocks * samples, emb), f32),
            pltpu.VMEM((tables, 1, samples), i32),
            pltpu.SemaphoreType.DMA((24,)),
            pltpu.SemaphoreType.DMA((24,)),
            pltpu.SemaphoreType.DMA((16,)),
        ],
        compiler_params=params(collective_id=1, has_side_effects=True),
        name="weights_kernel",
    )(hidden, back_low, cross_in, cotangent, values, place_t)

    new_frequent, new_frequent_accum, new_shard, new_shard_accum, grad_up, grad_down, grad_bias = reduce_all(
        parts, arrived, frequent_table, frequent_accum, shard_table, shard_accum, count, width, rank
    )
    new_frequent_accum, new_shard_accum = new_frequent_accum.reshape(-1), new_shard_accum.reshape(-1)
    grad_bias = grad_bias.reshape(-1)
    return (new_frequent, new_frequent_accum, new_shard, new_shard_accum, grad_up, grad_down, grad_bias)


def solution(mesh):
    both = ("dp", "rep")
    in_specs = (P(both, None), P(both, None), P(), P(), P(), P(both, None), P(), P(), P("dp", None), P("dp"))
    out_specs = (P(), P(), P("dp", None), P("dp"), P(both, None), P(both, None), P(both))
    return jax.shard_map(body, mesh=mesh, in_specs=in_specs, out_specs=out_specs, check_vma=False)
```

```python
import functools
import jax
import jax.numpy as jnp
from jax import lax
from jax.experimental import pallas as pl
from jax.experimental.pallas import tpu as pltpu
from jax.sharding import PartitionSpec as P

learn_rate = 0.05
eps_ada = 1e-08
f32, bf16, i32 = jnp.float32, jnp.bfloat16, jnp.int32
VLIM = 66 * 1000 * 1000


def row_adagrad(table, accum, grad_of, new, new_accum):
    def chunk(n, _):
        at = pl.ds(pl.multiple_of(n * 128, 128), 128)
        g = grad_of(n)
        before = jnp.broadcast_to(accum[pl.ds(n, 1), :], (128, 128)).T
        after = before + jnp.mean(g * g, axis=1, keepdims=True)
        new[at, :] = table[at, :] - learn_rate * g / (jnp.sqrt(after) + eps_ada)
        new_accum[pl.ds(n, 1), :] = after.T[0:1, :]
        return 0

    lax.fori_loop(0, table.shape[0] // 128, chunk, 0)


def move_kernel(*refs):
    n = len(refs) // 3
    src, dst, held, sems = refs[:n], refs[n : 2 * n], refs[2 * n : 3 * n], refs[3 * n]
    takes = [pltpu.make_async_copy(a, b, sems.at[0, i]) for i, (a, b) in enumerate(zip(src, held))]
    gives = [pltpu.make_async_copy(a, b, sems.at[1, i]) for i, (a, b) in enumerate(zip(held, dst))]
    for c in takes:
        c.start()
    for c, d in zip(takes, gives):
        c.wait()
        d.start()
    for d in gives:
        d.wait()


def dot_nt(a, b):
    return lax.dot_general(a, b, (((1,), (1,)), ((), ())), preferred_element_type=f32)


def dot_tn(a, b):
    return lax.dot_general(a, b, (((0,), (0,)), ((), ())), preferred_element_type=f32)


def hi_lo(v):
    hi = v.astype(bf16)
    lo = (v - hi.astype(f32)).astype(bf16)
    return jnp.concatenate([hi, lo], axis=1)


def one_hot(flags):
    return jnp.where(flags, 1.0, 0.0).astype(bf16)


def index_work(frequent, owned, place, idx, row_a, row_b, hot, cum):
    tables, samples = place.shape
    owners, slots = idx.shape
    at = lax.broadcasted_iota(i32, (1, samples), 1)
    owner_iota = lax.broadcasted_iota(i32, (owners, samples), 0)
    tri = one_hot(
        lax.broadcasted_iota(i32, (samples, samples), 0)
        < lax.broadcasted_iota(i32, (samples, samples), 1)
    )
    shift = owned.bit_length() - 1
    for t in range(tables):
        owner = lax.shift_right_arithmetic(place[t : t + 1, :] - frequent, shift)
        hot[t * owners : (t + 1) * owners, :] = one_hot(owner_iota == owner)
    cum[...] = jnp.dot(hot[...], tri, preferred_element_type=f32)
    base = jnp.zeros((owners, 1), f32)
    total = jnp.zeros((4 * owners, slots), f32)
    slot_iota = lax.broadcasted_iota(i32, (slots, samples), 0)
    at_hi = lax.shift_right_logical(at, 7).astype(f32)
    at_lo = (at & 127).astype(f32)
    blocks = samples // 128
    for t in range(tables):
        mine = hot[t * owners : (t + 1) * owners, :].astype(f32)
        before = cum[t * owners : (t + 1) * owners, :] + base
        rank = jnp.sum(mine * before, axis=0, keepdims=True).astype(i32)
        base = before[:, samples - 1 :] + mine[:, samples - 1 :]
        local = (place[t : t + 1, :] - frequent) & (owned - 1)
        parts = [
            mine * (at_hi + float((t + 1) * blocks)),
            mine * at_lo,
            mine * (lax.shift_right_logical(local, 7) + 1).astype(f32),
            mine * (local & 127).astype(f32),
        ]
        left = jnp.concatenate(parts, axis=0).astype(bf16)
        total = total + dot_nt(left, one_hot(slot_iota == rank))
    idx[...] = (total[:owners] * 128.0 + total[owners : 2 * owners]).astype(i32)
    row = (total[2 * owners : 3 * owners] - 1.0) * 128.0 + total[3 * owners :]
    row_a[...] = row[:, :128]
    row_b[...] = row[:, 128:]


def front_kernel(
    frequent, owned, place, bias, cross_hbm, cot_hbm, down_hbm, up_hbm,
    hidden, back_low, values_hbm, bucket_hbm,
    cross, cot, down, up, values, bucket, hot, cum, idx_v, row_a, row_b, idx, h_acc, b_acc, in_sems, v_sems, b_sems, i_sem,
):
    samples = hidden.shape[0]
    emb = values.shape[1]
    pieces = in_sems.shape[0]
    steps = v_sems.shape[0]
    wide = cross.shape[1] // steps
    thin = cross.shape[1] // pieces
    per = wide // emb
    owners = bucket.shape[0]
    slots = bucket.shape[1] - 8

    def loads(g):
        cols = pl.ds(pl.multiple_of(g * thin, 128), thin)
        return [
            pltpu.make_async_copy(cross_hbm.at[:, cols], cross.at[:, cols], in_sems.at[g, 0]),
            pltpu.make_async_copy(cot_hbm.at[:, cols], cot.at[:, cols], in_sems.at[g, 1]),
            pltpu.make_async_copy(down_hbm.at[cols, :], down.at[cols, :], in_sems.at[g, 2]),
            pltpu.make_async_copy(up_hbm.at[:, cols], up.at[:, cols], in_sems.at[g, 3]),
        ]

    for g in range(pieces):
        for c in loads(g):
            c.start()
    index_work(frequent, owned, place, idx_v, row_a, row_b, hot, cum)
    to_scalar = pltpu.make_async_copy(idx_v, idx, i_sem)
    to_scalar.start()
    h_acc[...] = jnp.zeros_like(h_acc)
    b_acc[...] = jnp.zeros_like(b_acc)

    def low(g, _):
        for n in range(pieces // steps):
            for c in loads(g * (pieces // steps) + n):
                c.wait()
        cols = pl.ds(pl.multiple_of(g * wide, wide), wide)
        x = cross[:, cols]
        inner = (cot[:, cols].astype(f32) * x.astype(f32)).astype(bf16)
        h_acc[...] += jnp.dot(x, down[cols, :], preferred_element_type=f32)
        b_acc[...] += dot_nt(inner, up[:, cols])
        return 0

    lax.fori_loop(0, steps, low, 0)
    hidden[...] = h_acc[...].astype(bf16)
    back_low[...] = b_acc[...].astype(bf16)

    def store(g):
        part = pl.ds(pl.multiple_of(g * per * samples, 128), per * samples)
        return pltpu.make_async_copy(values.at[part], values_hbm.at[part], v_sems.at[g])

    def high(g, _):
        cols = pl.ds(pl.multiple_of(g * wide, wide), wide)
        scaled = jnp.dot(hidden[...], up[:, cols], preferred_element_type=f32) + bias[cols].reshape(1, wide)
        v = cot[:, cols].astype(f32) * (scaled + 1.0) + dot_nt(back_low[...], down[cols, :])
        for k in range(per):
            values[pl.ds(pl.multiple_of((g * per + k) * samples, 128), samples), :] = v[:, k * emb : (k + 1) * emb]
        store(g).start()
        return 0

    lax.fori_loop(0, steps, high, 0)
    to_scalar.wait()

    def ship(o):
        return pltpu.make_async_copy(bucket.at[o], bucket_hbm.at[o], b_sems.at[o])

    def pick(o, _):
        for k in range(slots):
            src = idx[o, k]
            bucket[o, k : k + 1, :] = values[pl.ds(src, 1), :]
        bucket[o, slots : slots + 8, :] = jnp.zeros((8, emb), f32)
        bucket[o, slots : slots + 1, :] = row_a[pl.ds(o, 1), :]
        bucket[o, slots + 1 : slots + 2, :] = row_b[pl.ds(o, 1), :]
        ship(o).start()
        return 0

    lax.fori_loop(0, owners, pick, 0)
    lax.fori_loop(0, steps, lambda g, _: (store(g).wait(), 0)[1], 0)
    lax.fori_loop(0, owners, lambda o, _: (ship(o).wait(), 0)[1], 0)


PORT = (
    (104, 32, 16, "xzy"),
    (136, 24, 16, "xzy"),
    (160, 32, 16, "zxy"),
    (192, 32, 16, "zxy"),
    (72, 32, 16, "yxz"),
    (0, 40, 24, "yxz"),
    (40, 32, 16, "yzx"),
)
N_BULK = 5
BEGINS = [1 if p >= N_BULK else 0 for p in range(len(PORT))]


def mesh_place():
    dp, y = lax.axis_index("dp"), lax.axis_index("rep")
    core = dp % 2
    return {"x": dp // 8, "z": (dp // 2) % 4, "y": y}, core, (dp + 1 - 2 * core, y)


class Links:
    def __init__(self, send_sems, recv_sems):
        self.sems, self.used, self.sent = (send_sems, recv_sems), 0, []

    def base(self, n):
        self.used += n
        return self.used - n

    def make(self, k, src, dst, to):
        return pltpu.make_async_remote_copy(
            src_ref=src, dst_ref=dst, send_sem=self.sems[0].at[k], recv_sem=self.sems[1].at[k],
            device_id=to, device_id_type=pl.DeviceIdType.MESH,
        )

    def go(self, k, src, dst, to):
        copy = self.make(k, src(), dst, to())
        copy.start()
        self.sent.append(lambda: self.make(k, src(), dst, to()))
        return copy

    def __call__(self, src, dst, to):
        return self.go(self.base(1), lambda: src, dst, lambda: to)


class Reduce:
    def __init__(self, links, near, at, add, rows, half, lands):
        (_, up, far, down), to = near
        self.links, self.here, self.up, self.down = links, near[0][0], up, down
        self.at, self.add, self.rows, self.half, self.lands = at, add, rows, half, lands
        k = links.base(4)
        self.args = [
            (k, lambda: at(far, 0, half), lands[0], lambda: to[up]),
            (k + 1, lambda: at(far, half, rows), lands[1], lambda: to[down]),
            (k + 2, lambda: at(up, 0, rows), lands[2], lambda: to[up]),
            (k + 3, lambda: at(down, 0, rows), lands[3], lambda: to[down]),
        ]

    def go(self, i):
        k, src, dst, to = self.args[i]
        self.links.go(k, src, dst, to)

    def got(self, i):
        k, src, dst, to = self.args[i]
        self.links.make(k, src(), dst, to()).wait_recv()

    def start(self):
        self.go(0)
        self.go(1)

    def middle(self):
        self.got(0)
        self.add(self.up, 0, self.half, self.lands[:1])
        self.go(2)
        self.got(1)
        self.add(self.down, self.half, self.rows, self.lands[1:2])
        self.go(3)

    def finish(self):
        self.got(2)
        self.got(3)
        self.add(self.here, 0, self.rows, self.lands[2:4])


class Direct:
    def __init__(self, send, near, at, add, lands):
        self.send, self.near, self.at, self.add, self.lands = send, near, at, add, lands

    def start(self):
        places, to = self.near
        self.got = [self.send(self.at(places[d]), self.lands[d - 1], to[places[d]]) for d in (1, 3, 2)]

    def finish(self):
        for c in self.got:
            c.wait_recv()
        self.add(self.near[0][0], self.lands)


class Spread:
    def __init__(self, send, near, at):
        self.send, self.near, self.at = send, near, at

    def start(self):
        places, to = self.near
        src = self.at(places[0])
        self.got = [self.send(src, src, to[places[d]]) for d in (1, 3, 2)]

    def finish(self):
        for c in self.got:
            c.wait_recv()


class Ids:
    def __init__(self, make):
        self.make = make

    def __getitem__(self, t):
        return self.make(t)


def neighbours(me, core, axis):
    def device(to):
        at = dict(me, **{axis: to})
        return ((at["x"] * 4 + at["z"]) * 2 + core, at["y"])

    return [(me[axis] + d) % 4 for d in range(4)], Ids(device)


def greet(peers, meanwhile=lambda: None):
    barrier = pltpu.get_barrier_semaphore()
    for peer in peers:
        pl.semaphore_signal(barrier, inc=1, device_id=peer, device_id_type=pl.DeviceIdType.MESH)
    meanwhile()
    pl.semaphore_wait(barrier, len(peers))


def weights_kernel(steps, hidden, back_low, cross, cot, values_hbm, place_in, *rest):
    outs, rest = rest[: len(PORT)], rest[len(PORT) :]
    freq_out, rest = rest[0], rest[1:]
    pair, rest = rest[: len(PORT)], rest[len(PORT) :]
    y_land, rest = [rest[:4], rest[4:8]], rest[8:]
    f_both, f_pair, f_land, rest = rest[0], rest[1], rest[2:5], rest[5:]
    both, freq, hidden_t, down, up, bias, values, place, send_sems, recv_sems, local_sems = rest
    g = pl.program_id(0)
    rank = hidden.shape[1]
    wide = cross.shape[1]
    per = wide // 128
    frequent = freq.shape[0]
    samples = hidden.shape[0]
    count = frequent // 8
    width = wide * steps
    cols = per * steps
    up_rows = rank // count
    down_rows = width // count
    base = up_rows * cols
    bias_at = base + down_rows * rank // 128
    me, core, partner = mesh_place()
    near = neighbours(me, core, "y")
    load = pltpu.make_async_copy(values_hbm, values, local_sems.at[0])

    send = Links(send_sems, recv_sems)
    firsts = range(N_BULK, len(PORT))

    def part(p, c):
        first, rows = PORT[p][0], PORT[p][1]
        return both.at[:, c, :, pl.ds(first, rows), :]

    pair_base = send.base(len(PORT))
    pair_args = lambda p: (pair_base + p, lambda: part(p, 1 - core), pair[p], lambda: partner)

    def add_pair(p):
        first, rows = PORT[p][0], PORT[p][1]
        k, src, dst, to = pair_args(p)
        send.make(k, src(), dst, to()).wait_recv()

        def add(n, _):
            for y in range(4):
                both[n, core, y, first : first + rows, :] = both[n, core, y, first : first + rows, :] + pair[p][n, y]
            return 0

        lax.fori_loop(0, count // 8, add, 0)

    def y_phase(p):
        first, rows, half, _ = PORT[p]

        def at(t, lo, hi):
            return both.at[:, core, t, pl.ds(first + lo, hi - lo), :]

        def y_add(t, lo, hi, lands):
            def add(n, _):
                v = both[n, core, t, first + lo : first + hi, :]
                for ref in lands:
                    v = v + ref[n]
                both[n, core, t, first + lo : first + hi, :] = v
                return 0

            lax.fori_loop(0, count // 8, add, 0)

        return Reduce(send, near, at, y_add, rows, half, y_land[p - N_BULK])

    y_sums = {p: y_phase(p) for p in firsts}

    @pl.when(g == 0)
    def _():
        greet([partner] + [near[1][t] for t in near[0][1:]])
        load.start()
        hidden_t[...] = hidden[...].T
        for t in range(place.shape[0]):
            place[t] = place_in[t : t + 1, :]
        freq[...] = jnp.zeros_like(freq)

    inner = cot[...].astype(f32) * cross[...].astype(f32)
    bias[:, pl.ds(pl.multiple_of(g * wide, wide), wide)] = jnp.sum(inner, axis=0, keepdims=True)
    u = jnp.dot(hidden_t[...], inner.astype(bf16), preferred_element_type=f32)
    for k in range(per):
        up[k * rank : (k + 1) * rank, :] = u[:, k * 128 : (k + 1) * 128]
    d = dot_tn(cross[...], back_low[...])
    for k in range(rank // 128):
        down[pl.ds(pl.multiple_of(k * width + g * wide, 128), wide), :] = d[:, k * 128 : (k + 1) * 128]

    def put_up(n, _):
        for c in range(2):
            for y in range(4):
                i = n * 8 + c * 4 + y
                for k in range(per):
                    both[n, c, y, pl.ds(g * per + k, up_rows, stride=cols), :] = up[
                        pl.ds(k * rank + i * up_rows, up_rows), :
                    ]
        return 0

    lax.fori_loop(0, count // 8, put_up, 0)

    @pl.when(g == steps - 1)
    def _():
        for p in firsts:
            send.go(*pair_args(p))

        def put_down(n, _):
            for c in range(2):
                for y in range(4):
                    i = n * 8 + c * 4 + y
                    for k in range(rank // 128):
                        both[n, c, y, pl.ds(base + k, down_rows, stride=rank // 128), :] = down[
                            pl.ds(k * width + i * down_rows, down_rows), :
                        ]
                    both[n, c, y, bias_at : bias_at + 8, :] = jnp.zeros((8, 128), f32)
            return 0

        lax.fori_loop(0, count // 8, put_down, 0)
        for i in range(count):
            both[i // 8, (i // 4) % 2, i % 4, bias_at : bias_at + 1, 0:down_rows] = bias[
                :, i * down_rows : (i + 1) * down_rows
            ]
        for p in range(N_BULK):
            send.go(*pair_args(p))
        load.wait()
        row_iota = lax.broadcasted_iota(i32, (frequent, samples), 0)

        def tables(t, _):
            hots, parts = [], []
            for k in range(2):
                hots.append(one_hot(row_iota == place[2 * t + k]))
                parts.append(hi_lo(values[pl.ds(pl.multiple_of((2 * t + k + 1) * samples, 128), samples), :]))
            s = jnp.dot(jnp.concatenate(hots, axis=1), jnp.concatenate(parts, axis=0), preferred_element_type=f32)
            freq[...] += s[:, :128] + s[:, 128:]
            return 0

        def f_add(t, lands):
            v = f_both[:, core, t]
            for ref in lands:
                v = v + ref[...]
            f_both[:, core, t] = v

        f_sum = Direct(send, near, lambda t: f_both.at[:, core, t], f_add, f_land)
        pairs = place.shape[0] // 2
        lax.fori_loop(0, 2, tables, 0)
        for p in firsts:
            add_pair(p)
            y_sums[p].start()
        lax.fori_loop(2, pairs // 2 + 2, tables, 0)
        y_sums[N_BULK].middle()
        lax.fori_loop(pairs // 2 + 2, pairs, tables, 0)
        y_sums[N_BULK + 1].middle()

        def put_freq(n, _):
            for c in range(2):
                for y in range(4):
                    f_both[n, c, y] = freq[pl.ds(pl.multiple_of((n * 8 + c * 4 + y) * 8, 8), 8), :]
            return 0

        lax.fori_loop(0, count // 8, put_freq, 0)
        f_got = send(f_both.at[:, 1 - core], f_pair, partner)
        stores = []
        for p in range(N_BULK):
            add_pair(p)
            stores.append(pltpu.make_async_copy(part(p, core), outs[p], local_sems.at[1 + p]))
            stores[-1].start()
        f_got.wait_recv()
        f_both[:, core] = f_both[:, core] + f_pair[...]
        f_sum.start()
        for p in firsts:
            y_sums[p].finish()
            stores.append(pltpu.make_async_copy(y_sums[p].at(me["y"], 0, PORT[p][1]), outs[p], local_sems.at[1 + p]))
            stores[-1].start()
        f_sum.finish()
        stores.append(pltpu.make_async_copy(f_both.at[:, core, me["y"]], freq_out, local_sems.at[1 + len(PORT)]))
        stores[-1].start()
        for c in stores:
            c.wait()
        for c in send.sent:
            c().wait_send()


def params(**kw):
    return pltpu.CompilerParams(vmem_limit_bytes=VLIM, **kw)


def reduce_kernel(*refs):
    it = iter(refs)
    take = lambda n: [next(it) for _ in range(n)]
    pieces = range(len(PORT))
    begins = BEGINS
    loads, (load_f, arrived), given = take(len(PORT)), take(2), take(4)
    new_f, new_fa, new_s, new_sa, g_up, g_down, g_bias = take(7)
    work = take(len(PORT))
    land = {p: {k: take(3 if k == 2 else 4) for k in range(begins[p], 3)} for p in pieces}
    swork, sland, sgath = next(it), [take(4), take(4)], next(it)
    f_work, fx_land, fz_land, gath = next(it), take(3), take(3), next(it)
    mine, arr, ids, right, acc = take(5)
    f_table, f_accum, s_table, s_accum = held = take(4)
    send_sems, recv_sems, local_sems = take(3)
    me, core, partner = mesh_place()
    near = {a: neighbours(me, core, a) for a in "xzy"}
    copies = [pltpu.make_async_copy(loads[p], work[p], local_sems.at[p]) for p in pieces]
    more = [(load_f, f_work), (arrived, arr)] + list(zip(given, held))
    copy_f, copy_a, *rest = [
        pltpu.make_async_copy(a, b, local_sems.at[len(PORT) + i]) for i, (a, b) in enumerate(more)
    ]

    def load_all():
        for c in [copy_f, copies[0], copies[2], copies[4], copy_a, copies[1], copies[3], copies[5], copies[6]] + rest:
            c.start()

    greet([partner] + [near[a][1][t] for a in "xzy" for t in near[a][0][1:]], load_all)
    send = Links(send_sems, recv_sems)

    def where(dims, done, axis, t, rem=None):
        rem = iter(rem) if rem is not None else None
        out = []
        for a in dims:
            if a in done:
                out.append(me[a])
            elif a == axis:
                out.append(t)
            else:
                out.append(slice(None) if rem is None else next(rem))
        return tuple(out)

    def phase(p, k):
        _, rows, half, order = PORT[p]
        dims = "xz" if begins[p] else "xzy"
        done, axis = order[begins[p] : k], order[k]
        ref, left = work[p], 2 - k

        def at(t, lo, hi):
            return ref.at[where(dims, done, axis, t) + (pl.ds(lo, hi - lo), slice(None))]

        def add(t, lo, hi, lands):
            def one(rem):
                spot = where(dims, done, axis, t, rem) + (slice(lo, hi), slice(None))
                v = ref[spot]
                for x in lands:
                    v = v + x[rem + (slice(None), slice(None))]
                ref[spot] = v

            if left == 0:
                one(())
            elif left == 1:
                lax.fori_loop(0, 4, lambda i, _: (one((i,)), 0)[1], 0)
            else:
                lax.fori_loop(0, 16, lambda i, _: (one((i // 4, i % 4)), 0)[1], 0)

        if k == 2:
            whole = lambda t: at(t, 0, rows)
            return Direct(send, near[axis], whole, lambda t, lands: add(t, 0, rows, lands), land[p][k])
        return Reduce(send, near[axis], at, add, rows, half, land[p][k])

    sums = {(p, k): phase(p, k) for p in pieces for k in range(begins[p], 3)}

    owned = swork.shape[1]

    part = owned // 2

    def s_phase(h):
        def at(t, lo, hi):
            return swork.at[t, pl.ds(h * part + lo, hi - lo), :]

        def add(t, lo, hi, lands):
            for r in range(lo, hi, 128):
                v = swork[t, h * part + r : h * part + r + 128, :]
                for ref in lands:
                    v = v + ref[r - lo : r - lo + 128, :]
                swork[t, h * part + r : h * part + r + 128, :] = v

        return Reduce(send, near["y"], at, add, part, part // 2, sland[h])

    s_red = [s_phase(0), s_phase(1)]

    def f_add(spot, lands):
        v = f_work[spot]
        for ref in lands:
            v = v + ref[...]
        f_work[spot] = v

    f_x = Direct(send, near["x"], lambda t: f_work.at[t], lambda t, l: f_add((t,), l), fx_land)
    f_z = Direct(
        send, near["z"], lambda t: f_work.at[me["x"], t], lambda t, l: f_add((me["x"], t), l), fz_land
    )
    g_z = Spread(send, near["z"], lambda t: gath.at[me["x"], t, core, me["y"]])
    g_x = Spread(send, near["x"], lambda t: gath.at[t, :, core, me["y"]])
    g_y = Spread(send, near["y"], lambda t: gath.at[:, :, core, t])

    class SegGather:
        def __init__(self, h):
            self.first = h * part

        def at(self, t, lo, hi):
            return sgath.at[t, pl.ds(self.first + lo, hi - lo), :]

        def start(self):
            (here, up, far, down), to = near["y"]
            spot = (here, slice(self.first, self.first + part), slice(None))
            sgath[spot] = swork[spot]
            src = self.at(here, 0, part)
            self.c0, self.c1 = send(src, src, to[up]), send(src, src, to[down])

        def middle(self):
            (here, up, far, down), to = near["y"]
            self.c0.wait_recv()
            src = self.at(down, 0, part // 2)
            self.c2 = send(src, src, to[up])
            self.c1.wait_recv()
            src = self.at(up, part // 2, part)
            self.c3 = send(src, src, to[down])

        def finish(self):
            self.c2.wait_recv()
            self.c3.wait_recv()

    s_gat = [SegGather(0), SegGather(1)]
    slots = arr.shape[1] - 8
    some = ids.shape[0]
    each_of = arr.shape[0] // some
    chunk = each_of * slots

    def prepare(g, _):
        rows = []
        for b in range(each_of):
            n = g * each_of + b
            rows.append(arr[n, slots : slots + 1, :])
            rows.append(arr[n, slots + 1 : slots + 2, : slots - 128])
            right[pl.ds(pl.multiple_of(n * slots, 16), slots), :] = hi_lo(arr[n, :slots, :])
        ids[g] = jnp.concatenate(rows, axis=1).astype(i32)
        return 0

    def seg_block(t):
        acc[...] = jnp.zeros_like(acc)
        first = t * owned

        def one(g, _):
            hot = one_hot(lax.broadcasted_iota(i32, (owned, chunk), 0) + first == ids[g])
            acc[...] += jnp.dot(
                hot, right[pl.ds(pl.multiple_of(g * chunk, 16), chunk), :], preferred_element_type=f32
            )
            return 0

        lax.fori_loop(0, some, one, 0)
        swork[t] = acc[:, :128] + acc[:, 128:]

    _, y_up, y_far, y_down = near["y"][0]
    def done(p, k):
        sums[p, k].finish()
        if k < 2:
            sums[p, k + 1].start()

    copy_f.wait()
    f_x.start()
    for p in (0, 2, 4, 1, 3):
        copies[p].wait()
        sums[p, 0].start()
    copy_a.wait()
    lax.fori_loop(0, some, prepare, 0)
    f_x.finish()
    f_z.start()
    sums[4, 0].middle()
    seg_block(y_far)
    s_red[0].start()
    s_red[1].start()
    sums[0, 0].middle()
    sums[2, 0].middle()
    sums[1, 0].middle()
    sums[3, 0].middle()
    for p in (5, 6):
        copies[p].wait()
        sums[p, 1].start()
    seg_block(y_up)
    f_z.finish()
    gath[me["x"], me["z"], core, me["y"]] = f_work[me["x"], me["z"]]
    g_z.start()
    seg_block(y_down)
    s_red[0].middle()
    s_red[1].middle()
    done(4, 0)
    seg_block(me["y"])
    done(0, 0)
    done(2, 0)
    done(1, 0)
    done(3, 0)
    sums[5, 1].middle()
    sums[6, 1].middle()
    s_red[0].finish()
    s_gat[0].start()
    s_red[1].finish()
    s_gat[1].start()
    g_z.finish()
    g_x.start()
    for p in (4, 0, 2, 1, 3):
        sums[p, 1].middle()
    s_gat[0].middle()
    s_gat[1].middle()
    done(5, 1)
    done(6, 1)
    g_x.finish()
    g_y.start()
    for p in (4, 0, 2, 1, 3):
        done(p, 1)
    for c in rest:
        c.wait()
    s_gat[0].finish()
    s_gat[1].finish()
    row_adagrad(s_table, s_accum, lambda n: sgath[n // 4, pl.ds(pl.multiple_of(n % 4 * 128, 128), 128), :], new_s, new_sa)
    g_y.finish()
    g_c = send(gath.at[:, :, core], gath.at[:, :, core], partner)
    here = (me["x"], me["z"], me["y"])
    for p in (5, 6, 4, 0, 2, 1, 3):
        sums[p, 2].finish()
        first, rows = PORT[p][:2]
        mine[first : first + rows, :] = work[p][here[:2] if begins[p] else here]
    g_c.wait_recv()
    row_adagrad(f_table, f_accum, lambda n: gath[n // 2, pl.ds(n % 2 * 2, 2)].reshape(128, 128), new_f, new_fa)
    up_rows, down_rows = g_up.shape[0], g_down.shape[0]
    cols = g_up.shape[1] // 128
    for c in range(cols):
        g_up[:, c * 128 : (c + 1) * 128] = mine[pl.ds(c, up_rows, stride=cols), :]
    first, cols = up_rows * cols, g_down.shape[1] // 128
    for c in range(cols):
        g_down[:, c * 128 : (c + 1) * 128] = mine[pl.ds(first + c, down_rows, stride=cols), :]
    g_bias[...] = mine[first + down_rows * cols : first + down_rows * cols + 1, 0:down_rows]
    for c in send.sent:
        c().wait_send()


def reduce_scratch(owned, frequent, arrived):
    v = lambda *s: pltpu.VMEM(s, f32)
    begins = BEGINS
    out = [v(*(4,) * (3 - b), r, 128) for b, (_, r, _, _) in zip(begins, PORT)]
    for b, (_, r, h, _) in zip(begins, PORT):
        for k in range(b, 3):
            lead = (4,) * (2 - k)
            out += [v(*lead, n, 128) for n in ((r, r, r) if k == 2 else (h, r - h, r, r))]
    q = owned // 4
    out += [v(4, q, 128)] + [v(q // 4, 128), v(q // 4, 128), v(q // 2, 128), v(q // 2, 128)] * 2 + [v(4, q, 128)]
    out += [v(4, 4, 8, 128)] + [v(4, 8, 128)] * 3 + [v(8, 128)] * 3 + [v(4, 4, 2, 4, 8, 128)]
    n = arrived.shape[0] // 16
    flat = arrived.shape[0] * (arrived.shape[1] - 8)
    out += [v(max(a + r for a, r, _, _ in PORT), 128)]
    out += [v(*arrived.shape), pltpu.VMEM((n, 1, flat // n), i32), pltpu.VMEM((flat, 256), bf16), v(q, 256)]
    out += [v(frequent, 128), v(frequent // 128, 128), v(owned, 128), v(owned // 128, 128)]
    out += [pltpu.SemaphoreType.DMA((112,)), pltpu.SemaphoreType.DMA((112,)), pltpu.SemaphoreType.DMA((16,))]
    return out


def reduce_all(parts, arrived, f_table, f_accum, s_table, s_accum, count, width, rank):
    vmem = pl.BlockSpec(memory_space=pltpu.VMEM)
    anyw = pl.BlockSpec(memory_space=pl.ANY)
    frequent, owned = f_table.shape[0], s_table.shape[0]
    given = [f_table, f_accum.reshape(-1, 128), s_table, s_accum.reshape(-1, 128)]
    shapes = [g.shape for g in given] + [(rank // count, width), (width // count, rank), (1, width // count)]
    shapes = [jax.ShapeDtypeStruct(shape, f32) for shape in shapes]
    outs = pl.pallas_call(
        reduce_kernel,
        out_shape=tuple(shapes),
        in_specs=[anyw] * (len(PORT) + 6),
        out_specs=(vmem,) * 7,
        scratch_shapes=reduce_scratch(owned, frequent, arrived),
        compiler_params=params(collective_id=0, has_side_effects=True),
        name="reduce_kernel",
    )(*[w.reshape(4, 4, *w.shape[1:]) for w in parts], arrived, *given)
    return pl.pallas_call(
        move_kernel,
        out_shape=tuple(shapes),
        in_specs=[anyw] * 7,
        out_specs=(anyw,) * 7,
        scratch_shapes=[pltpu.VMEM(x.shape, f32) for x in shapes] + [pltpu.SemaphoreType.DMA((2, 7))],
        compiler_params=params(),
        name="move_kernel",
    )(*outs)


def body(cross_in, cotangent, weight_down, weight_up, cross_bias, row_place, frequent_table, frequent_accum, shard_table, shard_accum):
    samples, width = cross_in.shape
    rank = weight_down.shape[1]
    tables = row_place.shape[1]
    emb = frequent_table.shape[1]
    f_count = frequent_table.shape[0]
    owned = shard_table.shape[0]
    shards = lax.axis_size("dp")
    count = shards * lax.axis_size("rep")
    capacity = samples * tables // (2 * shards)
    blocks = width // emb
    per = 3
    steps = blocks // per
    wide = per * emb
    vmem = pl.BlockSpec(memory_space=pltpu.VMEM)

    place_t = row_place.T
    anyw = pl.BlockSpec(memory_space=pl.ANY)
    hidden, back_low, values, bucket = pl.pallas_call(
        functools.partial(front_kernel, f_count, owned),
        out_shape=(
            jax.ShapeDtypeStruct((samples, rank), bf16),
            jax.ShapeDtypeStruct((samples, rank), bf16),
            jax.ShapeDtypeStruct((blocks * samples, emb), f32),
            jax.ShapeDtypeStruct((shards, capacity + 8, emb), f32),
        ),
        in_specs=[vmem, vmem, anyw, anyw, anyw, anyw],
        out_specs=(vmem, vmem, anyw, anyw),
        scratch_shapes=[
            pltpu.VMEM((samples, width), bf16),
            pltpu.VMEM((samples, width), bf16),
            pltpu.VMEM((width, rank), bf16),
            pltpu.VMEM((rank, width), bf16),
            pltpu.VMEM((blocks * samples, emb), f32),
            pltpu.VMEM((shards, capacity + 8, emb), f32),
            pltpu.VMEM((tables * shards, samples), bf16),
            pltpu.VMEM((tables * shards, samples), f32),
            pltpu.VMEM((shards, 256), i32),
            pltpu.VMEM((shards, 128), f32),
            pltpu.VMEM((shards, 128), f32),
            pltpu.SMEM((shards, 256), i32),
            pltpu.VMEM((samples, rank), f32),
            pltpu.VMEM((samples, rank), f32),
            pltpu.SemaphoreType.DMA((steps, 4)),
            pltpu.SemaphoreType.DMA((3,)),
            pltpu.SemaphoreType.DMA((shards,)),
            pltpu.SemaphoreType.DMA,
        ],
        compiler_params=params(),
        name="front_kernel",
    )(place_t, cross_bias, cross_in, cotangent, weight_down, weight_up)

    arrived = lax.all_to_all(bucket, "dp", split_axis=0, concat_axis=0, tiled=True)

    parts = pl.pallas_call(
        functools.partial(weights_kernel, steps),
        grid=(steps,),
        out_shape=tuple(
            jax.ShapeDtypeStruct(shape, f32)
            for shape in [(16, 4, r, 128) for _, r, _, _ in PORT[:N_BULK]]
            + [(16, r, 128) for _, r, _, _ in PORT[N_BULK:]]
            + [(16, 8, 128)]
        ),
        in_specs=[
            pl.BlockSpec((samples, rank), lambda g: (0, 0)),
            pl.BlockSpec((samples, rank), lambda g: (0, 0)),
            pl.BlockSpec((samples, wide), lambda g: (0, g)),
            pl.BlockSpec((samples, wide), lambda g: (0, g)),
            anyw,
            pl.BlockSpec((tables, samples), lambda g: (0, 0)),
        ],
        out_specs=(anyw,) * (len(PORT) + 1),
        scratch_shapes=[pltpu.VMEM((16, 4, r, 128), f32) for _, r, _, _ in PORT]
        + [pltpu.VMEM((16, n, 128), f32) for _, r, h, _ in PORT[N_BULK:] for n in (h, r - h, r, r)]
        + [pltpu.VMEM((16, 2, 4, 8, 128), f32), pltpu.VMEM((16, 4, 8, 128), f32)]
        + [pltpu.VMEM((16, 8, 128), f32)] * 3
        + [
            pltpu.VMEM((16, 2, 4, max(a + r for a, r, _, _ in PORT), 128), f32),
            pltpu.VMEM((f_count, emb), f32),
            pltpu.VMEM((rank, samples), bf16),
            pltpu.VMEM((rank // 128 * width, 128), f32),
            pltpu.VMEM((per * rank, 128), f32),
            pltpu.VMEM((1, width), f32),
            pltpu.VMEM((blocks * samples, emb), f32),
            pltpu.VMEM((tables, 1, samples), i32),
            pltpu.SemaphoreType.DMA((24,)),
            pltpu.SemaphoreType.DMA((24,)),
            pltpu.SemaphoreType.DMA((16,)),
        ],
        compiler_params=params(collective_id=1, has_side_effects=True),
        name="weights_kernel",
    )(hidden, back_low, cross_in, cotangent, values, place_t)

    new_frequent, new_frequent_accum, new_shard, new_shard_accum, grad_up, grad_down, grad_bias = reduce_all(
        parts, arrived, frequent_table, frequent_accum, shard_table, shard_accum, count, width, rank
    )
    new_frequent_accum, new_shard_accum = new_frequent_accum.reshape(-1), new_shard_accum.reshape(-1)
    grad_bias = grad_bias.reshape(-1)
    return (new_frequent, new_frequent_accum, new_shard, new_shard_accum, grad_up, grad_down, grad_bias)


def solution(mesh):
    both = ("dp", "rep")
    in_specs = (P(both, None), P(both, None), P(), P(), P(), P(both, None), P(), P(), P("dp", None), P("dp"))
    out_specs = (P(), P(), P("dp", None), P("dp"), P(both, None), P(both, None), P(both))
    return jax.shard_map(body, mesh=mesh, in_specs=in_specs, out_specs=out_specs, check_vma=False)
```

```python
import functools
import jax
import jax.numpy as jnp
from jax import lax
from jax.experimental import pallas as pl
from jax.experimental.pallas import tpu as pltpu
from jax.sharding import PartitionSpec as P

learn_rate = 0.05
eps_ada = 1e-08
f32, bf16, i32 = jnp.float32, jnp.bfloat16, jnp.int32
VLIM = 66 * 1000 * 1000


def row_adagrad(table, accum, grad_of, new, new_accum):
    def chunk(n, _):
        at = pl.ds(pl.multiple_of(n * 128, 128), 128)
        g = grad_of(n)
        before = jnp.broadcast_to(accum[pl.ds(n, 1), :], (128, 128)).T
        after = before + jnp.mean(g * g, axis=1, keepdims=True)
        new[at, :] = table[at, :] - learn_rate * g / (jnp.sqrt(after) + eps_ada)
        new_accum[pl.ds(n, 1), :] = after.T[0:1, :]
        return 0

    lax.fori_loop(0, table.shape[0] // 128, chunk, 0)


def move_kernel(*refs):
    n = len(refs) // 3
    src, dst, held, sems = refs[:n], refs[n : 2 * n], refs[2 * n : 3 * n], refs[3 * n]
    takes = [pltpu.make_async_copy(a, b, sems.at[0, i]) for i, (a, b) in enumerate(zip(src, held))]
    gives = [pltpu.make_async_copy(a, b, sems.at[1, i]) for i, (a, b) in enumerate(zip(held, dst))]
    for c in takes:
        c.start()
    for c, d in zip(takes, gives):
        c.wait()
        d.start()
    for d in gives:
        d.wait()


def dot_nt(a, b):
    return lax.dot_general(a, b, (((1,), (1,)), ((), ())), preferred_element_type=f32)


def dot_tn(a, b):
    return lax.dot_general(a, b, (((0,), (0,)), ((), ())), preferred_element_type=f32)


def hi_lo(v):
    hi = v.astype(bf16)
    lo = (v - hi.astype(f32)).astype(bf16)
    return jnp.concatenate([hi, lo], axis=1)


def one_hot(flags):
    return jnp.where(flags, 1.0, 0.0).astype(bf16)


def index_work(frequent, owned, place, idx, row_a, row_b, hot, cum):
    tables, samples = place.shape
    owners, slots = idx.shape[0], 256
    at = lax.broadcasted_iota(i32, (1, samples), 1)
    owner_iota = lax.broadcasted_iota(i32, (owners, samples), 0)
    tri = one_hot(
        lax.broadcasted_iota(i32, (samples, samples), 0)
        < lax.broadcasted_iota(i32, (samples, samples), 1)
    )
    shift = owned.bit_length() - 1
    for t in range(tables):
        owner = lax.shift_right_arithmetic(place[t : t + 1, :] - frequent, shift)
        hot[t * owners : (t + 1) * owners, :] = one_hot(owner_iota == owner)
    cum[...] = jnp.dot(hot[...], tri, preferred_element_type=f32)
    base = jnp.zeros((owners, 1), f32)
    total = jnp.zeros((4 * owners, slots), f32)
    slot_iota = lax.broadcasted_iota(i32, (slots, samples), 0)
    at_hi = lax.shift_right_logical(at, 7).astype(f32)
    at_lo = (at & 127).astype(f32)
    blocks = samples // 128
    for t in range(tables):
        mine = hot[t * owners : (t + 1) * owners, :].astype(f32)
        before = cum[t * owners : (t + 1) * owners, :] + base
        rank = jnp.sum(mine * before, axis=0, keepdims=True).astype(i32)
        base = before[:, samples - 1 :] + mine[:, samples - 1 :]
        local = (place[t : t + 1, :] - frequent) & (owned - 1)
        parts = [
            mine * (at_hi + float((t + 1) * blocks)),
            mine * at_lo,
            mine * (lax.shift_right_logical(local, 7) + 1).astype(f32),
            mine * (local & 127).astype(f32),
        ]
        left = jnp.concatenate(parts, axis=0).astype(bf16)
        total = total + dot_nt(left, one_hot(slot_iota == rank))
    found = jnp.maximum((total[:owners] * 128.0 + total[owners : 2 * owners]).astype(i32), samples)
    idx[:, 0, :] = found[:, :128]
    idx[:, 1, :] = found[:, 128:]
    row = (total[2 * owners : 3 * owners] - 1.0) * 128.0 + total[3 * owners :]
    row_a[...] = row[:, :128]
    row_b[...] = row[:, 128:]


def spans(first, end, most):
    return [(at, min(most, end - at)) for at in range(first, end, most)]


def front_kernel(
    frequent, owned, place, bias, cross_hbm, cot_hbm, down_hbm, up_hbm,
    hidden, back_low, values_hbm, bucket_hbm,
    cross, cot, down, up, values, bucket, hot, cum, idx_v, row_a, row_b, idx, h_acc, b_acc, in_sems, v_sems, b_sems, i_sem,
):
    samples = hidden.shape[0]
    emb = values.shape[1]
    width = cross.shape[1]
    lows = spans(0, width, 1280)
    highs = spans(emb, width, 1280)
    owners = bucket.shape[0]
    slots = bucket.shape[1] - 8

    loads = []
    for g, (at, wide) in enumerate(lows):
        cols = pl.ds(at, wide)
        loads.append([
            pltpu.make_async_copy(cross_hbm.at[:, cols], cross.at[:, cols], in_sems.at[g, 0]),
            pltpu.make_async_copy(cot_hbm.at[:, cols], cot.at[:, cols], in_sems.at[g, 1]),
            pltpu.make_async_copy(down_hbm.at[cols, :], down.at[cols, :], in_sems.at[g, 2]),
            pltpu.make_async_copy(up_hbm.at[:, cols], up.at[:, cols], in_sems.at[g, 3]),
        ])
    for group in loads:
        for c in group:
            c.start()
    index_work(frequent, owned, place, idx_v, row_a, row_b, hot, cum)
    to_scalar = pltpu.make_async_copy(idx_v, idx, i_sem)
    to_scalar.start()
    for g, (at, wide) in enumerate(lows):
        for c in loads[g]:
            c.wait()
        x = cross[:, at : at + wide]
        inner = (cot[:, at : at + wide].astype(f32) * x.astype(f32)).astype(bf16)
        h = jnp.dot(x, down[at : at + wide, :], preferred_element_type=f32)
        b = dot_nt(inner, up[:, at : at + wide])
        if g == 0:
            h_acc[...] = h
            b_acc[...] = b
        else:
            h_acc[...] += h
            b_acc[...] += b
    hidden[...] = h_acc[...].astype(bf16)
    back_low[...] = b_acc[...].astype(bf16)
    stores = []
    for g, (at, wide) in enumerate(highs):
        scaled = jnp.dot(hidden[...], up[:, at : at + wide], preferred_element_type=f32)
        scaled = scaled + bias[pl.ds(at, wide)].reshape(1, wide)
        v = cot[:, at : at + wide].astype(f32) * (scaled + 1.0) + dot_nt(back_low[...], down[at : at + wide, :])
        for k in range(wide // emb):
            first = (at // emb + k) * samples
            values[first : first + samples, :] = v[:, k * emb : (k + 1) * emb]
        part = pl.ds(at // emb * samples, wide // emb * samples)
        stores.append(pltpu.make_async_copy(values.at[part], values_hbm.at[part], v_sems.at[g]))
        stores[-1].start()
    to_scalar.wait()

    def ship(o):
        return pltpu.make_async_copy(bucket.at[o], bucket_hbm.at[o], b_sems.at[o])

    def pick(o, _):
        for k in range(slots):
            src = idx[o, k // 128, k % 128]
            bucket[o, k : k + 1, :] = values[pl.ds(src, 1), :]
        bucket[o, slots : slots + 8, :] = jnp.zeros((8, emb), f32)
        bucket[o, slots : slots + 1, :] = row_a[pl.ds(o, 1), :]
        bucket[o, slots + 1 : slots + 2, :] = row_b[pl.ds(o, 1), :]
        ship(o).start()
        return 0

    lax.fori_loop(0, owners, pick, 0)
    for c in stores:
        c.wait()
    lax.fori_loop(0, owners, lambda o, _: (ship(o).wait(), 0)[1], 0)


PORT = (
    (104, 32, 16, "xzy"),
    (136, 24, 16, "xzy"),
    (160, 32, 16, "zxy"),
    (192, 32, 16, "zxy"),
    (72, 32, 16, "yxz"),
    (0, 40, 24, "yxz"),
    (40, 32, 16, "yzx"),
)
N_BULK = 5
BEGINS = [1 if p >= N_BULK else 0 for p in range(len(PORT))]


def mesh_place():
    dp, y = lax.axis_index("dp"), lax.axis_index("rep")
    core = dp % 2
    return {"x": dp // 8, "z": (dp // 2) % 4, "y": y}, core, (dp + 1 - 2 * core, y)


class Links:
    def __init__(self, send_sems, recv_sems):
        self.sems, self.used, self.sent = (send_sems, recv_sems), 0, []

    def base(self, n):
        self.used += n
        return self.used - n

    def make(self, k, src, dst, to):
        return pltpu.make_async_remote_copy(
            src_ref=src, dst_ref=dst, send_sem=self.sems[0].at[k], recv_sem=self.sems[1].at[k],
            device_id=to, device_id_type=pl.DeviceIdType.MESH,
        )

    def go(self, k, src, dst, to):
        copy = self.make(k, src(), dst, to())
        copy.start()
        self.sent.append(lambda: self.make(k, src(), dst, to()))
        return copy

    def __call__(self, src, dst, to):
        return self.go(self.base(1), lambda: src, dst, lambda: to)


class Reduce:
    def __init__(self, links, near, at, add, rows, half, lands):
        (_, up, far, down), to = near
        self.links, self.here, self.up, self.down = links, near[0][0], up, down
        self.at, self.add, self.rows, self.half, self.lands = at, add, rows, half, lands
        k = links.base(4)
        self.args = [
            (k, lambda: at(far, 0, half), lands[0], lambda: to[up]),
            (k + 1, lambda: at(far, half, rows), lands[1], lambda: to[down]),
            (k + 2, lambda: at(up, 0, rows), lands[2], lambda: to[up]),
            (k + 3, lambda: at(down, 0, rows), lands[3], lambda: to[down]),
        ]

    def go(self, i):
        k, src, dst, to = self.args[i]
        self.links.go(k, src, dst, to)

    def got(self, i):
        k, src, dst, to = self.args[i]
        self.links.make(k, src(), dst, to()).wait_recv()

    def start(self):
        self.go(0)
        self.go(1)

    def middle(self):
        self.got(0)
        self.add(self.up, 0, self.half, self.lands[:1])
        self.go(2)
        self.got(1)
        self.add(self.down, self.half, self.rows, self.lands[1:2])
        self.go(3)

    def finish(self):
        self.got(2)
        self.got(3)
        self.add(self.here, 0, self.rows, self.lands[2:4])


class Direct:
    def __init__(self, send, near, at, add, lands):
        self.send, self.near, self.at, self.add, self.lands = send, near, at, add, lands

    def start(self):
        places, to = self.near
        self.got = [self.send(self.at(places[d]), self.lands[d - 1], to[places[d]]) for d in (1, 3, 2)]

    def finish(self):
        for c in self.got:
            c.wait_recv()
        self.add(self.near[0][0], self.lands)


class Spread:
    def __init__(self, send, near, at):
        self.send, self.near, self.at = send, near, at

    def start(self):
        places, to = self.near
        src = self.at(places[0])
        self.got = [self.send(src, src, to[places[d]]) for d in (1, 3, 2)]

    def finish(self):
        for c in self.got:
            c.wait_recv()


class Ids:
    def __init__(self, make):
        self.make = make

    def __getitem__(self, t):
        return self.make(t)


def neighbours(me, core, axis):
    def device(to):
        at = dict(me, **{axis: to})
        return ((at["x"] * 4 + at["z"]) * 2 + core, at["y"])

    return [(me[axis] + d) % 4 for d in range(4)], Ids(device)


def greet(peers, meanwhile=lambda: None):
    barrier = pltpu.get_barrier_semaphore()
    for peer in peers:
        pl.semaphore_signal(barrier, inc=1, device_id=peer, device_id_type=pl.DeviceIdType.MESH)
    meanwhile()
    pl.semaphore_wait(barrier, len(peers))


def weights_kernel(steps, hidden, back_low, cross, cot, values_hbm, place_in, *rest):
    outs, rest = rest[: len(PORT)], rest[len(PORT) :]
    freq_out, rest = rest[0], rest[1:]
    pair, rest = rest[: len(PORT)], rest[len(PORT) :]
    y_land, rest = [rest[:4], rest[4:8]], rest[8:]
    f_both, f_pair, f_land, rest = rest[0], rest[1], rest[2:5], rest[5:]
    both, freq, hidden_t, down, up, bias, values, place, send_sems, recv_sems, local_sems = rest
    g = pl.program_id(0)
    rank = hidden.shape[1]
    wide = cross.shape[1]
    per = wide // 128
    frequent = freq.shape[0]
    samples = hidden.shape[0]
    count = frequent // 8
    width = wide * steps
    cols = per * steps
    up_rows = rank // count
    down_rows = width // count
    base = up_rows * cols
    bias_at = base + down_rows * rank // 128
    me, core, partner = mesh_place()
    near = neighbours(me, core, "y")
    load = pltpu.make_async_copy(values_hbm, values, local_sems.at[0])

    send = Links(send_sems, recv_sems)
    firsts = range(N_BULK, len(PORT))

    def part(p, c):
        first, rows = PORT[p][0], PORT[p][1]
        return both.at[:, c, :, pl.ds(first, rows), :]

    pair_base = send.base(len(PORT))
    pair_args = lambda p: (pair_base + p, lambda: part(p, 1 - core), pair[p], lambda: partner)

    def add_pair(p):
        first, rows = PORT[p][0], PORT[p][1]
        k, src, dst, to = pair_args(p)
        send.make(k, src(), dst, to()).wait_recv()

        def add(n, _):
            for y in range(4):
                both[n, core, y, first : first + rows, :] = both[n, core, y, first : first + rows, :] + pair[p][n, y]
            return 0

        lax.fori_loop(0, count // 8, add, 0)

    def y_phase(p):
        first, rows, half, _ = PORT[p]

        def at(t, lo, hi):
            return both.at[:, core, t, pl.ds(first + lo, hi - lo), :]

        def y_add(t, lo, hi, lands):
            def add(n, _):
                v = both[n, core, t, first + lo : first + hi, :]
                for ref in lands:
                    v = v + ref[n]
                both[n, core, t, first + lo : first + hi, :] = v
                return 0

            lax.fori_loop(0, count // 8, add, 0)

        return Reduce(send, near, at, y_add, rows, half, y_land[p - N_BULK])

    y_sums = {p: y_phase(p) for p in firsts}

    @pl.when(g == 0)
    def _():
        greet([partner] + [near[1][t] for t in near[0][1:]])
        load.start()
        hidden_t[...] = hidden[...].T
        for t in range(place.shape[0]):
            place[t] = place_in[t : t + 1, :]
        freq[...] = jnp.zeros_like(freq)

    inner = cot[...].astype(f32) * cross[...].astype(f32)
    bias[:, pl.ds(pl.multiple_of(g * wide, wide), wide)] = jnp.sum(inner, axis=0, keepdims=True)
    u = jnp.dot(hidden_t[...], inner.astype(bf16), preferred_element_type=f32)
    for k in range(per):
        up[k * rank : (k + 1) * rank, :] = u[:, k * 128 : (k + 1) * 128]
    d = dot_tn(cross[...], back_low[...])
    for k in range(rank // 128):
        down[pl.ds(pl.multiple_of(k * width + g * wide, 128), wide), :] = d[:, k * 128 : (k + 1) * 128]

    def put_up(n, _):
        for c in range(2):
            for y in range(4):
                i = n * 8 + c * 4 + y
                for k in range(per):
                    both[n, c, y, pl.ds(g * per + k, up_rows, stride=cols), :] = up[
                        pl.ds(k * rank + i * up_rows, up_rows), :
                    ]
        return 0

    lax.fori_loop(0, count // 8, put_up, 0)

    @pl.when(g == steps - 1)
    def _():
        for p in firsts:
            send.go(*pair_args(p))

        def put_down(n, _):
            for c in range(2):
                for y in range(4):
                    i = n * 8 + c * 4 + y
                    for k in range(rank // 128):
                        both[n, c, y, pl.ds(base + k, down_rows, stride=rank // 128), :] = down[
                            pl.ds(k * width + i * down_rows, down_rows), :
                        ]
                    both[n, c, y, bias_at : bias_at + 8, :] = jnp.zeros((8, 128), f32)
            return 0

        lax.fori_loop(0, count // 8, put_down, 0)
        for i in range(count):
            both[i // 8, (i // 4) % 2, i % 4, bias_at : bias_at + 1, 0:down_rows] = bias[
                :, i * down_rows : (i + 1) * down_rows
            ]
        for p in range(N_BULK):
            send.go(*pair_args(p))
        load.wait()
        row_iota = lax.broadcasted_iota(i32, (frequent, samples), 0)

        def tables(t, _):
            hots, parts = [], []
            for k in range(2):
                hots.append(one_hot(row_iota == place[2 * t + k]))
                parts.append(hi_lo(values[pl.ds(pl.multiple_of((2 * t + k + 1) * samples, 128), samples), :]))
            s = jnp.dot(jnp.concatenate(hots, axis=1), jnp.concatenate(parts, axis=0), preferred_element_type=f32)
            freq[...] += s[:, :128] + s[:, 128:]
            return 0

        def f_add(t, lands):
            v = f_both[:, core, t]
            for ref in lands:
                v = v + ref[...]
            f_both[:, core, t] = v

        f_sum = Direct(send, near, lambda t: f_both.at[:, core, t], f_add, f_land)
        pairs = place.shape[0] // 2
        lax.fori_loop(0, 2, tables, 0)
        for p in firsts:
            add_pair(p)
            y_sums[p].start()
        lax.fori_loop(2, pairs // 2 + 2, tables, 0)
        y_sums[N_BULK].middle()
        lax.fori_loop(pairs // 2 + 2, pairs, tables, 0)
        y_sums[N_BULK + 1].middle()

        def put_freq(n, _):
            for c in range(2):
                for y in range(4):
                    f_both[n, c, y] = freq[pl.ds(pl.multiple_of((n * 8 + c * 4 + y) * 8, 8), 8), :]
            return 0

        lax.fori_loop(0, count // 8, put_freq, 0)
        f_got = send(f_both.at[:, 1 - core], f_pair, partner)
        stores = []
        for p in range(N_BULK):
            add_pair(p)
            stores.append(pltpu.make_async_copy(part(p, core), outs[p], local_sems.at[1 + p]))
            stores[-1].start()
        f_got.wait_recv()
        f_both[:, core] = f_both[:, core] + f_pair[...]
        f_sum.start()
        for p in firsts:
            y_sums[p].finish()
            stores.append(pltpu.make_async_copy(y_sums[p].at(me["y"], 0, PORT[p][1]), outs[p], local_sems.at[1 + p]))
            stores[-1].start()
        f_sum.finish()
        stores.append(pltpu.make_async_copy(f_both.at[:, core, me["y"]], freq_out, local_sems.at[1 + len(PORT)]))
        stores[-1].start()
        for c in stores:
            c.wait()
        for c in send.sent:
            c().wait_send()


def params(**kw):
    return pltpu.CompilerParams(vmem_limit_bytes=VLIM, **kw)


def reduce_kernel(*refs):
    it = iter(refs)
    take = lambda n: [next(it) for _ in range(n)]
    pieces = range(len(PORT))
    begins = BEGINS
    loads, (load_f, arrived), given = take(len(PORT)), take(2), take(4)
    new_f, new_fa, new_s, new_sa, g_up, g_down, g_bias = take(7)
    work = take(len(PORT))
    land = {p: {k: take(3 if k == 2 else 4) for k in range(begins[p], 3)} for p in pieces}
    swork, sland, sgath = next(it), [take(4), take(4)], next(it)
    f_work, fx_land, fz_land, gath = next(it), take(3), take(3), next(it)
    mine, arr, ids, right, acc = take(5)
    f_table, f_accum, s_table, s_accum = held = take(4)
    send_sems, recv_sems, local_sems = take(3)
    me, core, partner = mesh_place()
    near = {a: neighbours(me, core, a) for a in "xzy"}
    copies = [pltpu.make_async_copy(loads[p], work[p], local_sems.at[p]) for p in pieces]
    more = [(load_f, f_work), (arrived, arr)] + list(zip(given, held))
    copy_f, copy_a, *rest = [
        pltpu.make_async_copy(a, b, local_sems.at[len(PORT) + i]) for i, (a, b) in enumerate(more)
    ]

    def load_all():
        for c in [copy_f, copies[0], copies[2], copies[4], copy_a, copies[1], copies[3], copies[5], copies[6]] + rest:
            c.start()

    greet([partner] + [near[a][1][t] for a in "xzy" for t in near[a][0][1:]], load_all)
    send = Links(send_sems, recv_sems)

    def where(dims, done, axis, t, rem=None):
        rem = iter(rem) if rem is not None else None
        out = []
        for a in dims:
            if a in done:
                out.append(me[a])
            elif a == axis:
                out.append(t)
            else:
                out.append(slice(None) if rem is None else next(rem))
        return tuple(out)

    def phase(p, k):
        _, rows, half, order = PORT[p]
        dims = "xz" if begins[p] else "xzy"
        done, axis = order[begins[p] : k], order[k]
        ref, left = work[p], 2 - k

        def at(t, lo, hi):
            return ref.at[where(dims, done, axis, t) + (pl.ds(lo, hi - lo), slice(None))]

        def add(t, lo, hi, lands):
            def one(rem):
                spot = where(dims, done, axis, t, rem) + (slice(lo, hi), slice(None))
                v = ref[spot]
                for x in lands:
                    v = v + x[rem + (slice(None), slice(None))]
                ref[spot] = v

            if left == 0:
                one(())
            elif left == 1:
                lax.fori_loop(0, 4, lambda i, _: (one((i,)), 0)[1], 0)
            else:
                lax.fori_loop(0, 16, lambda i, _: (one((i // 4, i % 4)), 0)[1], 0)

        if k == 2:
            whole = lambda t: at(t, 0, rows)
            return Direct(send, near[axis], whole, lambda t, lands: add(t, 0, rows, lands), land[p][k])
        return Reduce(send, near[axis], at, add, rows, half, land[p][k])

    sums = {(p, k): phase(p, k) for p in pieces for k in range(begins[p], 3)}

    owned = swork.shape[1]

    part = owned // 2

    def s_phase(h):
        def at(t, lo, hi):
            return swork.at[t, pl.ds(h * part + lo, hi - lo), :]

        def add(t, lo, hi, lands):
            for r in range(lo, hi, 128):
                v = swork[t, h * part + r : h * part + r + 128, :]
                for ref in lands:
                    v = v + ref[r - lo : r - lo + 128, :]
                swork[t, h * part + r : h * part + r + 128, :] = v

        return Reduce(send, near["y"], at, add, part, part // 2, sland[h])

    s_red = [s_phase(0), s_phase(1)]

    def f_add(spot, lands):
        v = f_work[spot]
        for ref in lands:
            v = v + ref[...]
        f_work[spot] = v

    f_x = Direct(send, near["x"], lambda t: f_work.at[t], lambda t, l: f_add((t,), l), fx_land)
    f_z = Direct(
        send, near["z"], lambda t: f_work.at[me["x"], t], lambda t, l: f_add((me["x"], t), l), fz_land
    )
    g_z = Spread(send, near["z"], lambda t: gath.at[me["x"], t, core, me["y"]])
    g_x = Spread(send, near["x"], lambda t: gath.at[t, :, core, me["y"]])
    g_y = Spread(send, near["y"], lambda t: gath.at[:, :, core, t])

    class SegGather:
        def __init__(self, h):
            self.first = h * part

        def at(self, t, lo, hi):
            return sgath.at[t, pl.ds(self.first + lo, hi - lo), :]

        def start(self):
            (here, up, far, down), to = near["y"]
            spot = (here, slice(self.first, self.first + part), slice(None))
            sgath[spot] = swork[spot]
            src = self.at(here, 0, part)
            self.c0, self.c1 = send(src, src, to[up]), send(src, src, to[down])

        def middle(self):
            (here, up, far, down), to = near["y"]
            self.c0.wait_recv()
            src = self.at(down, 0, part // 2)
            self.c2 = send(src, src, to[up])
            self.c1.wait_recv()
            src = self.at(up, part // 2, part)
            self.c3 = send(src, src, to[down])

        def finish(self):
            self.c2.wait_recv()
            self.c3.wait_recv()

    s_gat = [SegGather(0), SegGather(1)]
    slots = arr.shape[1] - 8
    some = ids.shape[0]
    each_of = arr.shape[0] // some
    chunk = each_of * slots

    def prepare(g, _):
        rows = []
        for b in range(each_of):
            n = g * each_of + b
            rows.append(arr[n, slots : slots + 1, :])
            rows.append(arr[n, slots + 1 : slots + 2, : slots - 128])
            right[pl.ds(pl.multiple_of(n * slots, 16), slots), :] = hi_lo(arr[n, :slots, :])
        ids[g] = jnp.concatenate(rows, axis=1).astype(i32)
        return 0

    def seg_block(t):
        acc[...] = jnp.zeros_like(acc)
        first = t * owned

        def one(g, _):
            hot = one_hot(lax.broadcasted_iota(i32, (owned, chunk), 0) + first == ids[g])
            acc[...] += jnp.dot(
                hot, right[pl.ds(pl.multiple_of(g * chunk, 16), chunk), :], preferred_element_type=f32
            )
            return 0

        lax.fori_loop(0, some, one, 0)
        swork[t] = acc[:, :128] + acc[:, 128:]

    _, y_up, y_far, y_down = near["y"][0]
    def done(p, k):
        sums[p, k].finish()
        if k < 2:
            sums[p, k + 1].start()

    copy_f.wait()
    f_x.start()
    for p in (0, 2, 4, 1, 3):
        copies[p].wait()
        sums[p, 0].start()
    copy_a.wait()
    lax.fori_loop(0, some, prepare, 0)
    f_x.finish()
    f_z.start()
    sums[4, 0].middle()
    seg_block(y_far)
    s_red[0].start()
    s_red[1].start()
    sums[0, 0].middle()
    sums[2, 0].middle()
    sums[1, 0].middle()
    sums[3, 0].middle()
    for p in (5, 6):
        copies[p].wait()
        sums[p, 1].start()
    seg_block(y_up)
    f_z.finish()
    gath[me["x"], me["z"], core, me["y"]] = f_work[me["x"], me["z"]]
    g_z.start()
    seg_block(y_down)
    s_red[0].middle()
    s_red[1].middle()
    done(4, 0)
    seg_block(me["y"])
    done(0, 0)
    done(2, 0)
    done(1, 0)
    done(3, 0)
    sums[5, 1].middle()
    sums[6, 1].middle()
    s_red[0].finish()
    s_gat[0].start()
    s_red[1].finish()
    s_gat[1].start()
    g_z.finish()
    g_x.start()
    for p in (4, 0, 2, 1, 3):
        sums[p, 1].middle()
    s_gat[0].middle()
    s_gat[1].middle()
    done(5, 1)
    done(6, 1)
    g_x.finish()
    g_y.start()
    for p in (4, 0, 2, 1, 3):
        done(p, 1)
    for c in rest:
        c.wait()
    s_gat[0].finish()
    s_gat[1].finish()
    row_adagrad(s_table, s_accum, lambda n: sgath[n // 4, pl.ds(pl.multiple_of(n % 4 * 128, 128), 128), :], new_s, new_sa)
    g_y.finish()
    g_c = send(gath.at[:, :, core], gath.at[:, :, core], partner)
    here = (me["x"], me["z"], me["y"])
    for p in (5, 6, 4, 0, 2, 1, 3):
        sums[p, 2].finish()
        first, rows = PORT[p][:2]
        mine[first : first + rows, :] = work[p][here[:2] if begins[p] else here]
    g_c.wait_recv()
    row_adagrad(f_table, f_accum, lambda n: gath[n // 2, pl.ds(n % 2 * 2, 2)].reshape(128, 128), new_f, new_fa)
    up_rows, down_rows = g_up.shape[0], g_down.shape[0]
    cols = g_up.shape[1] // 128
    for c in range(cols):
        g_up[:, c * 128 : (c + 1) * 128] = mine[pl.ds(c, up_rows, stride=cols), :]
    first, cols = up_rows * cols, g_down.shape[1] // 128
    for c in range(cols):
        g_down[:, c * 128 : (c + 1) * 128] = mine[pl.ds(first + c, down_rows, stride=cols), :]
    g_bias[...] = mine[first + down_rows * cols : first + down_rows * cols + 1, 0:down_rows]
    for c in send.sent:
        c().wait_send()


def reduce_scratch(owned, frequent, arrived):
    v = lambda *s: pltpu.VMEM(s, f32)
    begins = BEGINS
    out = [v(*(4,) * (3 - b), r, 128) for b, (_, r, _, _) in zip(begins, PORT)]
    for b, (_, r, h, _) in zip(begins, PORT):
        for k in range(b, 3):
            lead = (4,) * (2 - k)
            out += [v(*lead, n, 128) for n in ((r, r, r) if k == 2 else (h, r - h, r, r))]
    q = owned // 4
    out += [v(4, q, 128)] + [v(q // 4, 128), v(q // 4, 128), v(q // 2, 128), v(q // 2, 128)] * 2 + [v(4, q, 128)]
    out += [v(4, 4, 8, 128)] + [v(4, 8, 128)] * 3 + [v(8, 128)] * 3 + [v(4, 4, 2, 4, 8, 128)]
    n = arrived.shape[0] // 16
    flat = arrived.shape[0] * (arrived.shape[1] - 8)
    out += [v(max(a + r for a, r, _, _ in PORT), 128)]
    out += [v(*arrived.shape), pltpu.VMEM((n, 1, flat // n), i32), pltpu.VMEM((flat, 256), bf16), v(q, 256)]
    out += [v(frequent, 128), v(frequent // 128, 128), v(owned, 128), v(owned // 128, 128)]
    out += [pltpu.SemaphoreType.DMA((112,)), pltpu.SemaphoreType.DMA((112,)), pltpu.SemaphoreType.DMA((16,))]
    return out


def reduce_all(parts, arrived, f_table, f_accum, s_table, s_accum, count, width, rank):
    vmem = pl.BlockSpec(memory_space=pltpu.VMEM)
    anyw = pl.BlockSpec(memory_space=pl.ANY)
    frequent, owned = f_table.shape[0], s_table.shape[0]
    given = [f_table, f_accum.reshape(-1, 128), s_table, s_accum.reshape(-1, 128)]
    shapes = [g.shape for g in given] + [(rank // count, width), (width // count, rank), (1, width // count)]
    shapes = [jax.ShapeDtypeStruct(shape, f32) for shape in shapes]
    outs = pl.pallas_call(
        reduce_kernel,
        out_shape=tuple(shapes),
        in_specs=[anyw] * (len(PORT) + 6),
        out_specs=(vmem,) * 7,
        scratch_shapes=reduce_scratch(owned, frequent, arrived),
        compiler_params=params(collective_id=0, has_side_effects=True),
        name="reduce_kernel",
    )(*[w.reshape(4, 4, *w.shape[1:]) for w in parts], arrived, *given)
    return pl.pallas_call(
        move_kernel,
        out_shape=tuple(shapes),
        in_specs=[anyw] * 7,
        out_specs=(anyw,) * 7,
        scratch_shapes=[pltpu.VMEM(x.shape, f32) for x in shapes] + [pltpu.SemaphoreType.DMA((2, 7))],
        compiler_params=params(),
        name="move_kernel",
    )(*outs)


def body(cross_in, cotangent, weight_down, weight_up, cross_bias, row_place, frequent_table, frequent_accum, shard_table, shard_accum):
    samples, width = cross_in.shape
    rank = weight_down.shape[1]
    tables = row_place.shape[1]
    emb = frequent_table.shape[1]
    f_count = frequent_table.shape[0]
    owned = shard_table.shape[0]
    shards = lax.axis_size("dp")
    count = shards * lax.axis_size("rep")
    capacity = samples * tables // (2 * shards)
    blocks = width // emb
    per = 3
    steps = blocks // per
    wide = per * emb
    vmem = pl.BlockSpec(memory_space=pltpu.VMEM)

    place_t = row_place.T
    anyw = pl.BlockSpec(memory_space=pl.ANY)
    hidden, back_low, values, bucket = pl.pallas_call(
        functools.partial(front_kernel, f_count, owned),
        out_shape=(
            jax.ShapeDtypeStruct((samples, rank), bf16),
            jax.ShapeDtypeStruct((samples, rank), bf16),
            jax.ShapeDtypeStruct((blocks * samples, emb), f32),
            jax.ShapeDtypeStruct((shards, capacity + 8, emb), f32),
        ),
        in_specs=[vmem, vmem, anyw, anyw, anyw, anyw],
        out_specs=(vmem, vmem, anyw, anyw),
        scratch_shapes=[
            pltpu.VMEM((samples, width), bf16),
            pltpu.VMEM((samples, width), bf16),
            pltpu.VMEM((width, rank), bf16),
            pltpu.VMEM((rank, width), bf16),
            pltpu.VMEM((blocks * samples, emb), f32),
            pltpu.VMEM((shards, capacity + 8, emb), f32),
            pltpu.VMEM((tables * shards, samples), bf16),
            pltpu.VMEM((tables * shards, samples), f32),
            pltpu.VMEM((shards, 2, 128), i32),
            pltpu.VMEM((shards, 128), f32),
            pltpu.VMEM((shards, 128), f32),
            pltpu.SMEM((shards, 2, 128), i32),
            pltpu.VMEM((samples, rank), f32),
            pltpu.VMEM((samples, rank), f32),
            pltpu.SemaphoreType.DMA((steps, 4)),
            pltpu.SemaphoreType.DMA((3,)),
            pltpu.SemaphoreType.DMA((shards,)),
            pltpu.SemaphoreType.DMA,
        ],
        compiler_params=params(),
        name="front_kernel",
    )(place_t, cross_bias, cross_in, cotangent, weight_down, weight_up)

    arrived = lax.all_to_all(bucket, "dp", split_axis=0, concat_axis=0, tiled=True)

    parts = pl.pallas_call(
        functools.partial(weights_kernel, steps),
        grid=(steps,),
        out_shape=tuple(
            jax.ShapeDtypeStruct(shape, f32)
            for shape in [(16, 4, r, 128) for _, r, _, _ in PORT[:N_BULK]]
            + [(16, r, 128) for _, r, _, _ in PORT[N_BULK:]]
            + [(16, 8, 128)]
        ),
        in_specs=[
            pl.BlockSpec((samples, rank), lambda g: (0, 0)),
            pl.BlockSpec((samples, rank), lambda g: (0, 0)),
            pl.BlockSpec((samples, wide), lambda g: (0, g)),
            pl.BlockSpec((samples, wide), lambda g: (0, g)),
            anyw,
            pl.BlockSpec((tables, samples), lambda g: (0, 0)),
        ],
        out_specs=(anyw,) * (len(PORT) + 1),
        scratch_shapes=[pltpu.VMEM((16, 4, r, 128), f32) for _, r, _, _ in PORT]
        + [pltpu.VMEM((16, n, 128), f32) for _, r, h, _ in PORT[N_BULK:] for n in (h, r - h, r, r)]
        + [pltpu.VMEM((16, 2, 4, 8, 128), f32), pltpu.VMEM((16, 4, 8, 128), f32)]
        + [pltpu.VMEM((16, 8, 128), f32)] * 3
        + [
            pltpu.VMEM((16, 2, 4, max(a + r for a, r, _, _ in PORT), 128), f32),
            pltpu.VMEM((f_count, emb), f32),
            pltpu.VMEM((rank, samples), bf16),
            pltpu.VMEM((rank // 128 * width, 128), f32),
            pltpu.VMEM((per * rank, 128), f32),
            pltpu.VMEM((1, width), f32),
            pltpu.VMEM((blocks * samples, emb), f32),
            pltpu.VMEM((tables, 1, samples), i32),
            pltpu.SemaphoreType.DMA((24,)),
            pltpu.SemaphoreType.DMA((24,)),
            pltpu.SemaphoreType.DMA((16,)),
        ],
        compiler_params=params(collective_id=1, has_side_effects=True),
        name="weights_kernel",
    )(hidden, back_low, cross_in, cotangent, values, place_t)

    new_frequent, new_frequent_accum, new_shard, new_shard_accum, grad_up, grad_down, grad_bias = reduce_all(
        parts, arrived, frequent_table, frequent_accum, shard_table, shard_accum, count, width, rank
    )
    new_frequent_accum, new_shard_accum = new_frequent_accum.reshape(-1), new_shard_accum.reshape(-1)
    grad_bias = grad_bias.reshape(-1)
    return (new_frequent, new_frequent_accum, new_shard, new_shard_accum, grad_up, grad_down, grad_bias)


def solution(mesh):
    both = ("dp", "rep")
    in_specs = (P(both, None), P(both, None), P(), P(), P(), P(both, None), P(), P(), P("dp", None), P("dp"))
    out_specs = (P(), P(), P("dp", None), P("dp"), P(both, None), P(both, None), P(both))
    return jax.shard_map(body, mesh=mesh, in_specs=in_specs, out_specs=out_specs, check_vma=False)
```

```python
import functools
import jax
import jax.numpy as jnp
from jax import lax
from jax.experimental import pallas as pl
from jax.experimental.pallas import tpu as pltpu
from jax.sharding import PartitionSpec as P

learn_rate = 0.05
eps_ada = 1e-08
f32, bf16, i32 = jnp.float32, jnp.bfloat16, jnp.int32
VLIM = 66 * 1000 * 1000


def row_adagrad(table, accum, grad_of, new, new_accum):
    def chunk(n, _):
        at = pl.ds(pl.multiple_of(n * 128, 128), 128)
        g = grad_of(n)
        before = jnp.broadcast_to(accum[pl.ds(n, 1), :], (128, 128)).T
        after = before + jnp.mean(g * g, axis=1, keepdims=True)
        new[at, :] = table[at, :] - learn_rate * g / (jnp.sqrt(after) + eps_ada)
        new_accum[pl.ds(n, 1), :] = after.T[0:1, :]
        return 0

    lax.fori_loop(0, table.shape[0] // 128, chunk, 0)


def move_kernel(*refs):
    n = len(refs) // 3
    src, dst, held, sems = refs[:n], refs[n : 2 * n], refs[2 * n : 3 * n], refs[3 * n]
    takes = [pltpu.make_async_copy(a, b, sems.at[0, i]) for i, (a, b) in enumerate(zip(src, held))]
    gives = [pltpu.make_async_copy(a, b, sems.at[1, i]) for i, (a, b) in enumerate(zip(held, dst))]
    for c in takes:
        c.start()
    for c, d in zip(takes, gives):
        c.wait()
        d.start()
    for d in gives:
        d.wait()


def dot_nt(a, b):
    return lax.dot_general(a, b, (((1,), (1,)), ((), ())), preferred_element_type=f32)


def dot_tn(a, b):
    return lax.dot_general(a, b, (((0,), (0,)), ((), ())), preferred_element_type=f32)


def hi_lo(v):
    hi = v.astype(bf16)
    lo = (v - hi.astype(f32)).astype(bf16)
    return jnp.concatenate([hi, lo], axis=1)


def one_hot(flags):
    return jnp.where(flags, 1.0, 0.0).astype(bf16)


def index_work(frequent, owned, place, idx, row_a, row_b, hot, cum):
    tables, samples = place.shape
    owners, slots = idx.shape[0], 256
    at = lax.broadcasted_iota(i32, (1, samples), 1)
    owner_iota = lax.broadcasted_iota(i32, (owners, samples), 0)
    tri = one_hot(
        lax.broadcasted_iota(i32, (samples, samples), 0)
        < lax.broadcasted_iota(i32, (samples, samples), 1)
    )
    shift = owned.bit_length() - 1
    for t in range(tables):
        owner = lax.shift_right_arithmetic(place[t : t + 1, :] - frequent, shift)
        hot[t * owners : (t + 1) * owners, :] = one_hot(owner_iota == owner)
    cum[...] = jnp.dot(hot[...], tri, preferred_element_type=f32)
    base = jnp.zeros((owners, 1), f32)
    total = jnp.zeros((4 * owners, slots), f32)
    slot_iota = lax.broadcasted_iota(i32, (slots, samples), 0)
    at_hi = lax.shift_right_logical(at, 7).astype(f32)
    at_lo = (at & 127).astype(f32)
    blocks = samples // 128
    for t in range(tables):
        mine = hot[t * owners : (t + 1) * owners, :].astype(f32)
        before = cum[t * owners : (t + 1) * owners, :] + base
        rank = jnp.sum(mine * before, axis=0, keepdims=True).astype(i32)
        base = before[:, samples - 1 :] + mine[:, samples - 1 :]
        local = (place[t : t + 1, :] - frequent) & (owned - 1)
        parts = [
            mine * (at_hi + float((t + 1) * blocks)),
            mine * at_lo,
            mine * (lax.shift_right_logical(local, 7) + 1).astype(f32),
            mine * (local & 127).astype(f32),
        ]
        left = jnp.concatenate(parts, axis=0).astype(bf16)
        total = total + dot_nt(left, one_hot(slot_iota == rank))
    found = (total[:owners] * 128.0 + total[owners : 2 * owners]).astype(i32)
    idx[:, 0, :] = found[:, :128]
    idx[:, 1, :] = found[:, 128:]
    row = (total[2 * owners : 3 * owners] - 1.0) * 128.0 + total[3 * owners :]
    row_a[...] = row[:, :128]
    row_b[...] = row[:, 128:]


def front_kernel(
    frequent, owned, place, bias, cross_hbm, cot_hbm, down_hbm, up_hbm,
    hidden, back_low, values_hbm, bucket_hbm,
    cross, cot, down, up, values, bucket, hot, cum, idx_v, row_a, row_b, idx, h_acc, b_acc, in_sems, v_sems, b_sems, i_sem,
):
    samples = hidden.shape[0]
    emb = values.shape[1]
    pieces = in_sems.shape[0]
    steps = v_sems.shape[0]
    wide = cross.shape[1] // steps
    thin = cross.shape[1] // pieces
    per = wide // emb
    owners = bucket.shape[0]
    slots = bucket.shape[1] - 8

    def loads(g):
        cols = pl.ds(pl.multiple_of(g * thin, 128), thin)
        return [
            pltpu.make_async_copy(cross_hbm.at[:, cols], cross.at[:, cols], in_sems.at[g, 0]),
            pltpu.make_async_copy(cot_hbm.at[:, cols], cot.at[:, cols], in_sems.at[g, 1]),
            pltpu.make_async_copy(down_hbm.at[cols, :], down.at[cols, :], in_sems.at[g, 2]),
            pltpu.make_async_copy(up_hbm.at[:, cols], up.at[:, cols], in_sems.at[g, 3]),
        ]

    for g in range(pieces):
        for c in loads(g):
            c.start()
    index_work(frequent, owned, place, idx_v, row_a, row_b, hot, cum)
    to_scalar = pltpu.make_async_copy(idx_v, idx, i_sem)
    to_scalar.start()
    h_acc[...] = jnp.zeros_like(h_acc)
    b_acc[...] = jnp.zeros_like(b_acc)

    def low(g, _):
        for n in range(pieces // steps):
            for c in loads(g * (pieces // steps) + n):
                c.wait()
        cols = pl.ds(pl.multiple_of(g * wide, wide), wide)
        x = cross[:, cols]
        inner = (cot[:, cols].astype(f32) * x.astype(f32)).astype(bf16)
        h_acc[...] += jnp.dot(x, down[cols, :], preferred_element_type=f32)
        b_acc[...] += dot_nt(inner, up[:, cols])
        return 0

    lax.fori_loop(0, steps, low, 0)
    hidden[...] = h_acc[...].astype(bf16)
    back_low[...] = b_acc[...].astype(bf16)

    def store(g):
        part = pl.ds(pl.multiple_of(g * per * samples, 128), per * samples)
        return pltpu.make_async_copy(values.at[part], values_hbm.at[part], v_sems.at[g])

    def high(g, _):
        cols = pl.ds(pl.multiple_of(g * wide, wide), wide)
        scaled = jnp.dot(hidden[...], up[:, cols], preferred_element_type=f32) + bias[cols].reshape(1, wide)
        v = cot[:, cols].astype(f32) * (scaled + 1.0) + dot_nt(back_low[...], down[cols, :])
        for k in range(per):
            values[pl.ds(pl.multiple_of((g * per + k) * samples, 128), samples), :] = v[:, k * emb : (k + 1) * emb]
        store(g).start()
        return 0

    lax.fori_loop(0, steps, high, 0)
    to_scalar.wait()

    def ship(o):
        return pltpu.make_async_copy(bucket.at[o], bucket_hbm.at[o], b_sems.at[o])

    def pick(o, _):
        for k in range(slots):
            src = idx[o, k // 128, k % 128]
            bucket[o, k : k + 1, :] = values[pl.ds(src, 1), :]
        bucket[o, slots : slots + 8, :] = jnp.zeros((8, emb), f32)
        bucket[o, slots : slots + 1, :] = row_a[pl.ds(o, 1), :]
        bucket[o, slots + 1 : slots + 2, :] = row_b[pl.ds(o, 1), :]
        ship(o).start()
        return 0

    lax.fori_loop(0, owners, pick, 0)
    lax.fori_loop(0, steps, lambda g, _: (store(g).wait(), 0)[1], 0)
    lax.fori_loop(0, owners, lambda o, _: (ship(o).wait(), 0)[1], 0)


PORT = (
    (104, 32, 16, "xzy"),
    (136, 24, 16, "xzy"),
    (160, 32, 16, "zxy"),
    (192, 32, 16, "zxy"),
    (72, 32, 16, "yxz"),
    (0, 40, 24, "yxz"),
    (40, 32, 16, "yzx"),
)
N_BULK = 5
BEGINS = [1 if p >= N_BULK else 0 for p in range(len(PORT))]


def mesh_place():
    dp, y = lax.axis_index("dp"), lax.axis_index("rep")
    core = dp % 2
    return {"x": dp // 8, "z": (dp // 2) % 4, "y": y}, core, (dp + 1 - 2 * core, y)


class Links:
    def __init__(self, send_sems, recv_sems):
        self.sems, self.used, self.sent = (send_sems, recv_sems), 0, []

    def base(self, n):
        self.used += n
        return self.used - n

    def make(self, k, src, dst, to):
        return pltpu.make_async_remote_copy(
            src_ref=src, dst_ref=dst, send_sem=self.sems[0].at[k], recv_sem=self.sems[1].at[k],
            device_id=to, device_id_type=pl.DeviceIdType.MESH,
        )

    def go(self, k, src, dst, to):
        copy = self.make(k, src(), dst, to())
        copy.start()
        self.sent.append(lambda: self.make(k, src(), dst, to()))
        return copy

    def __call__(self, src, dst, to):
        return self.go(self.base(1), lambda: src, dst, lambda: to)


class Reduce:
    def __init__(self, links, near, at, add, rows, half, lands):
        (_, up, far, down), to = near
        self.links, self.here, self.up, self.down = links, near[0][0], up, down
        self.at, self.add, self.rows, self.half, self.lands = at, add, rows, half, lands
        k = links.base(4)
        self.args = [
            (k, lambda: at(far, 0, half), lands[0], lambda: to[up]),
            (k + 1, lambda: at(far, half, rows), lands[1], lambda: to[down]),
            (k + 2, lambda: at(up, 0, rows), lands[2], lambda: to[up]),
            (k + 3, lambda: at(down, 0, rows), lands[3], lambda: to[down]),
        ]

    def go(self, i):
        k, src, dst, to = self.args[i]
        self.links.go(k, src, dst, to)

    def got(self, i):
        k, src, dst, to = self.args[i]
        self.links.make(k, src(), dst, to()).wait_recv()

    def start(self):
        self.go(0)
        self.go(1)

    def middle(self):
        self.got(0)
        self.add(self.up, 0, self.half, self.lands[:1])
        self.go(2)
        self.got(1)
        self.add(self.down, self.half, self.rows, self.lands[1:2])
        self.go(3)

    def finish(self):
        self.got(2)
        self.got(3)
        self.add(self.here, 0, self.rows, self.lands[2:4])


class Direct:
    def __init__(self, send, near, at, add, lands):
        self.send, self.near, self.at, self.add, self.lands = send, near, at, add, lands

    def start(self):
        places, to = self.near
        self.got = [self.send(self.at(places[d]), self.lands[d - 1], to[places[d]]) for d in (1, 3, 2)]

    def finish(self):
        for c in self.got:
            c.wait_recv()
        self.add(self.near[0][0], self.lands)


class Spread:
    def __init__(self, send, near, at):
        self.send, self.near, self.at = send, near, at

    def start(self):
        places, to = self.near
        src = self.at(places[0])
        self.got = [self.send(src, src, to[places[d]]) for d in (1, 3, 2)]

    def finish(self):
        for c in self.got:
            c.wait_recv()


class Ids:
    def __init__(self, make):
        self.make = make

    def __getitem__(self, t):
        return self.make(t)


def neighbours(me, core, axis):
    def device(to):
        at = dict(me, **{axis: to})
        return ((at["x"] * 4 + at["z"]) * 2 + core, at["y"])

    return [(me[axis] + d) % 4 for d in range(4)], Ids(device)


def greet(peers, meanwhile=lambda: None):
    barrier = pltpu.get_barrier_semaphore()
    for peer in peers:
        pl.semaphore_signal(barrier, inc=1, device_id=peer, device_id_type=pl.DeviceIdType.MESH)
    meanwhile()
    pl.semaphore_wait(barrier, len(peers))


def weights_kernel(steps, hidden, back_low, cross, cot, values_hbm, place_in, *rest):
    outs, rest = rest[: len(PORT)], rest[len(PORT) :]
    freq_out, rest = rest[0], rest[1:]
    pair, rest = rest[: len(PORT)], rest[len(PORT) :]
    y_land, rest = [rest[:4], rest[4:8]], rest[8:]
    f_both, f_pair, f_land, rest = rest[0], rest[1], rest[2:5], rest[5:]
    both, freq, hidden_t, down, up, bias, values, place, send_sems, recv_sems, local_sems = rest
    g = pl.program_id(0)
    rank = hidden.shape[1]
    wide = cross.shape[1]
    per = wide // 128
    frequent = freq.shape[0]
    samples = hidden.shape[0]
    count = frequent // 8
    width = wide * steps
    cols = per * steps
    up_rows = rank // count
    down_rows = width // count
    base = up_rows * cols
    bias_at = base + down_rows * rank // 128
    me, core, partner = mesh_place()
    near = neighbours(me, core, "y")
    load = pltpu.make_async_copy(values_hbm, values, local_sems.at[0])

    send = Links(send_sems, recv_sems)
    firsts = range(N_BULK, len(PORT))

    def part(p, c):
        first, rows = PORT[p][0], PORT[p][1]
        return both.at[:, c, :, pl.ds(first, rows), :]

    pair_base = send.base(len(PORT))
    pair_args = lambda p: (pair_base + p, lambda: part(p, 1 - core), pair[p], lambda: partner)

    def add_pair(p):
        first, rows = PORT[p][0], PORT[p][1]
        k, src, dst, to = pair_args(p)
        send.make(k, src(), dst, to()).wait_recv()

        def add(n, _):
            for y in range(4):
                both[n, core, y, first : first + rows, :] = both[n, core, y, first : first + rows, :] + pair[p][n, y]
            return 0

        lax.fori_loop(0, count // 8, add, 0)

    def y_phase(p):
        first, rows, half, _ = PORT[p]

        def at(t, lo, hi):
            return both.at[:, core, t, pl.ds(first + lo, hi - lo), :]

        def y_add(t, lo, hi, lands):
            def add(n, _):
                v = both[n, core, t, first + lo : first + hi, :]
                for ref in lands:
                    v = v + ref[n]
                both[n, core, t, first + lo : first + hi, :] = v
                return 0

            lax.fori_loop(0, count // 8, add, 0)

        return Reduce(send, near, at, y_add, rows, half, y_land[p - N_BULK])

    y_sums = {p: y_phase(p) for p in firsts}

    @pl.when(g == 0)
    def _():
        greet([partner] + [near[1][t] for t in near[0][1:]])
        load.start()
        hidden_t[...] = hidden[...].T
        for t in range(place.shape[0]):
            place[t] = place_in[t : t + 1, :]
        freq[...] = jnp.zeros_like(freq)

    inner = cot[...].astype(f32) * cross[...].astype(f32)
    bias[:, pl.ds(pl.multiple_of(g * wide, wide), wide)] = jnp.sum(inner, axis=0, keepdims=True)
    u = jnp.dot(hidden_t[...], inner.astype(bf16), preferred_element_type=f32)
    for k in range(per):
        up[k * rank : (k + 1) * rank, :] = u[:, k * 128 : (k + 1) * 128]
    d = dot_tn(cross[...], back_low[...])
    for k in range(rank // 128):
        down[pl.ds(pl.multiple_of(k * width + g * wide, 128), wide), :] = d[:, k * 128 : (k + 1) * 128]

    def put_up(n, _):
        for c in range(2):
            for y in range(4):
                i = n * 8 + c * 4 + y
                for k in range(per):
                    both[n, c, y, pl.ds(g * per + k, up_rows, stride=cols), :] = up[
                        pl.ds(k * rank + i * up_rows, up_rows), :
                    ]
        return 0

    lax.fori_loop(0, count // 8, put_up, 0)

    @pl.when(g == steps - 1)
    def _():
        for p in firsts:
            send.go(*pair_args(p))

        def put_down(n, _):
            for c in range(2):
                for y in range(4):
                    i = n * 8 + c * 4 + y
                    for k in range(rank // 128):
                        both[n, c, y, pl.ds(base + k, down_rows, stride=rank // 128), :] = down[
                            pl.ds(k * width + i * down_rows, down_rows), :
                        ]
                    both[n, c, y, bias_at : bias_at + 8, :] = jnp.zeros((8, 128), f32)
            return 0

        lax.fori_loop(0, count // 8, put_down, 0)
        for i in range(count):
            both[i // 8, (i // 4) % 2, i % 4, bias_at : bias_at + 1, 0:down_rows] = bias[
                :, i * down_rows : (i + 1) * down_rows
            ]
        for p in range(N_BULK):
            send.go(*pair_args(p))
        load.wait()
        row_iota = lax.broadcasted_iota(i32, (frequent, samples), 0)

        def tables(t, _):
            hots, parts = [], []
            for k in range(2):
                hots.append(one_hot(row_iota == place[2 * t + k]))
                parts.append(hi_lo(values[pl.ds(pl.multiple_of((2 * t + k + 1) * samples, 128), samples), :]))
            s = jnp.dot(jnp.concatenate(hots, axis=1), jnp.concatenate(parts, axis=0), preferred_element_type=f32)
            freq[...] += s[:, :128] + s[:, 128:]
            return 0

        def f_add(t, lands):
            v = f_both[:, core, t]
            for ref in lands:
                v = v + ref[...]
            f_both[:, core, t] = v

        f_sum = Direct(send, near, lambda t: f_both.at[:, core, t], f_add, f_land)
        pairs = place.shape[0] // 2
        lax.fori_loop(0, 2, tables, 0)
        for p in firsts:
            add_pair(p)
            y_sums[p].start()
        lax.fori_loop(2, pairs // 2 + 2, tables, 0)
        y_sums[N_BULK].middle()
        lax.fori_loop(pairs // 2 + 2, pairs, tables, 0)
        y_sums[N_BULK + 1].middle()

        def put_freq(n, _):
            for c in range(2):
                for y in range(4):
                    f_both[n, c, y] = freq[pl.ds(pl.multiple_of((n * 8 + c * 4 + y) * 8, 8), 8), :]
            return 0

        lax.fori_loop(0, count // 8, put_freq, 0)
        f_got = send(f_both.at[:, 1 - core], f_pair, partner)
        stores = []
        for p in range(N_BULK):
            add_pair(p)
            stores.append(pltpu.make_async_copy(part(p, core), outs[p], local_sems.at[1 + p]))
            stores[-1].start()
        f_got.wait_recv()
        f_both[:, core] = f_both[:, core] + f_pair[...]
        f_sum.start()
        for p in firsts:
            y_sums[p].finish()
            stores.append(pltpu.make_async_copy(y_sums[p].at(me["y"], 0, PORT[p][1]), outs[p], local_sems.at[1 + p]))
            stores[-1].start()
        f_sum.finish()
        stores.append(pltpu.make_async_copy(f_both.at[:, core, me["y"]], freq_out, local_sems.at[1 + len(PORT)]))
        stores[-1].start()
        for c in stores:
            c.wait()
        for c in send.sent:
            c().wait_send()


def params(**kw):
    return pltpu.CompilerParams(vmem_limit_bytes=VLIM, **kw)


def reduce_kernel(*refs):
    it = iter(refs)
    take = lambda n: [next(it) for _ in range(n)]
    pieces = range(len(PORT))
    begins = BEGINS
    loads, (load_f, arrived), given = take(len(PORT)), take(2), take(4)
    new_f, new_fa, new_s, new_sa, g_up, g_down, g_bias = take(7)
    work = take(len(PORT))
    land = {p: {k: take(3 if k == 2 else 4) for k in range(begins[p], 3)} for p in pieces}
    swork, sland, sgath = next(it), [take(4), take(4)], next(it)
    f_work, fx_land, fz_land, gath = next(it), take(3), take(3), next(it)
    mine, arr, ids, right, acc = take(5)
    f_table, f_accum, s_table, s_accum = held = take(4)
    send_sems, recv_sems, local_sems = take(3)
    me, core, partner = mesh_place()
    near = {a: neighbours(me, core, a) for a in "xzy"}
    copies = [pltpu.make_async_copy(loads[p], work[p], local_sems.at[p]) for p in pieces]
    more = [(load_f, f_work), (arrived, arr)] + list(zip(given, held))
    copy_f, copy_a, *rest = [
        pltpu.make_async_copy(a, b, local_sems.at[len(PORT) + i]) for i, (a, b) in enumerate(more)
    ]

    def load_all():
        for c in [copy_f, copies[0], copies[2], copies[4], copy_a, copies[1], copies[3], copies[5], copies[6]] + rest:
            c.start()

    greet([partner] + [near[a][1][t] for a in "xzy" for t in near[a][0][1:]], load_all)
    send = Links(send_sems, recv_sems)

    def where(dims, done, axis, t, rem=None):
        rem = iter(rem) if rem is not None else None
        out = []
        for a in dims:
            if a in done:
                out.append(me[a])
            elif a == axis:
                out.append(t)
            else:
                out.append(slice(None) if rem is None else next(rem))
        return tuple(out)

    def phase(p, k):
        _, rows, half, order = PORT[p]
        dims = "xz" if begins[p] else "xzy"
        done, axis = order[begins[p] : k], order[k]
        ref, left = work[p], 2 - k

        def at(t, lo, hi):
            return ref.at[where(dims, done, axis, t) + (pl.ds(lo, hi - lo), slice(None))]

        def add(t, lo, hi, lands):
            def one(rem):
                spot = where(dims, done, axis, t, rem) + (slice(lo, hi), slice(None))
                v = ref[spot]
                for x in lands:
                    v = v + x[rem + (slice(None), slice(None))]
                ref[spot] = v

            if left == 0:
                one(())
            elif left == 1:
                lax.fori_loop(0, 4, lambda i, _: (one((i,)), 0)[1], 0)
            else:
                lax.fori_loop(0, 16, lambda i, _: (one((i // 4, i % 4)), 0)[1], 0)

        if k == 2:
            whole = lambda t: at(t, 0, rows)
            return Direct(send, near[axis], whole, lambda t, lands: add(t, 0, rows, lands), land[p][k])
        return Reduce(send, near[axis], at, add, rows, half, land[p][k])

    sums = {(p, k): phase(p, k) for p in pieces for k in range(begins[p], 3)}

    owned = swork.shape[1]

    part = owned // 2

    def s_phase(h):
        def at(t, lo, hi):
            return swork.at[t, pl.ds(h * part + lo, hi - lo), :]

        def add(t, lo, hi, lands):
            for r in range(lo, hi, 128):
                v = swork[t, h * part + r : h * part + r + 128, :]
                for ref in lands:
                    v = v + ref[r - lo : r - lo + 128, :]
                swork[t, h * part + r : h * part + r + 128, :] = v

        return Reduce(send, near["y"], at, add, part, part // 2, sland[h])

    s_red = [s_phase(0), s_phase(1)]

    def f_add(spot, lands):
        v = f_work[spot]
        for ref in lands:
            v = v + ref[...]
        f_work[spot] = v

    f_x = Direct(send, near["x"], lambda t: f_work.at[t], lambda t, l: f_add((t,), l), fx_land)
    f_z = Direct(
        send, near["z"], lambda t: f_work.at[me["x"], t], lambda t, l: f_add((me["x"], t), l), fz_land
    )
    g_z = Spread(send, near["z"], lambda t: gath.at[me["x"], t, core, me["y"]])
    g_x = Spread(send, near["x"], lambda t: gath.at[t, :, core, me["y"]])
    g_y = Spread(send, near["y"], lambda t: gath.at[:, :, core, t])

    class SegGather:
        def __init__(self, h):
            self.first = h * part

        def at(self, t, lo, hi):
            return sgath.at[t, pl.ds(self.first + lo, hi - lo), :]

        def start(self):
            (here, up, far, down), to = near["y"]
            spot = (here, slice(self.first, self.first + part), slice(None))
            sgath[spot] = swork[spot]
            src = self.at(here, 0, part)
            self.c0, self.c1 = send(src, src, to[up]), send(src, src, to[down])

        def middle(self):
            (here, up, far, down), to = near["y"]
            self.c0.wait_recv()
            src = self.at(down, 0, part // 2)
            self.c2 = send(src, src, to[up])
            self.c1.wait_recv()
            src = self.at(up, part // 2, part)
            self.c3 = send(src, src, to[down])

        def finish(self):
            self.c2.wait_recv()
            self.c3.wait_recv()

    s_gat = [SegGather(0), SegGather(1)]
    slots = arr.shape[1] - 8
    some = ids.shape[0]
    each_of = arr.shape[0] // some
    chunk = each_of * slots

    def prepare(g, _):
        rows = []
        for b in range(each_of):
            n = g * each_of + b
            rows.append(arr[n, slots : slots + 1, :])
            rows.append(arr[n, slots + 1 : slots + 2, : slots - 128])
            right[pl.ds(pl.multiple_of(n * slots, 16), slots), :] = hi_lo(arr[n, :slots, :])
        ids[g] = jnp.concatenate(rows, axis=1).astype(i32)
        return 0

    def seg_block(t):
        acc[...] = jnp.zeros_like(acc)
        first = t * owned

        def one(g, _):
            hot = one_hot(lax.broadcasted_iota(i32, (owned, chunk), 0) + first == ids[g])
            acc[...] += jnp.dot(
                hot, right[pl.ds(pl.multiple_of(g * chunk, 16), chunk), :], preferred_element_type=f32
            )
            return 0

        lax.fori_loop(0, some, one, 0)
        swork[t] = acc[:, :128] + acc[:, 128:]

    _, y_up, y_far, y_down = near["y"][0]
    def done(p, k):
        sums[p, k].finish()
        if k < 2:
            sums[p, k + 1].start()

    copy_f.wait()
    f_x.start()
    for p in (0, 2, 4, 1, 3):
        copies[p].wait()
        sums[p, 0].start()
    copy_a.wait()
    lax.fori_loop(0, some, prepare, 0)
    f_x.finish()
    f_z.start()
    seg_block(y_far)
    s_red[0].start()
    s_red[1].start()
    sums[0, 0].middle()
    sums[2, 0].middle()
    sums[4, 0].middle()
    seg_block(y_up)
    sums[1, 0].middle()
    sums[3, 0].middle()
    for p in (5, 6):
        copies[p].wait()
        sums[p, 1].start()
    f_z.finish()
    gath[me["x"], me["z"], core, me["y"]] = f_work[me["x"], me["z"]]
    g_z.start()
    seg_block(y_down)
    s_red[0].middle()
    s_red[1].middle()
    seg_block(me["y"])
    done(4, 0)
    done(0, 0)
    done(2, 0)
    done(1, 0)
    done(3, 0)
    sums[5, 1].middle()
    sums[6, 1].middle()
    s_red[0].finish()
    s_gat[0].start()
    s_red[1].finish()
    s_gat[1].start()
    g_z.finish()
    g_x.start()
    for p in (4, 0, 2, 1, 3):
        sums[p, 1].middle()
    s_gat[0].middle()
    s_gat[1].middle()
    done(5, 1)
    done(6, 1)
    g_x.finish()
    g_y.start()
    for p in (4, 0, 2, 1, 3):
        done(p, 1)
    for c in rest:
        c.wait()
    s_gat[0].finish()
    s_gat[1].finish()
    row_adagrad(s_table, s_accum, lambda n: sgath[n // 4, pl.ds(pl.multiple_of(n % 4 * 128, 128), 128), :], new_s, new_sa)
    g_y.finish()
    g_c = send(gath.at[:, :, core], gath.at[:, :, core], partner)
    here = (me["x"], me["z"], me["y"])
    for p in (5, 6, 4, 0, 2, 1, 3):
        sums[p, 2].finish()
        first, rows = PORT[p][:2]
        mine[first : first + rows, :] = work[p][here[:2] if begins[p] else here]
    g_c.wait_recv()
    row_adagrad(f_table, f_accum, lambda n: gath[n // 2, pl.ds(n % 2 * 2, 2)].reshape(128, 128), new_f, new_fa)
    up_rows, down_rows = g_up.shape[0], g_down.shape[0]
    cols = g_up.shape[1] // 128
    for c in range(cols):
        g_up[:, c * 128 : (c + 1) * 128] = mine[pl.ds(c, up_rows, stride=cols), :]
    first, cols = up_rows * cols, g_down.shape[1] // 128
    for c in range(cols):
        g_down[:, c * 128 : (c + 1) * 128] = mine[pl.ds(first + c, down_rows, stride=cols), :]
    g_bias[...] = mine[first + down_rows * cols : first + down_rows * cols + 1, 0:down_rows]
    for c in send.sent:
        c().wait_send()


def reduce_scratch(owned, frequent, arrived):
    v = lambda *s: pltpu.VMEM(s, f32)
    begins = BEGINS
    out = [v(*(4,) * (3 - b), r, 128) for b, (_, r, _, _) in zip(begins, PORT)]
    for b, (_, r, h, _) in zip(begins, PORT):
        for k in range(b, 3):
            lead = (4,) * (2 - k)
            out += [v(*lead, n, 128) for n in ((r, r, r) if k == 2 else (h, r - h, r, r))]
    q = owned // 4
    out += [v(4, q, 128)] + [v(q // 4, 128), v(q // 4, 128), v(q // 2, 128), v(q // 2, 128)] * 2 + [v(4, q, 128)]
    out += [v(4, 4, 8, 128)] + [v(4, 8, 128)] * 3 + [v(8, 128)] * 3 + [v(4, 4, 2, 4, 8, 128)]
    n = arrived.shape[0] // 16
    flat = arrived.shape[0] * (arrived.shape[1] - 8)
    out += [v(max(a + r for a, r, _, _ in PORT), 128)]
    out += [v(*arrived.shape), pltpu.VMEM((n, 1, flat // n), i32), pltpu.VMEM((flat, 256), bf16), v(q, 256)]
    out += [v(frequent, 128), v(frequent // 128, 128), v(owned, 128), v(owned // 128, 128)]
    out += [pltpu.SemaphoreType.DMA((112,)), pltpu.SemaphoreType.DMA((112,)), pltpu.SemaphoreType.DMA((16,))]
    return out


def reduce_all(parts, arrived, f_table, f_accum, s_table, s_accum, count, width, rank):
    vmem = pl.BlockSpec(memory_space=pltpu.VMEM)
    anyw = pl.BlockSpec(memory_space=pl.ANY)
    frequent, owned = f_table.shape[0], s_table.shape[0]
    given = [f_table, f_accum.reshape(-1, 128), s_table, s_accum.reshape(-1, 128)]
    shapes = [g.shape for g in given] + [(rank // count, width), (width // count, rank), (1, width // count)]
    shapes = [jax.ShapeDtypeStruct(shape, f32) for shape in shapes]
    outs = pl.pallas_call(
        reduce_kernel,
        out_shape=tuple(shapes),
        in_specs=[anyw] * (len(PORT) + 6),
        out_specs=(vmem,) * 7,
        scratch_shapes=reduce_scratch(owned, frequent, arrived),
        compiler_params=params(collective_id=0, has_side_effects=True),
        name="reduce_kernel",
    )(*[w.reshape(4, 4, *w.shape[1:]) for w in parts], arrived, *given)
    return pl.pallas_call(
        move_kernel,
        out_shape=tuple(shapes),
        in_specs=[anyw] * 7,
        out_specs=(anyw,) * 7,
        scratch_shapes=[pltpu.VMEM(x.shape, f32) for x in shapes] + [pltpu.SemaphoreType.DMA((2, 7))],
        compiler_params=params(),
        name="move_kernel",
    )(*outs)


def body(cross_in, cotangent, weight_down, weight_up, cross_bias, row_place, frequent_table, frequent_accum, shard_table, shard_accum):
    samples, width = cross_in.shape
    rank = weight_down.shape[1]
    tables = row_place.shape[1]
    emb = frequent_table.shape[1]
    f_count = frequent_table.shape[0]
    owned = shard_table.shape[0]
    shards = lax.axis_size("dp")
    count = shards * lax.axis_size("rep")
    capacity = samples * tables // (2 * shards)
    blocks = width // emb
    per = 3
    steps = blocks // per
    wide = per * emb
    vmem = pl.BlockSpec(memory_space=pltpu.VMEM)

    place_t = row_place.T
    anyw = pl.BlockSpec(memory_space=pl.ANY)
    hidden, back_low, values, bucket = pl.pallas_call(
        functools.partial(front_kernel, f_count, owned),
        out_shape=(
            jax.ShapeDtypeStruct((samples, rank), bf16),
            jax.ShapeDtypeStruct((samples, rank), bf16),
            jax.ShapeDtypeStruct((blocks * samples, emb), f32),
            jax.ShapeDtypeStruct((shards, capacity + 8, emb), f32),
        ),
        in_specs=[vmem, vmem, anyw, anyw, anyw, anyw],
        out_specs=(vmem, vmem, anyw, anyw),
        scratch_shapes=[
            pltpu.VMEM((samples, width), bf16),
            pltpu.VMEM((samples, width), bf16),
            pltpu.VMEM((width, rank), bf16),
            pltpu.VMEM((rank, width), bf16),
            pltpu.VMEM((blocks * samples, emb), f32),
            pltpu.VMEM((shards, capacity + 8, emb), f32),
            pltpu.VMEM((tables * shards, samples), bf16),
            pltpu.VMEM((tables * shards, samples), f32),
            pltpu.VMEM((shards, 2, 128), i32),
            pltpu.VMEM((shards, 128), f32),
            pltpu.VMEM((shards, 128), f32),
            pltpu.SMEM((shards, 2, 128), i32),
            pltpu.VMEM((samples, rank), f32),
            pltpu.VMEM((samples, rank), f32),
            pltpu.SemaphoreType.DMA((steps, 4)),
            pltpu.SemaphoreType.DMA((3,)),
            pltpu.SemaphoreType.DMA((shards,)),
            pltpu.SemaphoreType.DMA,
        ],
        compiler_params=params(),
        name="front_kernel",
    )(place_t, cross_bias, cross_in, cotangent, weight_down, weight_up)

    arrived = lax.all_to_all(bucket, "dp", split_axis=0, concat_axis=0, tiled=True)

    parts = pl.pallas_call(
        functools.partial(weights_kernel, steps),
        grid=(steps,),
        out_shape=tuple(
            jax.ShapeDtypeStruct(shape, f32)
            for shape in [(16, 4, r, 128) for _, r, _, _ in PORT[:N_BULK]]
            + [(16, r, 128) for _, r, _, _ in PORT[N_BULK:]]
            + [(16, 8, 128)]
        ),
        in_specs=[
            pl.BlockSpec((samples, rank), lambda g: (0, 0)),
            pl.BlockSpec((samples, rank), lambda g: (0, 0)),
            pl.BlockSpec((samples, wide), lambda g: (0, g)),
            pl.BlockSpec((samples, wide), lambda g: (0, g)),
            anyw,
            pl.BlockSpec((tables, samples), lambda g: (0, 0)),
        ],
        out_specs=(anyw,) * (len(PORT) + 1),
        scratch_shapes=[pltpu.VMEM((16, 4, r, 128), f32) for _, r, _, _ in PORT]
        + [pltpu.VMEM((16, n, 128), f32) for _, r, h, _ in PORT[N_BULK:] for n in (h, r - h, r, r)]
        + [pltpu.VMEM((16, 2, 4, 8, 128), f32), pltpu.VMEM((16, 4, 8, 128), f32)]
        + [pltpu.VMEM((16, 8, 128), f32)] * 3
        + [
            pltpu.VMEM((16, 2, 4, max(a + r for a, r, _, _ in PORT), 128), f32),
            pltpu.VMEM((f_count, emb), f32),
            pltpu.VMEM((rank, samples), bf16),
            pltpu.VMEM((rank // 128 * width, 128), f32),
            pltpu.VMEM((per * rank, 128), f32),
            pltpu.VMEM((1, width), f32),
            pltpu.VMEM((blocks * samples, emb), f32),
            pltpu.VMEM((tables, 1, samples), i32),
            pltpu.SemaphoreType.DMA((24,)),
            pltpu.SemaphoreType.DMA((24,)),
            pltpu.SemaphoreType.DMA((16,)),
        ],
        compiler_params=params(collective_id=1, has_side_effects=True),
        name="weights_kernel",
    )(hidden, back_low, cross_in, cotangent, values, place_t)

    new_frequent, new_frequent_accum, new_shard, new_shard_accum, grad_up, grad_down, grad_bias = reduce_all(
        parts, arrived, frequent_table, frequent_accum, shard_table, shard_accum, count, width, rank
    )
    new_frequent_accum, new_shard_accum = new_frequent_accum.reshape(-1), new_shard_accum.reshape(-1)
    grad_bias = grad_bias.reshape(-1)
    return (new_frequent, new_frequent_accum, new_shard, new_shard_accum, grad_up, grad_down, grad_bias)


def solution(mesh):
    both = ("dp", "rep")
    in_specs = (P(both, None), P(both, None), P(), P(), P(), P(both, None), P(), P(), P("dp", None), P("dp"))
    out_specs = (P(), P(), P("dp", None), P("dp"), P(both, None), P(both, None), P(both))
    return jax.shard_map(body, mesh=mesh, in_specs=in_specs, out_specs=out_specs, check_vma=False)
```

```python
import functools
import jax
import jax.numpy as jnp
from jax import lax
from jax.experimental import pallas as pl
from jax.experimental.pallas import tpu as pltpu
from jax.sharding import PartitionSpec as P

learn_rate = 0.05
eps_ada = 1e-08
f32, bf16, i32 = jnp.float32, jnp.bfloat16, jnp.int32
VLIM = 66 * 1000 * 1000


def row_adagrad(table, accum, grad_of, new, new_accum):
    def chunk(n, _):
        at = pl.ds(pl.multiple_of(n * 128, 128), 128)
        g = grad_of(n)
        before = jnp.broadcast_to(accum[pl.ds(n, 1), :], (128, 128)).T
        after = before + jnp.mean(g * g, axis=1, keepdims=True)
        new[at, :] = table[at, :] - learn_rate * g / (jnp.sqrt(after) + eps_ada)
        new_accum[pl.ds(n, 1), :] = after.T[0:1, :]
        return 0

    lax.fori_loop(0, table.shape[0] // 128, chunk, 0)


def move_kernel(*refs):
    n = len(refs) // 3
    src, dst, held, sems = refs[:n], refs[n : 2 * n], refs[2 * n : 3 * n], refs[3 * n]
    takes = [pltpu.make_async_copy(a, b, sems.at[0, i]) for i, (a, b) in enumerate(zip(src, held))]
    gives = [pltpu.make_async_copy(a, b, sems.at[1, i]) for i, (a, b) in enumerate(zip(held, dst))]
    for c in takes:
        c.start()
    for c, d in zip(takes, gives):
        c.wait()
        d.start()
    for d in gives:
        d.wait()


def dot_nt(a, b):
    return lax.dot_general(a, b, (((1,), (1,)), ((), ())), preferred_element_type=f32)


def dot_tn(a, b):
    return lax.dot_general(a, b, (((0,), (0,)), ((), ())), preferred_element_type=f32)


def hi_lo(v):
    hi = v.astype(bf16)
    lo = (v - hi.astype(f32)).astype(bf16)
    return jnp.concatenate([hi, lo], axis=1)


def one_hot(flags):
    return jnp.where(flags, 1.0, 0.0).astype(bf16)


def index_work(frequent, owned, place, idx, row_a, row_b, hot, cum):
    tables, samples = place.shape
    owners, slots = idx.shape[0], 256
    at = lax.broadcasted_iota(i32, (1, samples), 1)
    owner_iota = lax.broadcasted_iota(i32, (owners, samples), 0)
    tri = one_hot(
        lax.broadcasted_iota(i32, (samples, samples), 0)
        < lax.broadcasted_iota(i32, (samples, samples), 1)
    )
    shift = owned.bit_length() - 1
    for t in range(tables):
        owner = lax.shift_right_arithmetic(place[t : t + 1, :] - frequent, shift)
        hot[t * owners : (t + 1) * owners, :] = one_hot(owner_iota == owner)
    cum[...] = jnp.dot(hot[...], tri, preferred_element_type=f32)
    base = jnp.zeros((owners, 1), f32)
    total = jnp.zeros((4 * owners, slots), f32)
    slot_iota = lax.broadcasted_iota(i32, (slots, samples), 0)
    at_hi = lax.shift_right_logical(at, 7).astype(f32)
    at_lo = (at & 127).astype(f32)
    blocks = samples // 128
    for t in range(tables):
        mine = hot[t * owners : (t + 1) * owners, :].astype(f32)
        before = cum[t * owners : (t + 1) * owners, :] + base
        rank = jnp.sum(mine * before, axis=0, keepdims=True).astype(i32)
        base = before[:, samples - 1 :] + mine[:, samples - 1 :]
        local = (place[t : t + 1, :] - frequent) & (owned - 1)
        parts = [
            mine * (at_hi + float((t + 1) * blocks)),
            mine * at_lo,
            mine * (lax.shift_right_logical(local, 7) + 1).astype(f32),
            mine * (local & 127).astype(f32),
        ]
        left = jnp.concatenate(parts, axis=0).astype(bf16)
        total = total + dot_nt(left, one_hot(slot_iota == rank))
    found = (total[:owners] * 128.0 + total[owners : 2 * owners]).astype(i32)
    idx[:, 0, :] = found[:, :128]
    idx[:, 1, :] = found[:, 128:]
    row = (total[2 * owners : 3 * owners] - 1.0) * 128.0 + total[3 * owners :]
    row_a[...] = row[:, :128]
    row_b[...] = row[:, 128:]


def front_kernel(
    frequent, owned, place, bias, cross_hbm, cot_hbm, down_hbm, up_hbm,
    hidden, back_low, values_hbm, bucket_hbm,
    cross, cot, down, up, values, bucket, hot, cum, idx_v, row_a, row_b, idx, h_acc, b_acc, in_sems, v_sems, b_sems, i_sem,
):
    samples = hidden.shape[0]
    emb = values.shape[1]
    pieces = in_sems.shape[0]
    steps = v_sems.shape[0]
    wide = cross.shape[1] // steps
    thin = cross.shape[1] // pieces
    per = wide // emb
    owners = bucket.shape[0]
    slots = bucket.shape[1] - 8

    def loads(g):
        cols = pl.ds(pl.multiple_of(g * thin, 128), thin)
        return [
            pltpu.make_async_copy(cross_hbm.at[:, cols], cross.at[:, cols], in_sems.at[g, 0]),
            pltpu.make_async_copy(cot_hbm.at[:, cols], cot.at[:, cols], in_sems.at[g, 1]),
            pltpu.make_async_copy(down_hbm.at[cols, :], down.at[cols, :], in_sems.at[g, 2]),
            pltpu.make_async_copy(up_hbm.at[:, cols], up.at[:, cols], in_sems.at[g, 3]),
        ]

    for g in range(pieces):
        for c in loads(g):
            c.start()
    index_work(frequent, owned, place, idx_v, row_a, row_b, hot, cum)
    to_scalar = pltpu.make_async_copy(idx_v, idx, i_sem)
    to_scalar.start()
    h_acc[...] = jnp.zeros_like(h_acc)
    b_acc[...] = jnp.zeros_like(b_acc)

    def low(g, _):
        for n in range(pieces // steps):
            for c in loads(g * (pieces // steps) + n):
                c.wait()
        cols = pl.ds(pl.multiple_of(g * wide, wide), wide)
        x = cross[:, cols]
        inner = (cot[:, cols].astype(f32) * x.astype(f32)).astype(bf16)
        h_acc[...] += jnp.dot(x, down[cols, :], preferred_element_type=f32)
        b_acc[...] += dot_nt(inner, up[:, cols])
        return 0

    lax.fori_loop(0, steps, low, 0)
    hidden[...] = h_acc[...].astype(bf16)
    back_low[...] = b_acc[...].astype(bf16)

    def store(g):
        part = pl.ds(pl.multiple_of(g * per * samples, 128), per * samples)
        return pltpu.make_async_copy(values.at[part], values_hbm.at[part], v_sems.at[g])

    def high(g, _):
        cols = pl.ds(pl.multiple_of(g * wide, wide), wide)
        scaled = jnp.dot(hidden[...], up[:, cols], preferred_element_type=f32) + bias[cols].reshape(1, wide)
        v = cot[:, cols].astype(f32) * (scaled + 1.0) + dot_nt(back_low[...], down[cols, :])
        for k in range(per):
            values[pl.ds(pl.multiple_of((g * per + k) * samples, 128), samples), :] = v[:, k * emb : (k + 1) * emb]
        store(g).start()
        return 0

    lax.fori_loop(0, steps, high, 0)
    to_scalar.wait()

    def ship(o):
        return pltpu.make_async_copy(bucket.at[o], bucket_hbm.at[o], b_sems.at[o])

    def pick(o, _):
        for k in range(slots):
            src = idx[o, k // 128, k % 128]
            bucket[o, k : k + 1, :] = values[pl.ds(src, 1), :]
        bucket[o, slots : slots + 8, :] = jnp.zeros((8, emb), f32)
        bucket[o, slots : slots + 1, :] = row_a[pl.ds(o, 1), :]
        bucket[o, slots + 1 : slots + 2, :] = row_b[pl.ds(o, 1), :]
        ship(o).start()
        return 0

    lax.fori_loop(0, owners, pick, 0)
    lax.fori_loop(0, steps, lambda g, _: (store(g).wait(), 0)[1], 0)
    lax.fori_loop(0, owners, lambda o, _: (ship(o).wait(), 0)[1], 0)


PORT = (
    (104, 32, 16, "xzy"),
    (136, 24, 16, "xzy"),
    (160, 32, 16, "zxy"),
    (192, 32, 16, "zxy"),
    (72, 32, 16, "yxz"),
    (0, 40, 24, "yxz"),
    (40, 32, 16, "yzx"),
)
N_BULK = 5
BEGINS = [1 if p >= N_BULK else 0 for p in range(len(PORT))]


def mesh_place():
    dp, y = lax.axis_index("dp"), lax.axis_index("rep")
    core = dp % 2
    return {"x": dp // 8, "z": (dp // 2) % 4, "y": y}, core, (dp + 1 - 2 * core, y)


class Links:
    def __init__(self, send_sems, recv_sems):
        self.sems, self.used, self.sent = (send_sems, recv_sems), 0, []

    def base(self, n):
        self.used += n
        return self.used - n

    def make(self, k, src, dst, to):
        return pltpu.make_async_remote_copy(
            src_ref=src, dst_ref=dst, send_sem=self.sems[0].at[k], recv_sem=self.sems[1].at[k],
            device_id=to, device_id_type=pl.DeviceIdType.MESH,
        )

    def go(self, k, src, dst, to):
        copy = self.make(k, src(), dst, to())
        copy.start()
        self.sent.append(lambda: self.make(k, src(), dst, to()))
        return copy

    def __call__(self, src, dst, to):
        return self.go(self.base(1), lambda: src, dst, lambda: to)


class Reduce:
    def __init__(self, links, near, at, add, rows, half, lands):
        (_, up, far, down), to = near
        self.links, self.here, self.up, self.down = links, near[0][0], up, down
        self.at, self.add, self.rows, self.half, self.lands = at, add, rows, half, lands
        k = links.base(4)
        self.args = [
            (k, lambda: at(far, 0, half), lands[0], lambda: to[up]),
            (k + 1, lambda: at(far, half, rows), lands[1], lambda: to[down]),
            (k + 2, lambda: at(up, 0, rows), lands[2], lambda: to[up]),
            (k + 3, lambda: at(down, 0, rows), lands[3], lambda: to[down]),
        ]

    def go(self, i):
        k, src, dst, to = self.args[i]
        self.links.go(k, src, dst, to)

    def got(self, i):
        k, src, dst, to = self.args[i]
        self.links.make(k, src(), dst, to()).wait_recv()

    def start(self):
        self.go(0)
        self.go(1)

    def middle(self):
        self.got(0)
        self.add(self.up, 0, self.half, self.lands[:1])
        self.go(2)
        self.got(1)
        self.add(self.down, self.half, self.rows, self.lands[1:2])
        self.go(3)

    def finish(self):
        self.got(2)
        self.got(3)
        self.add(self.here, 0, self.rows, self.lands[2:4])


class Direct:
    def __init__(self, send, near, at, add, lands):
        self.send, self.near, self.at, self.add, self.lands = send, near, at, add, lands

    def start(self):
        places, to = self.near
        self.got = [self.send(self.at(places[d]), self.lands[d - 1], to[places[d]]) for d in (1, 3, 2)]

    def finish(self):
        for c in self.got:
            c.wait_recv()
        self.add(self.near[0][0], self.lands)


class Spread:
    def __init__(self, send, near, at):
        self.send, self.near, self.at = send, near, at

    def start(self):
        places, to = self.near
        src = self.at(places[0])
        self.got = [self.send(src, src, to[places[d]]) for d in (1, 3, 2)]

    def finish(self):
        for c in self.got:
            c.wait_recv()


class Ids:
    def __init__(self, make):
        self.make = make

    def __getitem__(self, t):
        return self.make(t)


def neighbours(me, core, axis):
    def device(to):
        at = dict(me, **{axis: to})
        return ((at["x"] * 4 + at["z"]) * 2 + core, at["y"])

    return [(me[axis] + d) % 4 for d in range(4)], Ids(device)


def greet(peers, meanwhile=lambda: None):
    barrier = pltpu.get_barrier_semaphore()
    for peer in peers:
        pl.semaphore_signal(barrier, inc=1, device_id=peer, device_id_type=pl.DeviceIdType.MESH)
    meanwhile()
    pl.semaphore_wait(barrier, len(peers))


def weights_kernel(steps, hidden, back_low, cross, cot, values_hbm, place_in, *rest):
    outs, rest = rest[: len(PORT)], rest[len(PORT) :]
    freq_out, rest = rest[0], rest[1:]
    pair, rest = rest[: len(PORT)], rest[len(PORT) :]
    y_land, rest = [rest[:4], rest[4:8]], rest[8:]
    f_both, f_pair, f_land, rest = rest[0], rest[1], rest[2:5], rest[5:]
    both, freq, hidden_t, down, up, bias, values, place, send_sems, recv_sems, local_sems = rest
    g = pl.program_id(0)
    rank = hidden.shape[1]
    wide = cross.shape[1]
    per = wide // 128
    frequent = freq.shape[0]
    samples = hidden.shape[0]
    count = frequent // 8
    width = wide * steps
    cols = per * steps
    up_rows = rank // count
    down_rows = width // count
    base = up_rows * cols
    bias_at = base + down_rows * rank // 128
    me, core, partner = mesh_place()
    near = neighbours(me, core, "y")
    load = pltpu.make_async_copy(values_hbm, values, local_sems.at[0])

    send = Links(send_sems, recv_sems)
    firsts = range(N_BULK, len(PORT))

    def part(p, c):
        first, rows = PORT[p][0], PORT[p][1]
        return both.at[:, c, :, pl.ds(first, rows), :]

    pair_base = send.base(len(PORT))
    pair_args = lambda p: (pair_base + p, lambda: part(p, 1 - core), pair[p], lambda: partner)

    def add_pair(p):
        first, rows = PORT[p][0], PORT[p][1]
        k, src, dst, to = pair_args(p)
        send.make(k, src(), dst, to()).wait_recv()

        def add(n, _):
            for y in range(4):
                both[n, core, y, first : first + rows, :] = both[n, core, y, first : first + rows, :] + pair[p][n, y]
            return 0

        lax.fori_loop(0, count // 8, add, 0)

    def y_phase(p):
        first, rows, half, _ = PORT[p]

        def at(t, lo, hi):
            return both.at[:, core, t, pl.ds(first + lo, hi - lo), :]

        def y_add(t, lo, hi, lands):
            def add(n, _):
                v = both[n, core, t, first + lo : first + hi, :]
                for ref in lands:
                    v = v + ref[n]
                both[n, core, t, first + lo : first + hi, :] = v
                return 0

            lax.fori_loop(0, count // 8, add, 0)

        return Reduce(send, near, at, y_add, rows, half, y_land[p - N_BULK])

    y_sums = {p: y_phase(p) for p in firsts}

    @pl.when(g == 0)
    def _():
        greet([partner] + [near[1][t] for t in near[0][1:]])
        load.start()
        hidden_t[...] = hidden[...].T
        for t in range(place.shape[0]):
            place[t] = place_in[t : t + 1, :]
        freq[...] = jnp.zeros_like(freq)

    inner = cot[...].astype(f32) * cross[...].astype(f32)
    bias[:, pl.ds(pl.multiple_of(g * wide, wide), wide)] = jnp.sum(inner, axis=0, keepdims=True)
    u = jnp.dot(hidden_t[...], inner.astype(bf16), preferred_element_type=f32)
    for k in range(per):
        up[k * rank : (k + 1) * rank, :] = u[:, k * 128 : (k + 1) * 128]
    d = dot_tn(cross[...], back_low[...])
    for k in range(rank // 128):
        down[pl.ds(pl.multiple_of(k * width + g * wide, 128), wide), :] = d[:, k * 128 : (k + 1) * 128]

    def put_up(n, _):
        for c in range(2):
            for y in range(4):
                i = n * 8 + c * 4 + y
                for k in range(per):
                    both[n, c, y, pl.ds(g * per + k, up_rows, stride=cols), :] = up[
                        pl.ds(k * rank + i * up_rows, up_rows), :
                    ]
        return 0

    lax.fori_loop(0, count // 8, put_up, 0)

    @pl.when(g == steps - 1)
    def _():
        for p in firsts:
            send.go(*pair_args(p))

        def put_down(n, _):
            for c in range(2):
                for y in range(4):
                    i = n * 8 + c * 4 + y
                    for k in range(rank // 128):
                        both[n, c, y, pl.ds(base + k, down_rows, stride=rank // 128), :] = down[
                            pl.ds(k * width + i * down_rows, down_rows), :
                        ]
                    both[n, c, y, bias_at : bias_at + 8, :] = jnp.zeros((8, 128), f32)
            return 0

        lax.fori_loop(0, count // 8, put_down, 0)
        for i in range(count):
            both[i // 8, (i // 4) % 2, i % 4, bias_at : bias_at + 1, 0:down_rows] = bias[
                :, i * down_rows : (i + 1) * down_rows
            ]
        for p in range(N_BULK):
            send.go(*pair_args(p))
        load.wait()
        row_iota = lax.broadcasted_iota(i32, (frequent, samples), 0)

        def tables(t, _):
            hots, parts = [], []
            for k in range(2):
                hots.append(one_hot(row_iota == place[2 * t + k]))
                parts.append(hi_lo(values[pl.ds(pl.multiple_of((2 * t + k + 1) * samples, 128), samples), :]))
            s = jnp.dot(jnp.concatenate(hots, axis=1), jnp.concatenate(parts, axis=0), preferred_element_type=f32)
            freq[...] += s[:, :128] + s[:, 128:]
            return 0

        def f_add(t, lands):
            v = f_both[:, core, t]
            for ref in lands:
                v = v + ref[...]
            f_both[:, core, t] = v

        f_sum = Direct(send, near, lambda t: f_both.at[:, core, t], f_add, f_land)
        pairs = place.shape[0] // 2
        lax.fori_loop(0, 2, tables, 0)
        for p in firsts:
            add_pair(p)
            y_sums[p].start()
        lax.fori_loop(2, pairs // 2 + 2, tables, 0)
        y_sums[N_BULK].middle()
        lax.fori_loop(pairs // 2 + 2, pairs, tables, 0)
        y_sums[N_BULK + 1].middle()

        def put_freq(n, _):
            for c in range(2):
                for y in range(4):
                    f_both[n, c, y] = freq[pl.ds(pl.multiple_of((n * 8 + c * 4 + y) * 8, 8), 8), :]
            return 0

        lax.fori_loop(0, count // 8, put_freq, 0)
        f_got = send(f_both.at[:, 1 - core], f_pair, partner)
        stores = []
        for p in range(N_BULK):
            add_pair(p)
            stores.append(pltpu.make_async_copy(part(p, core), outs[p], local_sems.at[1 + p]))
            stores[-1].start()
        f_got.wait_recv()
        f_both[:, core] = f_both[:, core] + f_pair[...]
        f_sum.start()
        for p in firsts:
            y_sums[p].finish()
            stores.append(pltpu.make_async_copy(y_sums[p].at(me["y"], 0, PORT[p][1]), outs[p], local_sems.at[1 + p]))
            stores[-1].start()
        f_sum.finish()
        stores.append(pltpu.make_async_copy(f_both.at[:, core, me["y"]], freq_out, local_sems.at[1 + len(PORT)]))
        stores[-1].start()
        for c in stores:
            c.wait()
        for c in send.sent:
            c().wait_send()


def params(**kw):
    return pltpu.CompilerParams(vmem_limit_bytes=VLIM, **kw)


def reduce_kernel(*refs):
    it = iter(refs)
    take = lambda n: [next(it) for _ in range(n)]
    pieces = range(len(PORT))
    begins = BEGINS
    loads, (load_f, arrived), given = take(len(PORT)), take(2), take(4)
    new_f, new_fa, new_s, new_sa, g_up, g_down, g_bias = take(7)
    work = take(len(PORT))
    land = {p: {k: take(3 if k == 2 else 4) for k in range(begins[p], 3)} for p in pieces}
    swork, sland, sgath = next(it), [take(4), take(4)], next(it)
    f_work, fx_land, fz_land, gath = next(it), take(3), take(3), next(it)
    mine, arr, ids, right, acc = take(5)
    f_table, f_accum, s_table, s_accum = held = take(4)
    send_sems, recv_sems, local_sems = take(3)
    me, core, partner = mesh_place()
    near = {a: neighbours(me, core, a) for a in "xzy"}
    copies = [pltpu.make_async_copy(loads[p], work[p], local_sems.at[p]) for p in pieces]
    more = [(load_f, f_work), (arrived, arr)] + list(zip(given, held))
    copy_f, copy_a, *rest = [
        pltpu.make_async_copy(a, b, local_sems.at[len(PORT) + i]) for i, (a, b) in enumerate(more)
    ]

    def load_all():
        for c in [copy_f, copies[0], copies[2], copies[4], copy_a, copies[1], copies[3], copies[5], copies[6]] + rest:
            c.start()

    greet([partner] + [near[a][1][t] for a in "xzy" for t in near[a][0][1:]], load_all)
    send = Links(send_sems, recv_sems)

    def where(dims, done, axis, t, rem=None):
        rem = iter(rem) if rem is not None else None
        out = []
        for a in dims:
            if a in done:
                out.append(me[a])
            elif a == axis:
                out.append(t)
            else:
                out.append(slice(None) if rem is None else next(rem))
        return tuple(out)

    def phase(p, k):
        _, rows, half, order = PORT[p]
        dims = "xz" if begins[p] else "xzy"
        done, axis = order[begins[p] : k], order[k]
        ref, left = work[p], 2 - k

        def at(t, lo, hi):
            return ref.at[where(dims, done, axis, t) + (pl.ds(lo, hi - lo), slice(None))]

        def add(t, lo, hi, lands):
            def one(rem):
                spot = where(dims, done, axis, t, rem) + (slice(lo, hi), slice(None))
                v = ref[spot]
                for x in lands:
                    v = v + x[rem + (slice(None), slice(None))]
                ref[spot] = v

            if left == 0:
                one(())
            elif left == 1:
                lax.fori_loop(0, 4, lambda i, _: (one((i,)), 0)[1], 0)
            else:
                lax.fori_loop(0, 16, lambda i, _: (one((i // 4, i % 4)), 0)[1], 0)

        if k == 2:
            whole = lambda t: at(t, 0, rows)
            return Direct(send, near[axis], whole, lambda t, lands: add(t, 0, rows, lands), land[p][k])
        return Reduce(send, near[axis], at, add, rows, half, land[p][k])

    sums = {(p, k): phase(p, k) for p in pieces for k in range(begins[p], 3)}

    owned = swork.shape[1]

    part = owned // 2

    def s_phase(h):
        def at(t, lo, hi):
            return swork.at[t, pl.ds(h * part + lo, hi - lo), :]

        def add(t, lo, hi, lands):
            for r in range(lo, hi, 128):
                v = swork[t, h * part + r : h * part + r + 128, :]
                for ref in lands:
                    v = v + ref[r - lo : r - lo + 128, :]
                swork[t, h * part + r : h * part + r + 128, :] = v

        return Reduce(send, near["y"], at, add, part, part // 2, sland[h])

    s_red = [s_phase(0), s_phase(1)]

    def f_add(spot, lands):
        v = f_work[spot]
        for ref in lands:
            v = v + ref[...]
        f_work[spot] = v

    f_x = Direct(send, near["x"], lambda t: f_work.at[t], lambda t, l: f_add((t,), l), fx_land)
    f_z = Direct(
        send, near["z"], lambda t: f_work.at[me["x"], t], lambda t, l: f_add((me["x"], t), l), fz_land
    )
    g_z = Spread(send, near["z"], lambda t: gath.at[me["x"], t, core, me["y"]])
    g_x = Spread(send, near["x"], lambda t: gath.at[t, :, core, me["y"]])
    g_y = Spread(send, near["y"], lambda t: gath.at[:, :, core, t])

    class SegGather:
        def __init__(self, h):
            self.first = h * part

        def at(self, t, lo, hi):
            return sgath.at[t, pl.ds(self.first + lo, hi - lo), :]

        def start(self):
            (here, up, far, down), to = near["y"]
            spot = (here, slice(self.first, self.first + part), slice(None))
            sgath[spot] = swork[spot]
            src = self.at(here, 0, part)
            self.c0, self.c1 = send(src, src, to[up]), send(src, src, to[down])

        def middle(self):
            (here, up, far, down), to = near["y"]
            self.c0.wait_recv()
            src = self.at(down, 0, part // 2)
            self.c2 = send(src, src, to[up])
            self.c1.wait_recv()
            src = self.at(up, part // 2, part)
            self.c3 = send(src, src, to[down])

        def finish(self):
            self.c2.wait_recv()
            self.c3.wait_recv()

    s_gat = [SegGather(0), SegGather(1)]
    slots = arr.shape[1] - 8
    some = ids.shape[0]
    each_of = arr.shape[0] // some
    chunk = each_of * slots

    def prepare(g, _):
        rows = []
        for b in range(each_of):
            n = g * each_of + b
            rows.append(arr[n, slots : slots + 1, :])
            rows.append(arr[n, slots + 1 : slots + 2, : slots - 128])
            right[pl.ds(pl.multiple_of(n * slots, 16), slots), :] = hi_lo(arr[n, :slots, :])
        ids[g] = jnp.concatenate(rows, axis=1).astype(i32)
        return 0

    def seg_block(t):
        acc[...] = jnp.zeros_like(acc)
        first = t * owned

        def one(g, _):
            hot = one_hot(lax.broadcasted_iota(i32, (owned, chunk), 0) + first == ids[g])
            acc[...] += jnp.dot(
                hot, right[pl.ds(pl.multiple_of(g * chunk, 16), chunk), :], preferred_element_type=f32
            )
            return 0

        lax.fori_loop(0, some, one, 0)
        swork[t] = acc[:, :128] + acc[:, 128:]

    _, y_up, y_far, y_down = near["y"][0]
    def done(p, k):
        sums[p, k].finish()
        if k < 2:
            sums[p, k + 1].start()

    copy_f.wait()
    f_x.start()
    for p in (0, 2, 4, 1, 3):
        copies[p].wait()
        sums[p, 0].start()
    copy_a.wait()
    lax.fori_loop(0, some, prepare, 0)
    f_x.finish()
    f_z.start()
    seg_block(y_far)
    s_red[0].start()
    s_red[1].start()
    sums[0, 0].middle()
    sums[2, 0].middle()
    sums[4, 0].middle()
    seg_block(y_up)
    sums[1, 0].middle()
    sums[3, 0].middle()
    for p in (5, 6):
        copies[p].wait()
        sums[p, 1].start()
    f_z.finish()
    gath[me["x"], me["z"], core, me["y"]] = f_work[me["x"], me["z"]]
    g_z.start()
    seg_block(y_down)
    s_red[0].middle()
    s_red[1].middle()
    seg_block(me["y"])
    done(0, 0)
    done(2, 0)
    s_red[0].finish()
    s_gat[0].start()
    done(1, 0)
    done(3, 0)
    s_red[1].finish()
    s_gat[1].start()
    done(4, 0)
    sums[5, 1].middle()
    sums[6, 1].middle()
    g_z.finish()
    g_x.start()
    for p in (4, 0, 2, 1, 3):
        sums[p, 1].middle()
    s_gat[0].middle()
    s_gat[1].middle()
    done(5, 1)
    done(6, 1)
    g_x.finish()
    g_y.start()
    for p in (4, 0, 2, 1, 3):
        done(p, 1)
    for c in rest:
        c.wait()
    s_gat[0].finish()
    s_gat[1].finish()
    row_adagrad(s_table, s_accum, lambda n: sgath[n // 4, pl.ds(pl.multiple_of(n % 4 * 128, 128), 128), :], new_s, new_sa)
    g_y.finish()
    g_c = send(gath.at[:, :, core], gath.at[:, :, core], partner)
    here = (me["x"], me["z"], me["y"])
    for p in (5, 6, 4, 0, 2, 1, 3):
        sums[p, 2].finish()
        first, rows = PORT[p][:2]
        mine[first : first + rows, :] = work[p][here[:2] if begins[p] else here]
    g_c.wait_recv()
    row_adagrad(f_table, f_accum, lambda n: gath[n // 2, pl.ds(n % 2 * 2, 2)].reshape(128, 128), new_f, new_fa)
    up_rows, down_rows = g_up.shape[0], g_down.shape[0]
    cols = g_up.shape[1] // 128
    for c in range(cols):
        g_up[:, c * 128 : (c + 1) * 128] = mine[pl.ds(c, up_rows, stride=cols), :]
    first, cols = up_rows * cols, g_down.shape[1] // 128
    for c in range(cols):
        g_down[:, c * 128 : (c + 1) * 128] = mine[pl.ds(first + c, down_rows, stride=cols), :]
    g_bias[...] = mine[first + down_rows * cols : first + down_rows * cols + 1, 0:down_rows]
    for c in send.sent:
        c().wait_send()


def reduce_scratch(owned, frequent, arrived):
    v = lambda *s: pltpu.VMEM(s, f32)
    begins = BEGINS
    out = [v(*(4,) * (3 - b), r, 128) for b, (_, r, _, _) in zip(begins, PORT)]
    for b, (_, r, h, _) in zip(begins, PORT):
        for k in range(b, 3):
            lead = (4,) * (2 - k)
            out += [v(*lead, n, 128) for n in ((r, r, r) if k == 2 else (h, r - h, r, r))]
    q = owned // 4
    out += [v(4, q, 128)] + [v(q // 4, 128), v(q // 4, 128), v(q // 2, 128), v(q // 2, 128)] * 2 + [v(4, q, 128)]
    out += [v(4, 4, 8, 128)] + [v(4, 8, 128)] * 3 + [v(8, 128)] * 3 + [v(4, 4, 2, 4, 8, 128)]
    n = arrived.shape[0] // 16
    flat = arrived.shape[0] * (arrived.shape[1] - 8)
    out += [v(max(a + r for a, r, _, _ in PORT), 128)]
    out += [v(*arrived.shape), pltpu.VMEM((n, 1, flat // n), i32), pltpu.VMEM((flat, 256), bf16), v(q, 256)]
    out += [v(frequent, 128), v(frequent // 128, 128), v(owned, 128), v(owned // 128, 128)]
    out += [pltpu.SemaphoreType.DMA((112,)), pltpu.SemaphoreType.DMA((112,)), pltpu.SemaphoreType.DMA((16,))]
    return out


def reduce_all(parts, arrived, f_table, f_accum, s_table, s_accum, count, width, rank):
    vmem = pl.BlockSpec(memory_space=pltpu.VMEM)
    anyw = pl.BlockSpec(memory_space=pl.ANY)
    frequent, owned = f_table.shape[0], s_table.shape[0]
    given = [f_table, f_accum.reshape(-1, 128), s_table, s_accum.reshape(-1, 128)]
    shapes = [g.shape for g in given] + [(rank // count, width), (width // count, rank), (1, width // count)]
    shapes = [jax.ShapeDtypeStruct(shape, f32) for shape in shapes]
    outs = pl.pallas_call(
        reduce_kernel,
        out_shape=tuple(shapes),
        in_specs=[anyw] * (len(PORT) + 6),
        out_specs=(vmem,) * 7,
        scratch_shapes=reduce_scratch(owned, frequent, arrived),
        compiler_params=params(collective_id=0, has_side_effects=True),
        name="reduce_kernel",
    )(*[w.reshape(4, 4, *w.shape[1:]) for w in parts], arrived, *given)
    return pl.pallas_call(
        move_kernel,
        out_shape=tuple(shapes),
        in_specs=[anyw] * 7,
        out_specs=(anyw,) * 7,
        scratch_shapes=[pltpu.VMEM(x.shape, f32) for x in shapes] + [pltpu.SemaphoreType.DMA((2, 7))],
        compiler_params=params(),
        name="move_kernel",
    )(*outs)


def body(cross_in, cotangent, weight_down, weight_up, cross_bias, row_place, frequent_table, frequent_accum, shard_table, shard_accum):
    samples, width = cross_in.shape
    rank = weight_down.shape[1]
    tables = row_place.shape[1]
    emb = frequent_table.shape[1]
    f_count = frequent_table.shape[0]
    owned = shard_table.shape[0]
    shards = lax.axis_size("dp")
    count = shards * lax.axis_size("rep")
    capacity = samples * tables // (2 * shards)
    blocks = width // emb
    per = 3
    steps = blocks // per
    wide = per * emb
    vmem = pl.BlockSpec(memory_space=pltpu.VMEM)

    place_t = row_place.T
    anyw = pl.BlockSpec(memory_space=pl.ANY)
    hidden, back_low, values, bucket = pl.pallas_call(
        functools.partial(front_kernel, f_count, owned),
        out_shape=(
            jax.ShapeDtypeStruct((samples, rank), bf16),
            jax.ShapeDtypeStruct((samples, rank), bf16),
            jax.ShapeDtypeStruct((blocks * samples, emb), f32),
            jax.ShapeDtypeStruct((shards, capacity + 8, emb), f32),
        ),
        in_specs=[vmem, vmem, anyw, anyw, anyw, anyw],
        out_specs=(vmem, vmem, anyw, anyw),
        scratch_shapes=[
            pltpu.VMEM((samples, width), bf16),
            pltpu.VMEM((samples, width), bf16),
            pltpu.VMEM((width, rank), bf16),
            pltpu.VMEM((rank, width), bf16),
            pltpu.VMEM((blocks * samples, emb), f32),
            pltpu.VMEM((shards, capacity + 8, emb), f32),
            pltpu.VMEM((tables * shards, samples), bf16),
            pltpu.VMEM((tables * shards, samples), f32),
            pltpu.VMEM((shards, 2, 128), i32),
            pltpu.VMEM((shards, 128), f32),
            pltpu.VMEM((shards, 128), f32),
            pltpu.SMEM((shards, 2, 128), i32),
            pltpu.VMEM((samples, rank), f32),
            pltpu.VMEM((samples, rank), f32),
            pltpu.SemaphoreType.DMA((steps, 4)),
            pltpu.SemaphoreType.DMA((3,)),
            pltpu.SemaphoreType.DMA((shards,)),
            pltpu.SemaphoreType.DMA,
        ],
        compiler_params=params(),
        name="front_kernel",
    )(place_t, cross_bias, cross_in, cotangent, weight_down, weight_up)

    arrived = lax.all_to_all(bucket, "dp", split_axis=0, concat_axis=0, tiled=True)

    parts = pl.pallas_call(
        functools.partial(weights_kernel, steps),
        grid=(steps,),
        out_shape=tuple(
            jax.ShapeDtypeStruct(shape, f32)
            for shape in [(16, 4, r, 128) for _, r, _, _ in PORT[:N_BULK]]
            + [(16, r, 128) for _, r, _, _ in PORT[N_BULK:]]
            + [(16, 8, 128)]
        ),
        in_specs=[
            pl.BlockSpec((samples, rank), lambda g: (0, 0)),
            pl.BlockSpec((samples, rank), lambda g: (0, 0)),
            pl.BlockSpec((samples, wide), lambda g: (0, g)),
            pl.BlockSpec((samples, wide), lambda g: (0, g)),
            anyw,
            pl.BlockSpec((tables, samples), lambda g: (0, 0)),
        ],
        out_specs=(anyw,) * (len(PORT) + 1),
        scratch_shapes=[pltpu.VMEM((16, 4, r, 128), f32) for _, r, _, _ in PORT]
        + [pltpu.VMEM((16, n, 128), f32) for _, r, h, _ in PORT[N_BULK:] for n in (h, r - h, r, r)]
        + [pltpu.VMEM((16, 2, 4, 8, 128), f32), pltpu.VMEM((16, 4, 8, 128), f32)]
        + [pltpu.VMEM((16, 8, 128), f32)] * 3
        + [
            pltpu.VMEM((16, 2, 4, max(a + r for a, r, _, _ in PORT), 128), f32),
            pltpu.VMEM((f_count, emb), f32),
            pltpu.VMEM((rank, samples), bf16),
            pltpu.VMEM((rank // 128 * width, 128), f32),
            pltpu.VMEM((per * rank, 128), f32),
            pltpu.VMEM((1, width), f32),
            pltpu.VMEM((blocks * samples, emb), f32),
            pltpu.VMEM((tables, 1, samples), i32),
            pltpu.SemaphoreType.DMA((24,)),
            pltpu.SemaphoreType.DMA((24,)),
            pltpu.SemaphoreType.DMA((16,)),
        ],
        compiler_params=params(collective_id=1, has_side_effects=True),
        name="weights_kernel",
    )(hidden, back_low, cross_in, cotangent, values, place_t)

    new_frequent, new_frequent_accum, new_shard, new_shard_accum, grad_up, grad_down, grad_bias = reduce_all(
        parts, arrived, frequent_table, frequent_accum, shard_table, shard_accum, count, width, rank
    )
    new_frequent_accum, new_shard_accum = new_frequent_accum.reshape(-1), new_shard_accum.reshape(-1)
    grad_bias = grad_bias.reshape(-1)
    return (new_frequent, new_frequent_accum, new_shard, new_shard_accum, grad_up, grad_down, grad_bias)


def solution(mesh):
    both = ("dp", "rep")
    in_specs = (P(both, None), P(both, None), P(), P(), P(), P(both, None), P(), P(), P("dp", None), P("dp"))
    out_specs = (P(), P(), P("dp", None), P("dp"), P(both, None), P(both, None), P(both))
    return jax.shard_map(body, mesh=mesh, in_specs=in_specs, out_specs=out_specs, check_vma=False)
```
